256 devices in a mesh: dp: 2 (over core), seq: 32 (over z, y), head: 4 (over x).
Axes of the slice: x: 4, y: 4, z: 8, core: 2. Of those that a mesh axis runs over, the one named last changes fastest.
Arguments:
- tokens: bfloat16 [8192, 2048], P(('dp', 'seq')), may hold values from -6 to 6
- tangents: bfloat16 [8192, 2048], P(('dp', 'seq')), may hold values from -6 to 6
- attn_gain: float32 [2048], replicated, may hold values from 0.5 to 1.5
- ffn_gain: float32 [2048], replicated, may hold values from 0.5 to 1.5
- w_query: bfloat16 [2048, 2048], P(None, 'head'), may hold values from -0.125 to 0.125
- w_key: bfloat16 [2048, 256], replicated, may hold values from -0.125 to 0.125
- w_value: bfloat16 [2048, 256], replicated, may hold values from -0.125 to 0.125
- w_out: bfloat16 [2048, 2048], P('head'), may hold values from -0.125 to 0.125
- query_gain: float32 [128], replicated, may hold values from 0.5 to 8
- key_gain: float32 [128], replicated, may hold values from 0.5 to 8
- expert_gate: bfloat16 [128, 2048, 768], P(('seq', 'head'), None, 'dp'), may hold values from -0.125 to 0.125
- expert_up: bfloat16 [128, 2048, 768], P(('seq', 'head'), None, 'dp'), may hold values from -0.125 to 0.125
- expert_down: bfloat16 [128, 2048, 768], P(('seq', 'head'), None, 'dp'), may hold values from -0.21875 to 0.21875
- routes: int32 [8192, 8], P(('dp', 'seq', 'head')), may hold values from 0 to 127, all different within a row; in each aligned block of 32 rows (0 to 31, 32 to 63, ...) at most 3 rows name the same one
- route_weights: float32 [8192, 8], P(('dp', 'seq', 'head')), may hold values from 0.3 to 1.2
Outputs:
- layer_out: bfloat16 [8192, 2048], P(('dp', 'seq', 'head'))
- layer_tangent: bfloat16 [8192, 2048], P(('dp', 'seq', 'head'))
The draws below stay inside these ranges and needn't reach their ends.
Inputs may be any that keep to these rules, and one draw needn't show every extreme that they name: `routes`: in each aligned block of 32 rows (the rows of one device) every row names 8 different experts, no expert is named by more than 3 rows, a bound that some block reaches.
All inputs are finite; a program needn't handle non-finite values.
Results may differ from the reference program's by a relative error of at most 0.025.
The reference program's roundings to bfloat16 on the way count: a program that leaves them out, or rounds other values in their place, can miss the bound.
Values may be sent and summed in bfloat16 or wider, within the bound.
No kernel may reach another device: no remote copies, remote signals or barrier semaphores. Data moves between devices by JAX's collectives and lax.ppermute only.
A program may use at most 128 MiB of HBM per device.

```python
import math
import jax
import jax.numpy as jnp
import numpy as np
from jax import lax

D = 2048
HD = 128
QH = 16
KVH = 2
FF = 768
TOPK = 8
EXPERTS = 128
TOK_MOE = 32
SEQ_LEN = 4096
TOKENS = 8192
CAP = 3


def draw_gain_table(key, salt):
    inner_key = jax.random.fold_in(key, salt)
    lower = math.log(0.5)
    upper = math.log(2.0)
    return jnp.exp(jax.random.uniform(inner_key, (HD,), jnp.float32, lower, upper))


def draw_query_gain(key, part):
    return draw_gain_table(key, 101)


def draw_key_gain(key, part):
    return draw_gain_table(key, 202)


def shard_levels(own_key, dims, split, least, top_value):
    loudness, own = 1.0, jax.random.fold_in(own_key, 6)
    for dim, shards_of in split:
        draws = jnp.exp(jax.random.uniform(jax.random.fold_in(own, dim), (shards_of,), jnp.float32, least / len(split), top_value / len(split)))
        loudness = loudness * jnp.repeat(draws, dims[dim] // shards_of).reshape([-1 if axis == dim else 1 for axis in range(len(dims))])
    return loudness


def routed_block(key, own, number, rows, number_of, top, most, skew):
    order = jax.random.permutation(key, number_of)
    crowded, common = load_shares(number_of, rows * top, most, skew, True), load_shares(number_of, rows * top, most, skew, False)
    places = jnp.arange(number_of)

    def named(sizes, offset_by):
        used = int((sizes > 0).sum())
        fixed = max(1, used // 4)
        shifted = fixed + (places - fixed + offset_by * (used - fixed)) % max(1, number_of - fixed)
        return jnp.zeros((number_of,), jnp.int32).at[order[jnp.where(places < fixed, places, shifted)]].set(jnp.asarray(sizes, jnp.int32))

    sizes = jnp.where(number % 4 == 0, named(crowded, number // 4), named(common, number - number // 4 - 1))
    mixed = jax.random.permutation(jax.random.fold_in(own, 3), number_of)
    donor, sink = mixed[0:number_of // 2 * 2:2], mixed[1:number_of // 2 * 2:2]
    room = jnp.minimum(sizes[donor] - 1, most - sizes[sink]) // 2
    room = jnp.where((donor == order[0]) | (sink == order[0]) | (sizes[sink] == 0), 0, jnp.maximum(room, 0))
    shifted = jax.random.randint(jax.random.fold_in(own, 4), (number_of // 2,), 0, 1 << 20) % (room + 1)
    sizes = sizes.at[donor].add(-shifted).at[sink].add(shifted)
    items = jnp.searchsorted(jnp.cumsum(sizes), jnp.arange(rows * top), side="right").astype(jnp.int32)
    table = items.reshape(top, rows).T
    table = table[jax.random.permutation(jax.random.fold_in(own, 1), rows)]
    offset_by = jax.random.randint(jax.random.fold_in(own, 2), (rows, 1), 0, top)
    return jnp.take_along_axis(table, (jnp.arange(top)[None, :] + offset_by) % top, axis=1)


def load_shares(amount, total, reach, lean, full):
    weights = [(1 << 20) // math.isqrt(grade ** lean) + 1 for grade in range(1, amount + 1)]
    largest = reach if full else min(reach, max(-(-total // amount), total * weights[0] // sum(weights)))
    least = 1 if total - largest >= amount - 1 else 0
    holding, surplus = [largest] + [least] * (amount - 1), total - largest - least * (amount - 1)
    while surplus > 0:
        movable = [i for i in range(1, amount) if holding[i] < largest] or [i for i in range(1, amount) if holding[i] < reach]
        mass, left = sum([weights[i] for i in movable]), surplus
        for i in movable:
            addition = min(reach - holding[i], max(1, left * weights[i] // mass), surplus)
            holding[i] = holding[i] + addition
            surplus = surplus - addition
    return np.array(holding)


def bell_draw(rng, extent, spread, limit, split=(), held_as=jnp.bfloat16):
    level = shard_levels(rng, extent, split, -0.22, 0.18) if split else 1.0
    drawn = jax.random.normal(rng, extent, jnp.float32) * spread * level
    return jnp.minimum(jnp.maximum(drawn, -limit), limit).astype(held_as)


def setup_inputs(seed: int = 0) -> dict:
    splits = jax.random.split(jax.random.key(seed), 16)
    tokens = bell_draw(splits[0], (TOKENS, D), 1.0, 6.0, ((0, 64),))
    tangents = bell_draw(splits[1], (TOKENS, D), 1.0, 6.0, ((0, 64),))
    attn_gain = jnp.clip(1.0 + 0.1 * jax.random.normal(splits[2], (D,), jnp.float32), 0.5, 1.5)
    ffn_gain = jnp.clip(1.0 + 0.1 * jax.random.normal(splits[3], (D,), jnp.float32), 0.5, 1.5)
    w_query = bell_draw(splits[4], (D, QH * HD), D ** -0.5, 0.125, ((1, 4),))
    w_key = bell_draw(splits[5], (D, KVH * HD), D ** -0.5, 0.125)
    w_value = bell_draw(splits[6], (D, KVH * HD), D ** -0.5, 0.125)
    w_out = bell_draw(splits[7], (QH * HD, D), (QH * HD) ** -0.5, 0.125, ((0, 4),))
    query_gain = draw_query_gain(jax.random.fold_in(splits[15], 71), 0)
    key_gain = draw_key_gain(jax.random.fold_in(splits[15], 71), 0)
    expert_gate = bell_draw(splits[10], (EXPERTS, D, FF), D ** -0.5, 0.125, ((0, 128), (2, 2)))
    expert_up = bell_draw(splits[11], (EXPERTS, D, FF), D ** -0.5, 0.125, ((0, 128), (2, 2)))
    expert_down = bell_draw(splits[12], (EXPERTS, D, FF), FF ** -0.5, 0.21875, ((0, 128), (2, 2)))
    routes_keys = jax.random.split(jax.random.fold_in(splits[13], 1), TOKENS // TOK_MOE)
    routes_turns = jax.random.permutation(jax.random.fold_in(splits[13], 3), TOKENS // TOK_MOE)
    routes = jax.vmap(lambda own, number: routed_block(jax.random.fold_in(splits[13], 2), own, number, TOK_MOE, EXPERTS, TOPK, CAP, 1))(routes_keys, routes_turns).reshape((TOKENS, TOPK))
    route_weights = jnp.clip(0.3 + 0.90000004 * jax.random.uniform(splits[14], (TOKENS, TOPK), jnp.float32) ** shard_levels(splits[14], (TOKENS, TOPK), ((0, 256),), -0.2, 0.2), 0.3, 1.2)
    return dict(tokens=tokens, tangents=tangents, attn_gain=attn_gain, ffn_gain=ffn_gain, w_query=w_query, w_key=w_key, w_value=w_value, w_out=w_out, query_gain=query_gain, key_gain=key_gain, expert_gate=expert_gate, expert_up=expert_up, expert_down=expert_down, routes=routes, route_weights=route_weights)


epsilon = 1e-06
rope_base = 1000000.0
masked_score = -1e+30

def rms_norm(values, gain):
    mean_square = lax.optimization_barrier(jnp.mean(values * values, axis=-1, keepdims=True))
    return values * lax.rsqrt(mean_square + epsilon) * gain

def norm_pair(values, tangent, gain):
    return jax.jvp(lambda inner: rms_norm(inner, gain), (values,), (tangent,))

def rotate(values, positions):
    head_width = values.shape[-1]
    half_width = head_width // 2
    exponent = jnp.arange(half_width, dtype=jnp.float32) * (2.0 / head_width)
    frequency = jnp.power(jnp.float32(rope_base), -exponent)
    angle = positions.astype(jnp.float32)[:, None] * frequency[None, :]
    cosine = jnp.concatenate([jnp.cos(angle), jnp.cos(angle)], -1)[:, None, :]
    sine = jnp.concatenate([jnp.sin(angle), jnp.sin(angle)], -1)[:, None, :]
    first_half = values[..., :half_width]
    second_half = values[..., half_width:]
    turned = jnp.concatenate([-second_half, first_half], -1)
    return values * cosine + turned * sine

def head_prep(values, gain, positions):
    return rotate(rms_norm(values, gain), positions)

def head_pair(values, tangent, gain, positions):
    return jax.jvp(lambda inner: head_prep(inner, gain, positions), (values,), (tangent,))

def expert_pair(expert_rows, gate_weight, up_weight, down_weight):
    row_count = expert_rows.shape[0]
    model_width = expert_rows.shape[-1]
    flat_rows = expert_rows.reshape(row_count * 2, model_width)
    gate_all = jnp.dot(flat_rows, gate_weight, preferred_element_type=jnp.float32)
    up_all = jnp.dot(flat_rows, up_weight, preferred_element_type=jnp.float32)
    unit_count = gate_all.shape[-1]
    gate_all = gate_all.reshape(row_count, 2, unit_count)
    up_all = up_all.reshape(row_count, 2, unit_count)
    gate_value = gate_all[:, 0]
    gate_tangent = gate_all[:, 1]
    up_value = up_all[:, 0]
    up_tangent = up_all[:, 1]
    sigmoid_gate = jax.nn.sigmoid(gate_value)
    active = gate_value * sigmoid_gate
    active_slope = sigmoid_gate * (1.0 + gate_value * (1.0 - sigmoid_gate))
    hidden = jnp.stack([active * up_value, active_slope * gate_tangent * up_value + active * up_tangent], 1)
    hidden = hidden.astype(jnp.bfloat16).reshape(row_count * 2, unit_count)
    result = lax.dot_general(hidden, down_weight, (((1,), (1,)), ((), ())), preferred_element_type=jnp.float32)
    return result.reshape(row_count, 2, model_width)

def attend_whole(operands):
    query, d_query, key, d_key, value, d_value = operands
    scale = query.shape[-1] ** (-0.5)
    score = jnp.dot(query, key.T, preferred_element_type=jnp.float32) * scale
    d_score = (jnp.dot(d_query, key.T, preferred_element_type=jnp.float32) + jnp.dot(query, d_key.T, preferred_element_type=jnp.float32)) * scale
    length = query.shape[0]
    allowed = jnp.arange(length)[None, :] <= jnp.arange(length)[:, None]
    row_top = lax.optimization_barrier(jnp.max(jnp.where(allowed, score, masked_score), axis=1, keepdims=True))
    weight = jnp.where(allowed, jnp.exp(score - row_top), 0.0)
    total = lax.optimization_barrier(jnp.sum(weight, axis=1, keepdims=True))
    slope = lax.optimization_barrier(jnp.sum(weight * d_score, axis=1, keepdims=True))
    weight_low = weight.astype(jnp.bfloat16)
    tilt_low = (weight * d_score).astype(jnp.bfloat16)
    primal = jnp.dot(weight_low, value, preferred_element_type=jnp.float32)
    tangent = jnp.dot(weight_low, d_value, preferred_element_type=jnp.float32) + jnp.dot(tilt_low, value, preferred_element_type=jnp.float32)
    output = primal / total
    d_output = tangent / total - slope / total * output
    return (output.astype(jnp.bfloat16), d_output.astype(jnp.bfloat16))

def reference(tokens, tangents, attn_gain, ffn_gain, w_query, w_key, w_value, w_out, query_gain, key_gain, expert_gate, expert_up, expert_down, routes, route_weights):
    seq_count = TOKENS // SEQ_LEN
    group_size = QH // KVH
    normed, d_normed = norm_pair(tokens.astype(jnp.float32), tangents.astype(jnp.float32), attn_gain)
    stacked = jnp.concatenate([normed.astype(jnp.bfloat16), d_normed.astype(jnp.bfloat16)], 0)
    query_all = jnp.dot(stacked, w_query, preferred_element_type=jnp.float32).reshape(2, TOKENS, QH, HD)
    key_all = jnp.dot(stacked, w_key, preferred_element_type=jnp.float32).reshape(2, TOKENS, KVH, HD)
    value_all = jnp.dot(stacked, w_value, preferred_element_type=jnp.float32).reshape(2, TOKENS, KVH, HD)
    value_all = value_all.astype(jnp.bfloat16)
    positions = jnp.tile(jnp.arange(SEQ_LEN, dtype=jnp.int32), seq_count)
    query, d_query = head_pair(query_all[0], query_all[1], query_gain, positions)
    key, d_key = head_pair(key_all[0], key_all[1], key_gain, positions)

    def by_head(values, repeat):
        values = values.astype(jnp.bfloat16).reshape(seq_count, SEQ_LEN, values.shape[1], HD)
        values = jnp.repeat(values, repeat, axis=2)
        return jnp.transpose(values, (0, 2, 1, 3)).reshape(seq_count * QH, SEQ_LEN, HD)
    operands = (by_head(query, 1), by_head(d_query, 1), by_head(key, group_size), by_head(d_key, group_size), by_head(value_all[0], group_size), by_head(value_all[1], group_size))
    output, d_output = lax.map(attend_whole, operands)

    def by_token(values):
        values = values.reshape(seq_count, QH, SEQ_LEN, HD)
        return jnp.transpose(values, (0, 2, 1, 3)).reshape(TOKENS, QH * HD)
    merged = jnp.concatenate([by_token(output), by_token(d_output)], 0)
    attn_all = jnp.dot(merged, w_out, preferred_element_type=jnp.float32)
    residual = tokens.astype(jnp.float32) + attn_all[:TOKENS]
    d_residual = tangents.astype(jnp.float32) + attn_all[TOKENS:]
    normed_two, d_normed_two = norm_pair(residual, d_residual, ffn_gain)
    moe_in = jnp.stack([normed_two.astype(jnp.bfloat16), d_normed_two.astype(jnp.bfloat16)], 1)
    block_count = TOKENS // TOK_MOE
    pair_count = TOK_MOE * TOPK
    flat_routes = routes.reshape(block_count, pair_count).astype(jnp.int32)
    onehot = (flat_routes[:, :, None] == jnp.arange(EXPERTS, dtype=jnp.int32)[None, None, :]).astype(jnp.int32)
    earlier = jnp.cumsum(onehot, axis=1) - onehot
    slots = lax.optimization_barrier(jnp.sum(earlier * onehot, axis=2)).astype(jnp.int32)
    token_ids = jnp.repeat(jnp.arange(TOKENS, dtype=jnp.int32), TOPK).reshape(block_count, pair_count)
    block_ids = jnp.broadcast_to(jnp.arange(block_count, dtype=jnp.int32)[:, None], (block_count, pair_count))
    table = jnp.zeros((EXPERTS, block_count, CAP), jnp.int32).at[flat_routes, block_ids, slots].set(token_ids)
    share_table = jnp.zeros((EXPERTS, block_count, CAP), jnp.float32).at[flat_routes, block_ids, slots].set(route_weights.reshape(block_count, pair_count))

    def expert_step(running, inputs):
        row_ids, shares, gate_weight, up_weight, down_weight = inputs
        row_ids = row_ids.reshape(-1)
        shares = shares.reshape(-1)
        result = expert_pair(moe_in[row_ids], gate_weight, up_weight, down_weight)
        return (running.at[row_ids].add(result * shares[:, None, None]), None)
    moe_sum, _ = lax.scan(expert_step, jnp.zeros((TOKENS, 2, D), jnp.float32), (table, share_table, expert_gate, expert_up, expert_down))
    layer_out = (residual + moe_sum[:, 0]).astype(jnp.bfloat16)
    layer_tangent = (d_residual + moe_sum[:, 1]).astype(jnp.bfloat16)
    return (layer_out, layer_tangent)
```

```python
import jax
import jax.numpy as jnp
from jax import lax
from jax.sharding import Mesh
from jax.sharding import PartitionSpec as P

SEQ = ("seq_0", "seq_1")
SEQ_HEAD = ("seq_0", "seq_1", "head")
DP_SEQ = ("dp", "seq_0", "seq_1")
DP_SEQ_HEAD = ("dp", "seq_0", "seq_1", "head")


epsilon = 1e-06
rope_base = 1000000.0
masked_score = -1e30


def gathered_by_axis(array, axes, dim):
    result = array
    for number in range(len(axes) - 1, -1, -1):
        result = lax.all_gather(result, axes[number], axis=dim, tiled=True)
    return result


def split_up(array, dim, size):
    before, after = (array.shape[:dim], array.shape[dim + 1 :])
    return jnp.moveaxis(array.reshape(*before, size, -1, *after), dim, 0)


def summed_on_arrival(array, axis, dim):
    size = lax.axis_size(axis)
    parts = lax.all_to_all(split_up(array, dim, size), axis, 0, 0, tiled=True)
    return jnp.sum(parts, axis=0)


def in_one_piece(arrays, axis, dim, along):
    widths = [a.shape[along] for a in arrays]
    both = jnp.concatenate(arrays, axis=along)
    result = lax.all_gather(both, axis, axis=dim, tiled=True)
    return tuple(jnp.split(result, [sum(widths[:k]) for k in range(1, len(widths))], axis=along))


def rms_norm(values, gain):
    mean_square = jnp.mean(values * values, axis=-1, keepdims=True)
    return values * lax.rsqrt(mean_square + epsilon) * gain


def norm_pair(values, tangent, gain):
    return jax.jvp(lambda inner: rms_norm(inner, gain), (values,), (tangent,))


def rotate(values, positions):
    head_width = values.shape[-1]
    half_width = head_width // 2
    exponent = jnp.arange(half_width, dtype=jnp.float32) * (2.0 / head_width)
    frequency = jnp.power(jnp.float32(rope_base), -exponent)
    angle = positions.astype(jnp.float32)[:, None] * frequency[None, :]
    cosine = jnp.concatenate([jnp.cos(angle), jnp.cos(angle)], -1)[:, None, :]
    sine = jnp.concatenate([jnp.sin(angle), jnp.sin(angle)], -1)[:, None, :]
    first_half = values[..., :half_width]
    second_half = values[..., half_width:]
    turned = jnp.concatenate([-second_half, first_half], -1)
    return values * cosine + turned * sine


def head_prep(values, gain, positions):
    return rotate(rms_norm(values, gain), positions)


def head_pair(values, tangent, gain, positions):
    return jax.jvp(lambda inner: head_prep(inner, gain, positions), (values,), (tangent,))


def expert_pair(expert_rows, gate_weight, up_weight, down_weight):
    row_count = expert_rows.shape[0]
    model_width = expert_rows.shape[-1]
    flat_rows = expert_rows.reshape(row_count * 2, model_width)
    gate_all = jnp.dot(flat_rows, gate_weight, preferred_element_type=jnp.float32)
    up_all = jnp.dot(flat_rows, up_weight, preferred_element_type=jnp.float32)
    unit_count = gate_all.shape[-1]
    gate_all = gate_all.reshape(row_count, 2, unit_count)
    up_all = up_all.reshape(row_count, 2, unit_count)
    gate_value = gate_all[:, 0]
    gate_tangent = gate_all[:, 1]
    up_value = up_all[:, 0]
    up_tangent = up_all[:, 1]
    sigmoid_gate = jax.nn.sigmoid(gate_value)
    active = gate_value * sigmoid_gate
    active_slope = sigmoid_gate * (1.0 + gate_value * (1.0 - sigmoid_gate))
    hidden = jnp.stack(
        [active * up_value, active_slope * gate_tangent * up_value + active * up_tangent], 1
    )
    hidden = hidden.astype(jnp.bfloat16).reshape(row_count * 2, unit_count)
    result = lax.dot_general(
        hidden, down_weight, (((1,), (1,)), ((), ())), preferred_element_type=jnp.float32
    )
    return result.reshape(row_count, 2, model_width)


def bf16_parts(values):
    high = lax.reduce_precision(values, 8, 7)
    rest = values - high
    middle = lax.reduce_precision(rest, 8, 7)
    low = lax.reduce_precision(rest - middle, 8, 7)
    return [high.astype(jnp.bfloat16), middle.astype(jnp.bfloat16), low.astype(jnp.bfloat16)]


def shifted(array, axis, offset):
    size = lax.axis_size(axis)
    return lax.ppermute(array, axis, [(i, (i + offset) % size) for i in range(size)])


def ring_blocks(block, axis):
    size = lax.axis_size(axis)
    found = {0: block}
    up = down = block
    for step in range(1, size // 2 + 1):
        up = shifted(up, axis, 1)
        found[-step] = up
        if 2 * step < size:
            down = shifted(down, axis, -1)
            found[step] = down
    return found


def attend_part(query_low, joint_query, blocks, block_pos, row_pos, scale):
    contract = (((1,), (1,)), ((), ()))
    width = query_low.shape[1]
    rows = jnp.concatenate(blocks, 0)
    key_pos = jnp.concatenate(block_pos, 0)
    score = lax.dot_general(
        query_low, rows[:, :width], contract, preferred_element_type=jnp.float32
    ) * scale
    d_score = lax.dot_general(
        joint_query, rows[:, : 2 * width], contract, preferred_element_type=jnp.float32
    ) * scale
    allowed = key_pos[None, :] <= row_pos[:, None]
    top = jnp.max(jnp.where(allowed, score, masked_score), axis=1)
    weight = jnp.where(allowed, jnp.exp(score - top[:, None]), 0.0)
    tilt = weight * d_score
    total = jnp.sum(weight, axis=1)
    slope = jnp.sum(tilt, axis=1)
    weight_low = weight.astype(jnp.bfloat16)
    tilt_low = tilt.astype(jnp.bfloat16)
    value = rows[:, 2 * width : 3 * width]
    d_value = rows[:, 3 * width :]
    primal = jnp.dot(weight_low, value, preferred_element_type=jnp.float32)
    tangent = jnp.dot(
        jnp.concatenate([weight_low, tilt_low], 1),
        jnp.concatenate([d_value, value], 0),
        preferred_element_type=jnp.float32,
    )
    some = total > 0.0
    share = jnp.where(some, 1.0 / jnp.where(some, total, 1.0), 0.0)
    output = primal * share[:, None]
    mean_slope = slope * share
    d_output = tangent * share[:, None] - mean_slope[:, None] * output
    level = jnp.where(some, top + jnp.log(jnp.where(some, total, 1.0)), masked_score)
    return output, d_output, level, mean_slope


def merged_parts(outputs, d_outputs, levels, slopes):
    top = jnp.max(levels, axis=0, keepdims=True)
    raw = jnp.exp(levels - top)
    raw_total = jnp.sum(raw, axis=0, keepdims=True)
    mix = raw / raw_total
    slope = jnp.sum(mix * slopes, axis=0, keepdims=True)
    tilt = mix * (slopes - slope)
    output = jnp.sum(mix[..., None] * outputs, axis=0)
    d_output = jnp.sum(mix[..., None] * d_outputs + tilt[..., None] * outputs, axis=0)
    return output, d_output, (top + jnp.log(raw_total))[0], slope[0]


def local(
    tokens,
    tangents,
    attn_gain,
    ffn_gain,
    w_query,
    w_key,
    w_value,
    w_out,
    query_gain,
    key_gain,
    expert_gate,
    expert_up,
    expert_down,
    routes,
    route_weights,
):
    tok_count, model_width = tokens.shape
    head_width = query_gain.shape[0]
    heads_here = w_query.shape[1] // head_width
    head_count = lax.axis_size("head")
    moe_rows = tok_count // head_count
    core = lax.axis_index("dp")
    other_core = [(0, 1), (1, 0)]

    half_rows = w_out.shape[0] // 2
    own_half = lax.dynamic_slice_in_dim(w_out, core * half_rows, half_rows, 0)
    from_left = shifted(own_half, "head", 1)
    from_right = shifted(own_half, "head", -1)
    quarter = half_rows // 2
    far_low = shifted(from_left[:quarter], "head", 1)
    far_high = shifted(from_right[quarter:], "head", -1)
    fetched = jnp.concatenate([own_half, from_left, from_right, far_low, far_high], 0)
    partner_fetched = lax.ppermute(fetched, "dp", other_core)
    both_fetched = jnp.concatenate([fetched, partner_fetched], 0)

    gate_half = expert_gate[0]
    up_half = expert_up[0]
    down_half = expert_down[0]
    full_gate, full_up, full_down = (
        jnp.concatenate([half, lax.ppermute(half, "dp", other_core)], 1)
        for half in (gate_half, up_half, down_half)
    )

    plane = lax.axis_index("seq_0")
    row_in_plane = lax.axis_index("seq_1")
    plane_rows = lax.axis_size("seq_1") * tok_count
    plane_count = lax.axis_size("seq_0")
    first_pos = plane * plane_rows + row_in_plane * tok_count
    positions = first_pos + jnp.arange(tok_count, dtype=jnp.int32)
    kv_count = w_key.shape[1] // head_width
    devices_per_kv = lax.axis_size("head") // kv_count
    kv_start = lax.axis_index("head") // devices_per_kv * head_width
    key_cols = lax.dynamic_slice_in_dim(w_key, kv_start, head_width, 1)
    value_cols = lax.dynamic_slice_in_dim(w_value, kv_start, head_width, 1)
    normed, d_normed = norm_pair(
        tokens.astype(jnp.float32), tangents.astype(jnp.float32), attn_gain
    )
    stacked = jnp.concatenate([normed.astype(jnp.bfloat16), d_normed.astype(jnp.bfloat16)], 0)
    kv_cols = jnp.concatenate([key_cols, value_cols], 1)
    kv_all = jnp.dot(stacked, kv_cols, preferred_element_type=jnp.float32)
    key_all = kv_all[:, :head_width].reshape(2, tok_count, 1, head_width)
    value_all = kv_all[:, head_width:].reshape(2, tok_count, head_width)
    key, d_key = head_pair(key_all[0], key_all[1], key_gain, positions)
    packed = jnp.concatenate(
        [
            key.reshape(tok_count, head_width),
            d_key.reshape(tok_count, head_width),
            value_all[0],
            value_all[1],
        ],
        1,
    ).astype(jnp.bfloat16)
    blocks = ring_blocks(packed, "seq_0")

    query_all = jnp.dot(stacked, w_query, preferred_element_type=jnp.float32)
    query_all = query_all.reshape(2, tok_count, heads_here, head_width)
    query, d_query = head_pair(query_all[0], query_all[1], query_gain, positions)

    def by_receiver(values):
        values = values.astype(jnp.bfloat16).reshape(head_count, moe_rows, heads_here, head_width)
        return jnp.transpose(values, (0, 2, 1, 3)).reshape(tok_count * heads_here, head_width)

    joint_own = jnp.concatenate([by_receiver(d_query), by_receiver(query)], 1)
    own_rows = joint_own.shape[0]
    row_groups = lax.axis_size("seq_1")
    joint_query = lax.all_to_all(
        jnp.broadcast_to(joint_own[None], (row_groups, own_rows, 2 * head_width)),
        "seq_1",
        0,
        0,
        tiled=True,
    ).reshape(row_groups * own_rows, 2 * head_width)
    query_low = joint_query[:, head_width:]
    row_id = jnp.arange(row_groups * own_rows, dtype=jnp.int32)
    row_pos = (
        plane * plane_rows
        + row_id // own_rows * tok_count
        + row_id % own_rows // (heads_here * moe_rows) * moe_rows
        + row_id % moe_rows
    )
    scale = head_width ** (-0.5)

    def positions_of(offset):
        owner = lax.rem(plane + offset + plane_count, plane_count)
        return owner * plane_rows + row_in_plane * tok_count + jnp.arange(tok_count, dtype=jnp.int32)

    near = [0, -1, 1]
    far = [k for k in blocks if k not in near]
    parts = [
        attend_part(
            query_low,
            joint_query,
            [blocks[k] for k in group],
            [positions_of(k) for k in group],
            row_pos,
            scale,
        )
        for group in (near, far)
    ]
    output, d_output, level, mean_slope = merged_parts(*(jnp.stack(p) for p in zip(*parts)))

    receivers = row_groups * head_count
    rows_each = heads_here * moe_rows
    level = jnp.maximum(level, masked_score).reshape(receivers, rows_each)
    stats = jnp.stack(bf16_parts(level) + bf16_parts(mean_slope.reshape(receivers, rows_each)), 1)
    stats = jnp.pad(stats, ((0, 0), (0, 16 - stats.shape[1]), (0, 0)))
    stats = stats.reshape(receivers, 8, 2 * rows_each)
    both = jnp.concatenate([output, d_output], 1).astype(jnp.bfloat16)
    sent = jnp.concatenate([both.reshape(receivers, rows_each, 2 * head_width), stats], 1)
    arrived = lax.all_to_all(sent, ("seq_1", "head"), 0, 0, tiled=True)
    stats = arrived[:, rows_each:].reshape(receivers, 16, rows_each).astype(jnp.float32)
    stats = stats.reshape(row_groups, head_count, 16, rows_each)
    arrived = arrived[:, :rows_each].astype(jnp.float32)
    arrived = arrived.reshape(row_groups, head_count, rows_each, 2 * head_width)
    output, d_output, _, _ = merged_parts(
        arrived[..., :head_width],
        arrived[..., head_width:],
        stats[:, :, 0] + stats[:, :, 1] + stats[:, :, 2],
        stats[:, :, 3] + stats[:, :, 4] + stats[:, :, 5],
    )
    merged = jnp.stack([output, d_output], 0).astype(jnp.bfloat16)
    merged = merged.reshape(2, head_count, heads_here, moe_rows, head_width)
    merged = jnp.transpose(merged, (1, 0, 3, 2, 4)).reshape(
        head_count, 2 * moe_rows, heads_here * head_width
    )
    here = lax.axis_index("head")

    def columns(offset, half):
        group = lax.rem(here + offset + head_count, head_count)
        block = lax.dynamic_index_in_dim(merged, group, 0, keepdims=False)
        return lax.dynamic_slice_in_dim(block, half * half_rows, half_rows, 1)

    ordered = [columns(offset, half) for half in (core, 1 - core) for offset in (0, -1, 1, 2)]
    attn_rows = jnp.dot(
        jnp.concatenate(ordered, 1), both_fetched, preferred_element_type=jnp.float32
    ).reshape(2, moe_rows, model_width)
    row_start = lax.axis_index("head") * moe_rows
    own_tokens = lax.dynamic_slice_in_dim(tokens, row_start, moe_rows, 0).astype(jnp.float32)
    own_tangents = lax.dynamic_slice_in_dim(tangents, row_start, moe_rows, 0).astype(jnp.float32)
    residual = own_tokens + attn_rows[0]
    d_residual = own_tangents + attn_rows[1]
    normed_two, d_normed_two = norm_pair(residual, d_residual, ffn_gain)
    moe_in = jnp.stack([normed_two.astype(jnp.bfloat16), d_normed_two.astype(jnp.bfloat16)], 1)
    moe_in = moe_in.reshape(moe_rows, 2 * model_width)
    expert_total = lax.axis_size(SEQ) * lax.axis_size("head") * expert_gate.shape[0]
    top_count = routes.shape[1]
    capacity = max(2, 3 * moe_rows * top_count // (2 * expert_total))
    pair_count = moe_rows * top_count
    flat_routes = routes.reshape(pair_count)
    onehot = (flat_routes[:, None] == jnp.arange(expert_total, dtype=jnp.int32)[None, :]).astype(
        jnp.float32
    )
    lower = (jnp.arange(pair_count)[:, None] > jnp.arange(pair_count)[None, :]).astype(jnp.float32)
    earlier = jnp.dot(lower, onehot, preferred_element_type=jnp.float32)
    slots = jnp.sum(earlier * onehot, axis=1).astype(jnp.int32)
    column = (flat_routes * capacity + slots).reshape(moe_rows, top_count)
    hits = column[:, :, None] == jnp.arange(expert_total * capacity, dtype=jnp.int32)[None, None, :]
    placing = jnp.sum(hits.astype(jnp.float32), axis=1).astype(jnp.bfloat16)
    mixing = jnp.sum(jnp.where(hits, route_weights[:, :, None], 0.0), axis=1)
    outgoing = lax.dot_general(
        placing, moe_in, (((0,), (0,)), ((), ())), preferred_element_type=jnp.float32
    )
    outgoing = outgoing.astype(jnp.bfloat16).reshape(expert_total, capacity, 2, model_width)
    received = lax.all_to_all(outgoing, SEQ_HEAD, split_axis=0, concat_axis=0, tiled=True)
    source_count = received.shape[0]
    slot_count = received.shape[1]
    flat_rows = received.reshape(source_count * slot_count, 2, model_width)
    result = expert_pair(flat_rows, full_gate, full_up, full_down)
    result = result.reshape(source_count, slot_count, 2, model_width)
    returned = lax.all_to_all(result, SEQ_HEAD, split_axis=0, concat_axis=0, tiled=True)
    returned = returned.reshape(expert_total * capacity, 2 * model_width)
    moe_sum = jnp.dot(mixing, returned, preferred_element_type=jnp.float32)
    moe_sum = moe_sum.reshape(moe_rows, 2, model_width)
    layer_out = (residual + moe_sum[:, 0]).astype(jnp.bfloat16)
    layer_tangent = (d_residual + moe_sum[:, 1]).astype(jnp.bfloat16)
    return (layer_out, layer_tangent)


def solution(mesh):
    split = Mesh(
        mesh.devices.reshape(mesh.shape["dp"], 8, 4, mesh.shape["head"]),
        ("dp", "seq_0", "seq_1", "head"),
    )
    return jax.shard_map(
        local,
        mesh=split,
        in_specs=(
            P(DP_SEQ, None),
            P(DP_SEQ, None),
            P(),
            P(),
            P(None, "head"),
            P(),
            P(),
            P("head", None),
            P(),
            P(),
            P(SEQ_HEAD, None, "dp"),
            P(SEQ_HEAD, None, "dp"),
            P(SEQ_HEAD, None, "dp"),
            P(DP_SEQ_HEAD, None),
            P(DP_SEQ_HEAD, None),
        ),
        out_specs=(P(DP_SEQ_HEAD, None), P(DP_SEQ_HEAD, None)),
        check_vma=False,
    )
```

```python
import jax
import jax.numpy as jnp
from jax import lax
from jax.experimental import pallas as pl
from jax.experimental.pallas import tpu as pltpu
from jax.sharding import Mesh
from jax.sharding import PartitionSpec as P

SEQ = ("seq_0", "seq_1")
SEQ_HEAD = ("seq_0", "seq_1", "head")
DP_SEQ = ("dp", "seq_0", "seq_1")
DP_SEQ_HEAD = ("dp", "seq_0", "seq_1", "head")


epsilon = 1e-06
rope_base = 1000000.0
masked_score = -1e30


def rms_norm(values, gain):
    mean_square = jnp.mean(values * values, axis=-1, keepdims=True)
    return values * lax.rsqrt(mean_square + epsilon) * gain


def norm_pair(values, tangent, gain):
    return jax.jvp(lambda inner: rms_norm(inner, gain), (values,), (tangent,))


def rotate(values, positions):
    head_width = values.shape[-1]
    half_width = head_width // 2
    exponent = jnp.arange(half_width, dtype=jnp.float32) * (2.0 / head_width)
    frequency = jnp.power(jnp.float32(rope_base), -exponent)
    angle = positions.astype(jnp.float32)[:, None] * frequency[None, :]
    cosine = jnp.concatenate([jnp.cos(angle), jnp.cos(angle)], -1)[:, None, :]
    sine = jnp.concatenate([jnp.sin(angle), jnp.sin(angle)], -1)[:, None, :]
    first_half = values[..., :half_width]
    second_half = values[..., half_width:]
    turned = jnp.concatenate([-second_half, first_half], -1)
    return values * cosine + turned * sine


def head_prep(values, gain, positions):
    return rotate(rms_norm(values, gain), positions)


def head_pair(values, tangent, gain, positions):
    return jax.jvp(lambda inner: head_prep(inner, gain, positions), (values,), (tangent,))


def bf16_parts(values):
    high = lax.reduce_precision(values, 8, 7)
    rest = values - high
    middle = lax.reduce_precision(rest, 8, 7)
    low = lax.reduce_precision(rest - middle, 8, 7)
    return [high.astype(jnp.bfloat16), middle.astype(jnp.bfloat16), low.astype(jnp.bfloat16)]


def shifted(array, axis, offset):
    size = lax.axis_size(axis)
    return lax.ppermute(array, axis, [(i, (i + offset) % size) for i in range(size)])


def ring_blocks(block, axis):
    size = lax.axis_size(axis)
    found = {0: block}
    up = down = block
    for step in range(1, size // 2 + 1):
        up = shifted(up, axis, 1)
        found[-step] = up
        if 2 * step < size:
            down = shifted(down, axis, -1)
            found[step] = down
    return found


def attend_part(query_low, joint_query, blocks, block_pos, row_pos, scale):
    contract = (((1,), (1,)), ((), ()))
    width = query_low.shape[1]
    rows = jnp.concatenate(blocks, 0)
    key_pos = jnp.concatenate(block_pos, 0)
    score = lax.dot_general(
        query_low, rows[:, :width], contract, preferred_element_type=jnp.float32
    ) * scale
    d_score = lax.dot_general(
        joint_query, rows[:, : 2 * width], contract, preferred_element_type=jnp.float32
    ) * scale
    allowed = key_pos[None, :] <= row_pos[:, None]
    top = jnp.max(jnp.where(allowed, score, masked_score), axis=1)
    weight = jnp.where(allowed, jnp.exp(score - top[:, None]), 0.0)
    tilt = weight * d_score
    total = jnp.sum(weight, axis=1)
    slope = jnp.sum(tilt, axis=1)
    weight_low = weight.astype(jnp.bfloat16)
    tilt_low = tilt.astype(jnp.bfloat16)
    value = rows[:, 2 * width : 3 * width]
    d_value = rows[:, 3 * width :]
    primal = jnp.dot(weight_low, value, preferred_element_type=jnp.float32)
    tangent = jnp.dot(
        jnp.concatenate([weight_low, tilt_low], 1),
        jnp.concatenate([d_value, value], 0),
        preferred_element_type=jnp.float32,
    )
    some = total > 0.0
    share = jnp.where(some, 1.0 / jnp.where(some, total, 1.0), 0.0)
    output = primal * share[:, None]
    mean_slope = slope * share
    d_output = tangent * share[:, None] - mean_slope[:, None] * output
    level = jnp.where(some, top + jnp.log(jnp.where(some, total, 1.0)), masked_score)
    return output, d_output, level, mean_slope


def merged_parts(outputs, d_outputs, levels, slopes):
    top = jnp.max(levels, axis=0, keepdims=True)
    raw = jnp.exp(levels - top)
    raw_total = jnp.sum(raw, axis=0, keepdims=True)
    mix = raw / raw_total
    slope = jnp.sum(mix * slopes, axis=0, keepdims=True)
    tilt = mix * (slopes - slope)
    output = jnp.sum(mix[..., None] * outputs, axis=0)
    d_output = jnp.sum(mix[..., None] * d_outputs + tilt[..., None] * outputs, axis=0)
    return output, d_output, (top + jnp.log(raw_total))[0], slope[0]


def expert_kernel(rows_ref, gate_a, gate_b, up_a, up_b, down_a, down_b, out_ref):
    rows = rows_ref[...]
    count = rows.shape[0]
    hidden = []
    for gate_ref, up_ref in ((gate_a, up_a), (gate_b, up_b)):
        units = gate_ref.shape[1]
        weight = jnp.concatenate([gate_ref[...], up_ref[...]], axis=1)
        both = jnp.dot(rows, weight, preferred_element_type=jnp.float32)
        both = both.reshape(count // 24, 3, 8, 2 * units)
        gate, up = both[..., :units], both[..., units:]

        def pair(gate_value, gate_tangent, up_value, up_tangent):
            sigmoid_gate = jax.nn.sigmoid(gate_value)
            active = gate_value * sigmoid_gate
            active_slope = sigmoid_gate * (1.0 + gate_value * (1.0 - sigmoid_gate))
            primal = active * up_value
            return primal, active_slope * gate_tangent * up_value + active * up_tangent

        primal, tangent = pair(gate[:, 0], gate[:, 1], up[:, 0], up[:, 1])
        mixed_gate, mixed_up = gate[:, 2], up[:, 2]
        turned_gate = pltpu.roll(mixed_gate, 4, 1)
        turned_up = pltpu.roll(mixed_up, 4, 1)
        first = lax.broadcasted_iota(jnp.int32, mixed_gate.shape, 1) < 4
        last_primal, last_tangent = pair(
            jnp.where(first, mixed_gate, turned_gate),
            jnp.where(first, turned_gate, mixed_gate),
            jnp.where(first, mixed_up, turned_up),
            jnp.where(first, turned_up, mixed_up),
        )
        last = jnp.where(first, last_primal, last_tangent)
        units_hidden = jnp.stack([primal, tangent, last], 1).reshape(count, units)
        hidden.append(units_hidden.astype(jnp.bfloat16))
    down = jnp.concatenate([down_a[...], down_b[...]], axis=1)
    result = lax.dot_general(
        jnp.concatenate(hidden, axis=1),
        down,
        (((1,), (1,)), ((), ())),
        preferred_element_type=jnp.float32,
    )
    out_ref[...] = result.astype(out_ref.dtype)


def expert_rows(rows, weights):
    return pl.pallas_call(
        expert_kernel,
        out_shape=jax.ShapeDtypeStruct(rows.shape, jnp.bfloat16),
        compiler_params=pltpu.CompilerParams(vmem_limit_bytes=56 << 20),
        name="expert_rows",
    )(rows, *weights)


def project_kernel(rows_ref, *refs):
    out_ref = refs[-1]
    start = 0
    total = None
    for piece in refs[:-1]:
        depth = piece.shape[0]
        term = jnp.dot(
            rows_ref[:, start : start + depth], piece[...], preferred_element_type=jnp.float32
        )
        total = term if total is None else total + term
        start += depth
    out_ref[...] = total


def project(rows, pieces):
    return pl.pallas_call(
        project_kernel,
        out_shape=jax.ShapeDtypeStruct((rows.shape[0], pieces[0].shape[1]), jnp.float32),
        compiler_params=pltpu.CompilerParams(vmem_limit_bytes=48 << 20),
        name="project",
    )(rows, *pieces)


def local(
    tokens,
    tangents,
    attn_gain,
    ffn_gain,
    w_query,
    w_key,
    w_value,
    w_out,
    query_gain,
    key_gain,
    expert_gate,
    expert_up,
    expert_down,
    routes,
    route_weights,
):
    tok_count, model_width = tokens.shape
    head_width = query_gain.shape[0]
    heads_here = w_query.shape[1] // head_width
    head_count = lax.axis_size("head")
    moe_rows = tok_count // head_count
    core = lax.axis_index("dp")
    other_core = [(0, 1), (1, 0)]

    half_rows = w_out.shape[0] // 2
    ring = range(head_count)
    sides = [(i, (i + 1) % head_count) for i in ring]
    sides += [(head_count + i, head_count + (i - 1) % head_count) for i in ring]
    near_own = lax.ppermute(w_out, ("dp", "head"), sides)
    far_own = shifted(
        lax.dynamic_slice_in_dim(w_out, core * half_rows, half_rows, 0), "head", head_count // 2
    )
    near_other = lax.ppermute(near_own, "dp", other_core)
    far_other = lax.ppermute(far_own, "dp", other_core)
    out_pieces = (w_out, near_own, near_other, far_own, far_other)

    expert_halves = []
    for half in (expert_gate[0], expert_up[0], expert_down[0]):
        expert_halves += [half, lax.ppermute(half, "dp", other_core)]

    plane = lax.axis_index("seq_0")
    row_in_plane = lax.axis_index("seq_1")
    plane_rows = lax.axis_size("seq_1") * tok_count
    plane_count = lax.axis_size("seq_0")
    first_pos = plane * plane_rows + row_in_plane * tok_count
    positions = first_pos + jnp.arange(tok_count, dtype=jnp.int32)
    kv_count = w_key.shape[1] // head_width
    devices_per_kv = lax.axis_size("head") // kv_count
    kv_start = lax.axis_index("head") // devices_per_kv * head_width
    key_cols = lax.dynamic_slice_in_dim(w_key, kv_start, head_width, 1)
    value_cols = lax.dynamic_slice_in_dim(w_value, kv_start, head_width, 1)
    normed, d_normed = norm_pair(
        tokens.astype(jnp.float32), tangents.astype(jnp.float32), attn_gain
    )
    stacked = jnp.concatenate([normed.astype(jnp.bfloat16), d_normed.astype(jnp.bfloat16)], 0)
    kv_cols = jnp.concatenate([key_cols, value_cols], 1)
    kv_all = jnp.dot(stacked, kv_cols, preferred_element_type=jnp.float32)
    key_all = kv_all[:, :head_width].reshape(2, tok_count, 1, head_width)
    value_all = kv_all[:, head_width:].reshape(2, tok_count, head_width)
    key, d_key = head_pair(key_all[0], key_all[1], key_gain, positions)
    packed = jnp.concatenate(
        [
            key.reshape(tok_count, head_width),
            d_key.reshape(tok_count, head_width),
            value_all[0],
            value_all[1],
        ],
        1,
    ).astype(jnp.bfloat16)
    weight_parts = bf16_parts(route_weights)
    routing = jnp.concatenate(
        [routes.astype(jnp.bfloat16), weight_parts[0], weight_parts[1], weight_parts[2]], 1
    )
    routing_shape = routing.shape
    routing = routing.reshape(-1, packed.shape[1])
    routing_rows = routing.shape[0]
    routing = jnp.pad(routing, ((0, 8 - routing_rows), (0, 0)))
    found = ring_blocks(jnp.concatenate([packed, routing], 0), "seq_0")
    blocks = {k: v[:tok_count] for k, v in found.items()}
    routing = {
        k: v[tok_count : tok_count + routing_rows].reshape(routing_shape).astype(jnp.float32)
        for k, v in found.items()
    }

    query_all = jnp.dot(stacked, w_query, preferred_element_type=jnp.float32)
    query_all = query_all.reshape(2, tok_count, heads_here, head_width)
    query, d_query = head_pair(query_all[0], query_all[1], query_gain, positions)

    def by_receiver(values):
        values = values.astype(jnp.bfloat16).reshape(head_count, moe_rows, heads_here, head_width)
        return jnp.transpose(values, (0, 2, 1, 3)).reshape(tok_count * heads_here, head_width)

    joint_own = jnp.concatenate([by_receiver(d_query), by_receiver(query)], 1)
    own_rows = joint_own.shape[0]
    row_groups = lax.axis_size("seq_1")
    joint_query = lax.all_to_all(
        jnp.broadcast_to(joint_own[None], (row_groups, own_rows, 2 * head_width)),
        "seq_1",
        0,
        0,
        tiled=True,
    ).reshape(row_groups * own_rows, 2 * head_width)
    query_low = joint_query[:, head_width:]
    row_id = jnp.arange(row_groups * own_rows, dtype=jnp.int32)
    row_pos = (
        plane * plane_rows
        + row_id // own_rows * tok_count
        + row_id % own_rows // (heads_here * moe_rows) * moe_rows
        + row_id % moe_rows
    )
    scale = head_width ** (-0.5)

    def positions_of(offset):
        owner = lax.rem(plane + offset + plane_count, plane_count)
        return owner * plane_rows + row_in_plane * tok_count + jnp.arange(tok_count, dtype=jnp.int32)

    order = sorted(blocks)
    output, d_output, level, mean_slope = attend_part(
        query_low,
        joint_query,
        [blocks[k] for k in order],
        [positions_of(k) for k in order],
        row_pos,
        scale,
    )

    receivers = row_groups * head_count
    rows_each = heads_here * moe_rows
    level = jnp.maximum(level, masked_score).reshape(receivers, rows_each)
    stats = jnp.stack(bf16_parts(level) + bf16_parts(mean_slope.reshape(receivers, rows_each)), 1)
    stats = jnp.pad(stats, ((0, 0), (0, 16 - stats.shape[1]), (0, 0)))
    stats = stats.reshape(receivers, 8, 2 * rows_each)
    both = jnp.concatenate([output, d_output], 1).astype(jnp.bfloat16)
    sent = jnp.concatenate([both.reshape(receivers, rows_each, 2 * head_width), stats], 1)
    arrived = lax.all_to_all(sent, ("seq_1", "head"), 0, 0, tiled=True)
    stats = arrived[:, rows_each:].reshape(receivers, 16, rows_each).astype(jnp.float32)
    stats = stats.reshape(row_groups, head_count, 16, rows_each)
    arrived = arrived[:, :rows_each].astype(jnp.float32)
    arrived = arrived.reshape(row_groups, head_count, rows_each, 2 * head_width)
    output, d_output, _, _ = merged_parts(
        arrived[..., :head_width],
        arrived[..., head_width:],
        stats[:, :, 0] + stats[:, :, 1] + stats[:, :, 2],
        stats[:, :, 3] + stats[:, :, 4] + stats[:, :, 5],
    )
    merged = jnp.stack([output, d_output], 0).astype(jnp.bfloat16)
    merged = merged.reshape(2, head_count, heads_here, moe_rows, head_width)
    merged = jnp.transpose(merged, (1, 0, 3, 2, 4)).reshape(
        head_count, 2 * moe_rows, heads_here * head_width
    )
    here = lax.axis_index("head")

    def group_at(offset):
        group = lax.rem(here + offset + head_count, head_count)
        return lax.dynamic_index_in_dim(merged, group, 0, keepdims=False)

    side = 1 - 2 * core
    far_group = group_at(head_count // 2)
    ordered = [group_at(0), group_at(-side), group_at(side)]
    ordered += [
        lax.dynamic_slice_in_dim(far_group, half * half_rows, half_rows, 1)
        for half in (core, 1 - core)
    ]
    attn_rows = project(jnp.concatenate(ordered, 1), out_pieces).reshape(2, moe_rows, model_width)
    row_start = lax.axis_index("head") * moe_rows
    own_tokens = lax.dynamic_slice_in_dim(tokens, row_start, moe_rows, 0).astype(jnp.float32)
    own_tangents = lax.dynamic_slice_in_dim(tangents, row_start, moe_rows, 0).astype(jnp.float32)
    residual = own_tokens + attn_rows[0]
    d_residual = own_tangents + attn_rows[1]
    normed_two, d_normed_two = norm_pair(residual, d_residual, ffn_gain)
    moe_in = jnp.concatenate(
        [normed_two.astype(jnp.bfloat16), d_normed_two.astype(jnp.bfloat16)], 0
    )
    gathered = ring_blocks(moe_in, "seq_0")

    plane_experts = row_groups * head_count
    capacity = 3
    expert_id = plane * plane_experts + jnp.arange(plane_experts, dtype=jnp.int32)
    before = (jnp.arange(moe_rows)[:, None] > jnp.arange(moe_rows)[None, :]).astype(jnp.float32)
    near, far = [0, 1, -1, 2], [-2, 3, -3, -4]
    block_rows = 2 * moe_rows
    slot_rows = 2 * capacity * len(near)
    top_count = routes.shape[1]
    row = jnp.arange(slot_rows, dtype=jnp.int32)
    row_is_tangent = (row // 8 == 1) | (row >= 20)
    row_slot = jnp.where(row < 8, row, jnp.where(row < 20, row - 8, row - 12))
    packs, mixes = [], []
    for group in (near, far):
        info = jnp.stack([routing[k] for k in group], 0)
        named = info[:, :, None, :top_count] == expert_id[None, None, :, None].astype(jnp.float32)
        hit = jnp.sum(named.astype(jnp.float32), axis=3)
        rank = jnp.einsum("ts,bse->bte", before, hit, preferred_element_type=jnp.float32)
        number = jnp.arange(len(group), dtype=jnp.float32)[:, None, None] * capacity + rank
        number = jnp.where(hit > 0.0, number, -1.0).astype(jnp.int32)
        number = jnp.transpose(number, (2, 0, 1))[:, None, :, None, :]
        tangent_half = jnp.arange(2, dtype=jnp.int32)[:, None] == 1
        chosen = (number == row_slot[None, :, None, None, None]) & (
            tangent_half == row_is_tangent[None, :, None, None, None]
        )
        flat = (plane_experts * slot_rows, len(group) * block_rows)
        packs.append(chosen.astype(jnp.bfloat16).reshape(flat))
        parts = []
        for part in range(2):
            share = info[:, :, None, top_count * (1 + part) : top_count * (2 + part)]
            share = jnp.sum(jnp.where(named, share, 0.0), axis=3)
            share = jnp.transpose(share, (2, 0, 1))[:, None, :, None, :]
            parts.append(jnp.where(chosen, share, 0.0).astype(jnp.bfloat16).reshape(flat))
        mixes.append(parts)

    results = []
    for group, pack in zip((near, far), packs):
        source = jnp.concatenate([gathered[k] for k in group], 0)
        outgoing = jnp.dot(pack, source, preferred_element_type=jnp.float32).astype(jnp.bfloat16)
        outgoing = outgoing.reshape(plane_experts, slot_rows, model_width)
        received = lax.all_to_all(outgoing, ("seq_1", "head"), 0, 0, tiled=True)
        results.append(
            expert_rows(received.reshape(plane_experts * slot_rows, model_width), expert_halves)
        )
    share_of = {}
    for group, result, parts in reversed(list(zip((near, far), results, mixes))):
        result = result.reshape(plane_experts, slot_rows, model_width)
        returned = lax.all_to_all(result, ("seq_1", "head"), 0, 0, tiled=True)
        returned = returned.reshape(plane_experts * slot_rows, model_width)
        down = (((0,), (0,)), ((), ()))
        mixed = lax.dot_general(
            parts[0], returned, down, preferred_element_type=jnp.float32
        ) + lax.dot_general(parts[1], returned, down, preferred_element_type=jnp.float32)
        mixed = mixed.reshape(len(group), block_rows, model_width)
        for number, k in enumerate(group):
            share_of[k] = mixed[number]
    low = jnp.bfloat16
    up = shifted(share_of[-4].astype(low), "seq_0", 1)
    down = shifted(share_of[-3].astype(low), "seq_0", -1)
    for k in (3, 2, 1):
        up = shifted((share_of[k] + up.astype(jnp.float32)).astype(low), "seq_0", 1)
    for k in (-2, -1):
        down = shifted((share_of[k] + down.astype(jnp.float32)).astype(low), "seq_0", -1)
    moe_sum = share_of[0] + up.astype(jnp.float32) + down.astype(jnp.float32)
    moe_sum = moe_sum.reshape(2, moe_rows, model_width)
    layer_out = (residual + moe_sum[0]).astype(jnp.bfloat16)
    layer_tangent = (d_residual + moe_sum[1]).astype(jnp.bfloat16)
    return (layer_out, layer_tangent)


def solution(mesh):
    split = Mesh(
        mesh.devices.reshape(mesh.shape["dp"], 8, 4, mesh.shape["head"]),
        ("dp", "seq_0", "seq_1", "head"),
    )
    return jax.shard_map(
        local,
        mesh=split,
        in_specs=(
            P(DP_SEQ, None),
            P(DP_SEQ, None),
            P(),
            P(),
            P(None, "head"),
            P(),
            P(),
            P("head", None),
            P(),
            P(),
            P(SEQ_HEAD, None, "dp"),
            P(SEQ_HEAD, None, "dp"),
            P(SEQ_HEAD, None, "dp"),
            P(DP_SEQ_HEAD, None),
            P(DP_SEQ_HEAD, None),
        ),
        out_specs=(P(DP_SEQ_HEAD, None), P(DP_SEQ_HEAD, None)),
        check_vma=False,
    )
```

```python
import functools

import jax
import jax.numpy as jnp
from jax import lax
from jax.experimental import pallas as pl
from jax.experimental.pallas import tpu as pltpu
from jax.sharding import Mesh
from jax.sharding import PartitionSpec as P

SEQ = ("seq_0", "seq_1")
SEQ_HEAD = ("seq_0", "seq_1", "head")
DP_SEQ = ("dp", "seq_0", "seq_1")
DP_SEQ_HEAD = ("dp", "seq_0", "seq_1", "head")


epsilon = 1e-06
rope_base = 1000000.0
masked_score = -1e30


def rms_norm(values, gain):
    mean_square = jnp.mean(values * values, axis=-1, keepdims=True)
    return values * lax.rsqrt(mean_square + epsilon) * gain


def norm_pair(values, tangent, gain):
    return jax.jvp(lambda inner: rms_norm(inner, gain), (values,), (tangent,))


def rotate(values, positions):
    head_width = values.shape[-1]
    half_width = head_width // 2
    exponent = jnp.arange(half_width, dtype=jnp.float32) * (2.0 / head_width)
    frequency = jnp.power(jnp.float32(rope_base), -exponent)
    angle = positions.astype(jnp.float32)[:, None] * frequency[None, :]
    cosine = jnp.concatenate([jnp.cos(angle), jnp.cos(angle)], -1)[:, None, :]
    sine = jnp.concatenate([jnp.sin(angle), jnp.sin(angle)], -1)[:, None, :]
    first_half = values[..., :half_width]
    second_half = values[..., half_width:]
    turned = jnp.concatenate([-second_half, first_half], -1)
    return values * cosine + turned * sine


def head_prep(values, gain, positions):
    return rotate(rms_norm(values, gain), positions)


def head_pair(values, tangent, gain, positions):
    return jax.jvp(lambda inner: head_prep(inner, gain, positions), (values,), (tangent,))


def bf16_parts(values):
    high = lax.reduce_precision(values, 8, 7)
    rest = values - high
    middle = lax.reduce_precision(rest, 8, 7)
    low = lax.reduce_precision(rest - middle, 8, 7)
    return [high.astype(jnp.bfloat16), middle.astype(jnp.bfloat16), low.astype(jnp.bfloat16)]


def shifted(array, axis, offset):
    size = lax.axis_size(axis)
    return lax.ppermute(array, axis, [(i, (i + offset) % size) for i in range(size)])


def ring_blocks(block, axis):
    size = lax.axis_size(axis)
    found = {0: block}
    up = down = block
    for step in range(1, size // 2 + 1):
        up = shifted(up, axis, 1)
        found[-step] = up
        if 2 * step < size:
            down = shifted(down, axis, -1)
            found[step] = down
    return found


def three_parts(values):
    high = values.astype(jnp.bfloat16).astype(jnp.float32)
    rest = values - high
    middle = rest.astype(jnp.bfloat16).astype(jnp.float32)
    low = rest - middle
    row = lax.broadcasted_iota(jnp.int32, values.shape, 0)
    return jnp.where(row == 0, high, jnp.where(row == 1, middle, jnp.where(row == 2, low, 0.0)))


def attend_kernel(scale, group_rows, moe_rows, span_ref, joint_ref, *refs):
    blocks, out_ref, score_ref = refs[:-2], refs[-2], refs[-1]
    rows, width = joint_ref.shape[0], joint_ref.shape[1] // 2
    joint = joint_ref[...]
    query = joint[:, width:]
    contract = (((1,), (1,)), ((), ()))
    keys = blocks[0].shape[0] // 8 * 8
    shape = (rows, keys)
    row = pl.program_id(0) * rows + lax.broadcasted_iota(jnp.int32, shape, 0)
    own = row // group_rows * keys + row % group_rows // keys * moe_rows + row % moe_rows
    own = own - lax.broadcasted_iota(jnp.int32, shape, 1)
    top = jnp.full(shape, masked_score, jnp.float32)
    for number, block in enumerate(blocks):
        score = lax.dot_general(
            query, block[:, :width], contract, preferred_element_type=jnp.float32
        )
        score = jnp.where(span_ref[number] <= own, score * scale, masked_score)
        score_ref[number] = score
        top = jnp.maximum(top, score)
    top = jnp.max(top, axis=1, keepdims=True)
    total = jnp.zeros(shape, jnp.float32)
    slope = jnp.zeros(shape, jnp.float32)
    sums = jnp.zeros((rows, 2 * width), jnp.float32)
    tilted = jnp.zeros((rows, width), jnp.float32)
    for number, block in enumerate(blocks):
        score = score_ref[number]
        d_score = lax.dot_general(
            joint, block[:, : 2 * width], contract, preferred_element_type=jnp.float32
        ) * scale
        weight = jnp.where(score > 0.5 * masked_score, jnp.exp(score - top), 0.0)
        tilt = weight * d_score
        total = total + weight
        slope = slope + tilt
        sums = sums + jnp.dot(
            weight.astype(jnp.bfloat16), block[:, 2 * width :], preferred_element_type=jnp.float32
        )
        tilted = tilted + jnp.dot(
            tilt.astype(jnp.bfloat16),
            block[:, 2 * width : 3 * width],
            preferred_element_type=jnp.float32,
        )
    total = jnp.sum(total, axis=1, keepdims=True)
    slope = jnp.sum(slope, axis=1, keepdims=True)
    some = total > 0.0
    share = jnp.where(some, 1.0 / jnp.where(some, total, 1.0), 0.0)
    output = sums[:, :width] * share
    mean_slope = slope * share
    d_output = (sums[:, width:] + tilted) * share - mean_slope * output
    level = jnp.where(some, top + jnp.log(jnp.where(some, total, 1.0)), masked_score)
    both = jnp.concatenate([output, d_output], axis=1).astype(jnp.bfloat16)
    lane = lax.broadcasted_iota(jnp.int32, (rows, width), 1)
    figures = jnp.where(lane < width // 2, level, mean_slope)
    each = out_ref.shape[1] - 8
    for number in range(out_ref.shape[0]):
        out_ref[number, :each] = both[number * each : (number + 1) * each]
        turned = figures[number * each : (number + 1) * each].T
        stats = jnp.concatenate(
            [three_parts(turned[:8]), three_parts(turned[width // 2 : width // 2 + 8])], axis=1
        )
        out_ref[number, each:] = stats.astype(jnp.bfloat16)


def attend(spans, joint_query, blocks, receivers, rows_each, group_rows, moe_rows):
    width = joint_query.shape[1]
    count = 2
    rows = count * rows_each
    whole = pl.BlockSpec(blocks[0].shape, lambda i: (0, 0))
    return pl.pallas_call(
        functools.partial(attend_kernel, (width // 2) ** (-0.5), group_rows, moe_rows),
        grid=(receivers // count,),
        in_specs=[
            pl.BlockSpec(memory_space=pltpu.SMEM),
            pl.BlockSpec((rows, width), lambda i: (i, 0)),
            *[whole] * len(blocks),
        ],
        out_specs=pl.BlockSpec((count, rows_each + 8, width), lambda i: (i, 0, 0)),
        out_shape=jax.ShapeDtypeStruct((receivers, rows_each + 8, width), jnp.bfloat16),
        scratch_shapes=[pltpu.VMEM((len(blocks), rows, blocks[0].shape[0]), jnp.float32)],
        compiler_params=pltpu.CompilerParams(vmem_limit_bytes=40 << 20),
        name="attend",
    )(spans, joint_query, *blocks)


def merge_kernel(
    place_ref,
    arrived_ref,
    tokens_ref,
    tangents_ref,
    gain_ref,
    routing_ref,
    w_own,
    w_near_own,
    w_near_other,
    w_far_own,
    w_far_other,
    residual_ref,
    block_ref,
    held_ref,
):
    parts, each = arrived_ref.shape[0], arrived_ref.shape[1] - 8
    width = arrived_ref.shape[2] // 2
    groups = held_ref.shape[0] // 2
    row_groups = parts // groups
    moe_rows = held_ref.shape[1] // 2
    half_cols = held_ref.shape[2]
    for group in range(groups):
        stats = [
            jnp.sum(
                arrived_ref[part * groups + group, each:].astype(jnp.float32),
                axis=0,
                keepdims=True,
            )
            for part in range(row_groups)
        ]
        level = jnp.concatenate([v[:, :width] for v in stats], axis=0)
        slopes = jnp.concatenate([v[:, width:] for v in stats], axis=0)
        raw = jnp.exp(level - jnp.max(level, axis=0, keepdims=True))
        mix = raw / jnp.sum(raw, axis=0, keepdims=True)
        slope = jnp.sum(mix * slopes, axis=0, keepdims=True)
        turned = jnp.concatenate([mix, mix * (slopes - slope)], axis=0).T
        output = d_output = None
        for part in range(row_groups):
            data = arrived_ref[part * groups + group, :each].astype(jnp.float32)
            share = turned[:, part : part + 1]
            tilt = turned[:, row_groups + part : row_groups + part + 1]
            term = share * data[:, :width]
            d_term = share * data[:, width:] + tilt * data[:, :width]
            output = term if output is None else output + term
            d_output = d_term if d_output is None else d_output + d_term
        per_half = half_cols // width
        for head in range(each // moe_rows):
            place = 2 * group + head // per_half
            cols = slice(head % per_half * width, (head % per_half + 1) * width)
            rows = slice(head * moe_rows, (head + 1) * moe_rows)
            held_ref[place, :moe_rows, cols] = output[rows].astype(jnp.bfloat16)
            held_ref[place, moe_rows:, cols] = d_output[rows].astype(jnp.bfloat16)
    here, near_own, near_other, far, core = (place_ref[k] for k in range(5))
    order = [
        (2 * here, w_own, 0),
        (2 * here + 1, w_own, 1),
        (2 * near_own, w_near_own, 0),
        (2 * near_own + 1, w_near_own, 1),
        (2 * near_other, w_near_other, 0),
        (2 * near_other + 1, w_near_other, 1),
        (2 * far + core, w_far_own, 0),
        (2 * far + 1 - core, w_far_other, 0),
    ]
    total = None
    for place, piece, half in order:
        term = jnp.dot(
            held_ref[place],
            piece[half * half_cols : (half + 1) * half_cols],
            preferred_element_type=jnp.float32,
        )
        total = term if total is None else total + term
    start = pl.multiple_of(here * moe_rows, moe_rows)
    own = pl.ds(start, moe_rows)
    residual = tokens_ref[own].astype(jnp.float32) + total[:moe_rows]
    d_residual = tangents_ref[own].astype(jnp.float32) + total[moe_rows:]
    residual_ref[:moe_rows] = residual
    residual_ref[moe_rows:] = d_residual
    gain = gain_ref[...]
    root = lax.rsqrt(jnp.mean(residual * residual, axis=1, keepdims=True) + epsilon)
    slope = jnp.mean(residual * d_residual, axis=1, keepdims=True) * root * root * root
    block_ref[:moe_rows] = (residual * root * gain).astype(jnp.bfloat16)
    d_normed = (d_residual * root - residual * slope) * gain
    block_ref[moe_rows : 2 * moe_rows] = d_normed.astype(jnp.bfloat16)
    block_ref[2 * moe_rows :] = routing_ref[...]


def merge(places, arrived, tokens, tangents, gain, routing, pieces, head_count, moe_rows):
    model_width = tokens.shape[1]
    half_cols = pieces[0].shape[0] // 2
    vmem = pl.BlockSpec(memory_space=pltpu.VMEM)
    return pl.pallas_call(
        merge_kernel,
        in_specs=[pl.BlockSpec(memory_space=pltpu.SMEM)] + [vmem] * (5 + len(pieces)),
        out_specs=(vmem, vmem),
        out_shape=(
            jax.ShapeDtypeStruct((2 * moe_rows, model_width), jnp.float32),
            jax.ShapeDtypeStruct((2 * moe_rows + 8, model_width), jnp.bfloat16),
        ),
        scratch_shapes=[pltpu.VMEM((2 * head_count, 2 * moe_rows, half_cols), jnp.bfloat16)],
        compiler_params=pltpu.CompilerParams(vmem_limit_bytes=48 << 20),
        name="merge",
    )(places, arrived, tokens, tangents, gain, routing, *pieces)


def table_of(refs, rows, number):
    lanes = slice(128 * number, 128 * (number + 1))
    tiles = [ref[rows : rows + 8, lanes].astype(jnp.float32) for ref in refs]
    pairs = [tiles[k] + pltpu.roll(tiles[k + 1], 64, 1) for k in range(0, len(tiles), 2)]
    return jnp.concatenate(pairs, axis=1)


def placing(first_expert, routes, experts, capacity, slot_rows, moe_rows):
    count, cols = routes.shape
    expert = first_expert + lax.broadcasted_iota(jnp.int32, (experts, cols), 0)
    named = [
        jnp.broadcast_to(routes[k : k + 1], (experts, cols)) == expert.astype(jnp.float32)
        for k in range(count)
    ]
    hit = jnp.zeros((experts, cols), jnp.float32)
    for each in named:
        hit = hit + jnp.where(each, 1.0, 0.0)
    source = lax.broadcasted_iota(jnp.int32, (cols, cols), 0)
    target = lax.broadcasted_iota(jnp.int32, (cols, cols), 1)
    before = (source // moe_rows == target // moe_rows) & (source < target)
    rank = jnp.dot(
        hit.astype(jnp.bfloat16),
        jnp.where(before, 1.0, 0.0).astype(jnp.bfloat16),
        preferred_element_type=jnp.float32,
    )
    block = (lax.broadcasted_iota(jnp.int32, (experts, cols), 1) // (2 * moe_rows)).astype(jnp.float32)
    slot = jnp.where(hit > 0.0, block * capacity + rank, -1.0)
    row = lax.broadcasted_iota(jnp.int32, (slot_rows, cols), 0)
    half = lax.broadcasted_iota(jnp.int32, (slot_rows, cols), 1) // moe_rows % 2
    is_tangent = jnp.where((row // 8 == 1) | (row >= 20), 1, 0)
    row_slot = jnp.where(row < 8, row, jnp.where(row < 20, row - 8, row - 12))
    code = jnp.where(half == is_tangent, row_slot, -2).astype(jnp.float32)
    chosen = [
        jnp.broadcast_to(slot[j : j + 1], (slot_rows, cols)) == code for j in range(experts)
    ]
    return chosen, named


def pack_kernel(experts, capacity, slot_rows, moe_rows, first_ref, *refs):
    blocks, out_ref = refs[:-1], refs[-1]
    rows = 2 * moe_rows
    routes = table_of(blocks, rows, 0)
    chosen, _ = placing(first_ref[0], routes, experts, capacity, slot_rows, moe_rows)
    pick = jnp.concatenate([jnp.where(c, 1.0, 0.0) for c in chosen], axis=0).astype(jnp.bfloat16)
    source = jnp.concatenate([block[:rows] for block in blocks], axis=0)
    out_ref[...] = jnp.dot(pick, source, preferred_element_type=jnp.float32).astype(jnp.bfloat16)


def mix_kernel(experts, capacity, slot_rows, moe_rows, first_ref, returned_ref, *refs):
    tables, out_ref = refs[:-1], refs[-1]
    routes = table_of(tables, 0, 0)
    chosen, named = placing(first_ref[0], routes, experts, capacity, slot_rows, moe_rows)
    returned = returned_ref[...]
    total = None
    for number in (1, 2):
        shares = table_of(tables, 0, number)
        share = jnp.zeros(named[0].shape, jnp.float32)
        for k, each in enumerate(named):
            share = share + jnp.where(each, jnp.broadcast_to(shares[k : k + 1], each.shape), 0.0)
        held = jnp.concatenate(
            [
                jnp.where(c, jnp.broadcast_to(share[j : j + 1], c.shape), 0.0)
                for j, c in enumerate(chosen)
            ],
            axis=0,
        )
        term = jnp.dot(
            held.T.astype(jnp.bfloat16), returned, preferred_element_type=jnp.float32
        )
        total = term if total is None else total + term
    out_ref[...] = total


def pack(first, blocks, experts, capacity, slot_rows, moe_rows):
    vmem = pl.BlockSpec(memory_space=pltpu.VMEM)
    return pl.pallas_call(
        functools.partial(pack_kernel, experts, capacity, slot_rows, moe_rows),
        in_specs=[pl.BlockSpec(memory_space=pltpu.SMEM)] + [vmem] * len(blocks),
        out_specs=vmem,
        out_shape=jax.ShapeDtypeStruct((experts * slot_rows, blocks[0].shape[1]), jnp.bfloat16),
        compiler_params=pltpu.CompilerParams(vmem_limit_bytes=40 << 20),
        name="pack",
    )(first, *blocks)


def mixed(first, returned, blocks, experts, capacity, slot_rows, moe_rows):
    vmem = pl.BlockSpec(memory_space=pltpu.VMEM)
    table = pl.BlockSpec((8, 512), lambda i: (2 * moe_rows // 8, 0))
    rows = 2 * moe_rows * len(blocks)
    return pl.pallas_call(
        functools.partial(mix_kernel, experts, capacity, slot_rows, moe_rows),
        grid=(1,),
        in_specs=[
            pl.BlockSpec(memory_space=pltpu.SMEM),
            pl.BlockSpec(returned.shape, lambda i: (0, 0)),
            *[table] * len(blocks),
        ],
        out_specs=pl.BlockSpec((rows, returned.shape[1]), lambda i: (0, 0)),
        out_shape=jax.ShapeDtypeStruct((rows, returned.shape[1]), jnp.float32),
        compiler_params=pltpu.CompilerParams(vmem_limit_bytes=40 << 20),
        name="mixed",
    )(first, returned, *blocks)


def expert_kernel(rows_ref, gate_a, gate_b, up_a, up_b, down_a, down_b, out_ref):
    rows = rows_ref[...]
    count = rows.shape[0]
    hidden = []
    for gate_ref, up_ref in ((gate_a, up_a), (gate_b, up_b)):
        units = gate_ref.shape[1]
        weight = jnp.concatenate([gate_ref[...], up_ref[...]], axis=1)
        both = jnp.dot(rows, weight, preferred_element_type=jnp.float32)
        both = both.reshape(count // 24, 3, 8, 2 * units)
        gate, up = both[..., :units], both[..., units:]

        def pair(gate_value, gate_tangent, up_value, up_tangent):
            sigmoid_gate = jax.nn.sigmoid(gate_value)
            active = gate_value * sigmoid_gate
            active_slope = sigmoid_gate * (1.0 + gate_value * (1.0 - sigmoid_gate))
            primal = active * up_value
            return primal, active_slope * gate_tangent * up_value + active * up_tangent

        primal, tangent = pair(gate[:, 0], gate[:, 1], up[:, 0], up[:, 1])
        mixed_gate, mixed_up = gate[:, 2], up[:, 2]
        turned_gate = pltpu.roll(mixed_gate, 4, 1)
        turned_up = pltpu.roll(mixed_up, 4, 1)
        first = lax.broadcasted_iota(jnp.int32, mixed_gate.shape, 1) < 4
        last_primal, last_tangent = pair(
            jnp.where(first, mixed_gate, turned_gate),
            jnp.where(first, turned_gate, mixed_gate),
            jnp.where(first, mixed_up, turned_up),
            jnp.where(first, turned_up, mixed_up),
        )
        last = jnp.where(first, last_primal, last_tangent)
        units_hidden = jnp.stack([primal, tangent, last], 1).reshape(count, units)
        hidden.append(units_hidden.astype(jnp.bfloat16))
    down = jnp.concatenate([down_a[...], down_b[...]], axis=1)
    result = lax.dot_general(
        jnp.concatenate(hidden, axis=1),
        down,
        (((1,), (1,)), ((), ())),
        preferred_element_type=jnp.float32,
    )
    out_ref[...] = result.astype(out_ref.dtype)


def expert_rows(rows, weights):
    return pl.pallas_call(
        expert_kernel,
        out_shape=jax.ShapeDtypeStruct(rows.shape, jnp.bfloat16),
        compiler_params=pltpu.CompilerParams(vmem_limit_bytes=56 << 20),
        name="expert_rows",
    )(rows, *weights)


def local(
    tokens,
    tangents,
    attn_gain,
    ffn_gain,
    w_query,
    w_key,
    w_value,
    w_out,
    query_gain,
    key_gain,
    expert_gate,
    expert_up,
    expert_down,
    routes,
    route_weights,
):
    tok_count, model_width = tokens.shape
    head_width = query_gain.shape[0]
    heads_here = w_query.shape[1] // head_width
    head_count = lax.axis_size("head")
    moe_rows = tok_count // head_count
    core = lax.axis_index("dp")
    other_core = [(0, 1), (1, 0)]

    half_rows = w_out.shape[0] // 2
    ring = range(head_count)
    sides = [(i, (i + 1) % head_count) for i in ring]
    sides += [(head_count + i, head_count + (i - 1) % head_count) for i in ring]
    near_own = lax.ppermute(w_out, ("dp", "head"), sides)
    far_own = shifted(
        lax.dynamic_slice_in_dim(w_out, core * half_rows, half_rows, 0), "head", head_count // 2
    )
    near_other = lax.ppermute(near_own, "dp", other_core)
    far_other = lax.ppermute(far_own, "dp", other_core)
    out_pieces = (w_out, near_own, near_other, far_own, far_other)

    expert_halves = []
    for half in (expert_gate[0], expert_up[0], expert_down[0]):
        expert_halves += [half, lax.ppermute(half, "dp", other_core)]

    plane = lax.axis_index("seq_0")
    row_in_plane = lax.axis_index("seq_1")
    plane_rows = lax.axis_size("seq_1") * tok_count
    plane_count = lax.axis_size("seq_0")
    first_pos = plane * plane_rows + row_in_plane * tok_count
    positions = first_pos + jnp.arange(tok_count, dtype=jnp.int32)
    kv_count = w_key.shape[1] // head_width
    devices_per_kv = lax.axis_size("head") // kv_count
    kv_start = lax.axis_index("head") // devices_per_kv * head_width
    key_cols = lax.dynamic_slice_in_dim(w_key, kv_start, head_width, 1)
    value_cols = lax.dynamic_slice_in_dim(w_value, kv_start, head_width, 1)
    normed, d_normed = norm_pair(
        tokens.astype(jnp.float32), tangents.astype(jnp.float32), attn_gain
    )
    stacked = jnp.concatenate([normed.astype(jnp.bfloat16), d_normed.astype(jnp.bfloat16)], 0)
    kv_cols = jnp.concatenate([key_cols, value_cols], 1)
    kv_all = jnp.dot(stacked, kv_cols, preferred_element_type=jnp.float32)
    key_all = kv_all[:, :head_width].reshape(2, tok_count, 1, head_width)
    value_all = kv_all[:, head_width:].reshape(2, tok_count, head_width)
    key, d_key = head_pair(key_all[0], key_all[1], key_gain, positions)
    packed = jnp.concatenate(
        [
            key.reshape(tok_count, head_width),
            d_key.reshape(tok_count, head_width),
            value_all[0],
            value_all[1],
        ],
        1,
    ).astype(jnp.bfloat16)
    blocks = ring_blocks(packed, "seq_0")

    top_count = routes.shape[1]
    weight_parts = bf16_parts(route_weights)
    tables = jnp.stack([routes.astype(jnp.bfloat16), weight_parts[0], weight_parts[1]], 0)
    tables = jnp.transpose(tables, (2, 0, 1))
    tables = jnp.concatenate([tables, tables, jnp.zeros_like(tables), jnp.zeros_like(tables)], 2)
    tables = tables.reshape(top_count, 3 * 4 * moe_rows)
    tables = jnp.pad(tables, ((0, 0), (0, model_width - tables.shape[1])))

    query_all = jnp.dot(stacked, w_query, preferred_element_type=jnp.float32)
    query_all = query_all.reshape(2, tok_count, heads_here, head_width)
    query, d_query = head_pair(query_all[0], query_all[1], query_gain, positions)

    def by_receiver(values):
        values = values.astype(jnp.bfloat16).reshape(head_count, moe_rows, heads_here, head_width)
        return jnp.transpose(values, (0, 2, 1, 3)).reshape(tok_count * heads_here, head_width)

    joint_own = jnp.concatenate([by_receiver(d_query), by_receiver(query)], 1)
    own_rows = joint_own.shape[0]
    row_groups = lax.axis_size("seq_1")
    joint_query = lax.all_to_all(
        jnp.broadcast_to(joint_own[None], (row_groups, own_rows, 2 * head_width)),
        "seq_1",
        0,
        0,
        tiled=True,
    ).reshape(row_groups * own_rows, 2 * head_width)
    order = sorted(blocks)
    spans = jnp.stack(
        [
            (lax.rem(plane + k + plane_count, plane_count) - plane) * plane_rows
            + row_in_plane * tok_count
            for k in order
        ]
    ).astype(jnp.int32)
    receivers = row_groups * head_count
    rows_each = heads_here * moe_rows
    sent = attend(
        spans, joint_query, [blocks[k] for k in order], receivers, rows_each, own_rows, moe_rows
    )
    arrived = lax.all_to_all(sent, ("seq_1", "head"), 0, 0, tiled=True)
    here = lax.axis_index("head")
    side = 1 - 2 * core
    places = jnp.stack(
        [
            here,
            lax.rem(here - side + head_count, head_count),
            lax.rem(here + side + head_count, head_count),
            lax.rem(here + head_count // 2, head_count),
            core,
        ]
    ).astype(jnp.int32)
    residual, moe_in = merge(
        places,
        arrived,
        tokens,
        tangents,
        ffn_gain[None],
        tables,
        out_pieces,
        head_count,
        moe_rows,
    )
    gathered = ring_blocks(moe_in, "seq_0")

    plane_experts = row_groups * head_count
    capacity = 3
    first_expert = (plane * plane_experts).astype(jnp.int32)[None]
    near, far = [0, 1, -1, 2], [-2, 3, -3, -4]
    block_rows = 2 * moe_rows
    slot_rows = 2 * capacity * len(near)
    layout = (plane_experts, capacity, slot_rows, moe_rows)

    results = []
    for group in (near, far):
        outgoing = pack(first_expert, [gathered[k] for k in group], *layout)
        outgoing = outgoing.reshape(plane_experts, slot_rows, model_width)
        received = lax.all_to_all(outgoing, ("seq_1", "head"), 0, 0, tiled=True)
        results.append(
            expert_rows(received.reshape(plane_experts * slot_rows, model_width), expert_halves)
        )
    share_of = {}
    for group, result in ((far, results[1]), (near, results[0])):
        result = result.reshape(plane_experts, slot_rows, model_width)
        returned = lax.all_to_all(result, ("seq_1", "head"), 0, 0, tiled=True)
        returned = returned.reshape(plane_experts * slot_rows, model_width)
        sums = mixed(first_expert, returned, [gathered[k] for k in group], *layout)
        sums = sums.reshape(len(group), block_rows, model_width)
        for number, k in enumerate(group):
            share_of[k] = sums[number]
    low = jnp.bfloat16
    up = shifted(share_of[-4].astype(low), "seq_0", 1)
    down = shifted(share_of[-3].astype(low), "seq_0", -1)
    for k in (3, 2, 1):
        up = shifted((share_of[k] + up.astype(jnp.float32)).astype(low), "seq_0", 1)
    for k in (-2, -1):
        down = shifted((share_of[k] + down.astype(jnp.float32)).astype(low), "seq_0", -1)
    moe_sum = share_of[0] + up.astype(jnp.float32) + down.astype(jnp.float32)
    result = (residual + moe_sum).astype(jnp.bfloat16)
    layer_out, layer_tangent = result[:moe_rows], result[moe_rows:]
    return (layer_out, layer_tangent)


def solution(mesh):
    split = Mesh(
        mesh.devices.reshape(mesh.shape["dp"], 8, 4, mesh.shape["head"]),
        ("dp", "seq_0", "seq_1", "head"),
    )
    return jax.shard_map(
        local,
        mesh=split,
        in_specs=(
            P(DP_SEQ, None),
            P(DP_SEQ, None),
            P(),
            P(),
            P(None, "head"),
            P(),
            P(),
            P("head", None),
            P(),
            P(),
            P(SEQ_HEAD, None, "dp"),
            P(SEQ_HEAD, None, "dp"),
            P(SEQ_HEAD, None, "dp"),
            P(DP_SEQ_HEAD, None),
            P(DP_SEQ_HEAD, None),
        ),
        out_specs=(P(DP_SEQ_HEAD, None), P(DP_SEQ_HEAD, None)),
        check_vma=False,
    )
```

```python
import functools

import jax
import jax.numpy as jnp
from jax import lax
from jax.experimental import pallas as pl
from jax.experimental.pallas import tpu as pltpu
from jax.sharding import Mesh
from jax.sharding import PartitionSpec as P


SEQ_HEAD = ("seq_0", "seq_1", "head")
DP_SEQ = ("dp", "seq_0", "seq_1")
DP_SEQ_HEAD = ("dp", "seq_0", "seq_1", "head")


epsilon = 1e-06
rope_base = 1000000.0
masked_score = -1e30


def rms_norm(values, gain):
    mean_square = jnp.mean(values * values, axis=-1, keepdims=True)
    return values * lax.rsqrt(mean_square + epsilon) * gain


def turns_of(positions, head_width):
    half_width = head_width // 2
    exponent = jnp.arange(half_width, dtype=jnp.float32) * (2.0 / head_width)
    frequency = jnp.power(jnp.float32(rope_base), -exponent)
    angle = positions.astype(jnp.float32)[:, None] * frequency[None, :]
    return lax.optimization_barrier((jnp.cos(angle), jnp.sin(angle)))


def rotate(values, turns):
    half_width = values.shape[-1] // 2
    cosine, sine = (jnp.concatenate([t, t], -1)[:, None, :] for t in turns)
    first_half = values[..., :half_width]
    second_half = values[..., half_width:]
    turned = jnp.concatenate([-second_half, first_half], -1)
    return values * cosine + turned * sine


def head_prep(values, gain, turns):
    return rotate(rms_norm(values, gain), turns)


def head_pair(values, tangent, gain, turns):
    return jax.jvp(lambda inner: head_prep(inner, gain, turns), (values,), (tangent,))


def shifted(array, axis, offset):
    size = lax.axis_size(axis)
    return lax.ppermute(array, axis, [(i, (i + offset) % size) for i in range(size)])


def ring_blocks(block, axis):
    size = lax.axis_size(axis)
    found = {0: block}
    up = down = block
    for step in range(1, size // 2 + 1):
        up = shifted(up, axis, 1)
        found[-step] = up
        if 2 * step < size:
            down = shifted(down, axis, -1)
            found[step] = down
    return found


def three_parts(values):
    high = values.astype(jnp.bfloat16).astype(jnp.float32)
    rest = values - high
    middle = rest.astype(jnp.bfloat16).astype(jnp.float32)
    low = rest - middle
    row = lax.broadcasted_iota(jnp.int32, values.shape, 0)
    return jnp.where(row == 0, high, jnp.where(row == 1, middle, jnp.where(row == 2, low, 0.0)))


def attend_kernel(scale, group_rows, moe_rows, span_ref, joint_ref, *refs):
    blocks, (out_ref, held_ref, score_ref) = refs[:-3], refs[-3:]
    rows, width = joint_ref.shape[0], joint_ref.shape[1] // 2
    keys = blocks[0].shape[0]
    chunk = held_ref.shape[1]
    each_chunk = chunk // keys

    @pl.when(pl.program_id(0) == 0)
    def _():
        for number, block in enumerate(blocks):
            start = number % each_chunk * keys
            held_ref[number // each_chunk, start : start + keys] = block[...]

    joint = joint_ref[...]
    query = joint[:, width:]
    contract = (((1,), (1,)), ((), ()))
    shape = (rows, chunk)
    row = pl.program_id(0) * rows + lax.broadcasted_iota(jnp.int32, shape, 0)
    own = row // group_rows * keys + row % group_rows // keys * moe_rows + row % moe_rows
    lane = lax.broadcasted_iota(jnp.int32, shape, 1)
    own = own - lane % keys
    top = jnp.full(shape, masked_score, jnp.float32)
    for number in range(held_ref.shape[0]):
        score = lax.dot_general(
            query, held_ref[number, :, :width], contract, preferred_element_type=jnp.float32
        )
        first = number * each_chunk
        span = jnp.where(lane < keys, span_ref[first], span_ref[first + 1])
        score = jnp.where(span <= own, score * scale, masked_score)
        score_ref[number] = score
        top = jnp.maximum(top, score)
    top = jnp.max(top, axis=1, keepdims=True)
    total = jnp.zeros(shape, jnp.float32)
    slope = jnp.zeros(shape, jnp.float32)
    sums = jnp.zeros((rows, 2 * width), jnp.float32)
    tilted = jnp.zeros((rows, width), jnp.float32)
    for number in range(held_ref.shape[0]):
        score = score_ref[number]
        d_score = lax.dot_general(
            joint, held_ref[number, :, : 2 * width], contract, preferred_element_type=jnp.float32
        ) * scale
        weight = jnp.where(score > 0.5 * masked_score, jnp.exp(score - top), 0.0)
        tilt = weight * d_score
        total = total + weight
        slope = slope + tilt
        sums = sums + jnp.dot(
            weight.astype(jnp.bfloat16),
            held_ref[number, :, 2 * width :],
            preferred_element_type=jnp.float32,
        )
        tilted = tilted + jnp.dot(
            tilt.astype(jnp.bfloat16),
            held_ref[number, :, 2 * width : 3 * width],
            preferred_element_type=jnp.float32,
        )
    total = jnp.sum(total, axis=1, keepdims=True)
    slope = jnp.sum(slope, axis=1, keepdims=True)
    some = total > 0.0
    share = jnp.where(some, 1.0 / jnp.where(some, total, 1.0), 0.0)
    output = sums[:, :width] * share
    mean_slope = slope * share
    d_output = (sums[:, width:] + tilted) * share - mean_slope * output
    level = jnp.where(some, top + jnp.log(jnp.where(some, total, 1.0)), masked_score)
    both = jnp.concatenate([output, d_output], axis=1).astype(jnp.bfloat16)
    lane = lax.broadcasted_iota(jnp.int32, (rows, width), 1)
    figures = jnp.where(lane < width // 2, level, mean_slope)
    each = out_ref.shape[1] - 8
    for number in range(out_ref.shape[0]):
        out_ref[number, :each] = both[number * each : (number + 1) * each]
        turned = figures[number * each : (number + 1) * each].T
        stats = jnp.concatenate(
            [three_parts(turned[:8]), three_parts(turned[width // 2 : width // 2 + 8])], axis=1
        )
        out_ref[number, each:] = stats.astype(jnp.bfloat16)


def attend(spans, joint_query, blocks, receivers, rows_each, group_rows, moe_rows):
    width = joint_query.shape[1]
    count = 2
    rows = count * rows_each
    whole = pl.BlockSpec(blocks[0].shape, lambda i: (0, 0))
    return pl.pallas_call(
        functools.partial(attend_kernel, (width // 2) ** (-0.5), group_rows, moe_rows),
        grid=(receivers // count,),
        in_specs=[
            pl.BlockSpec(memory_space=pltpu.SMEM),
            pl.BlockSpec((rows, width), lambda i: (i, 0)),
            *[whole] * len(blocks),
        ],
        out_specs=pl.BlockSpec((count, rows_each + 8, width), lambda i: (i, 0, 0)),
        out_shape=jax.ShapeDtypeStruct((receivers, rows_each + 8, width), jnp.bfloat16),
        scratch_shapes=[
            pltpu.VMEM((len(blocks) // 2, 2 * blocks[0].shape[0], blocks[0].shape[1]), jnp.bfloat16),
            pltpu.VMEM((len(blocks) // 2, rows, 2 * blocks[0].shape[0]), jnp.float32),
        ],
        compiler_params=pltpu.CompilerParams(vmem_limit_bytes=40 << 20),
        name="attend",
    )(spans, joint_query, *blocks)


def merge_kernel(
    place_ref,
    arrived_ref,
    tokens_ref,
    tangents_ref,
    gain_ref,
    routing_ref,
    w_own,
    w_near_own,
    w_near_other,
    w_far_own,
    w_far_other,
    residual_ref,
    block_ref,
    held_ref,
    sum_ref,
):
    parts, each = arrived_ref.shape[0], arrived_ref.shape[1] - 8
    width = arrived_ref.shape[2] // 2
    groups = held_ref.shape[0] // 2
    row_groups = parts // groups
    moe_rows = held_ref.shape[1] // 2
    half_cols = held_ref.shape[2]

    def merge_group(group, carry):
        stats = [
            jnp.sum(
                arrived_ref[part * groups + group, each:].astype(jnp.float32),
                axis=0,
                keepdims=True,
            )
            for part in range(row_groups)
        ]
        level = jnp.concatenate([v[:, :width] for v in stats], axis=0)
        slopes = jnp.concatenate([v[:, width:] for v in stats], axis=0)
        raw = jnp.exp(level - jnp.max(level, axis=0, keepdims=True))
        mix = raw / jnp.sum(raw, axis=0, keepdims=True)
        slope = jnp.sum(mix * slopes, axis=0, keepdims=True)
        turned = jnp.concatenate([mix, mix * (slopes - slope)], axis=0).T
        output = d_output = None
        for part in range(row_groups):
            data = arrived_ref[part * groups + group, :each].astype(jnp.float32)
            share = turned[:, part : part + 1]
            tilt = turned[:, row_groups + part : row_groups + part + 1]
            term = share * data[:, :width]
            d_term = share * data[:, width:] + tilt * data[:, :width]
            output = term if output is None else output + term
            d_output = d_term if d_output is None else d_output + d_term
        per_half = half_cols // width
        for head in range(each // moe_rows):
            place = 2 * group + head // per_half
            cols = slice(head % per_half * width, (head % per_half + 1) * width)
            rows = slice(head * moe_rows, (head + 1) * moe_rows)
            held_ref[place, :moe_rows, cols] = output[rows].astype(jnp.bfloat16)
            held_ref[place, moe_rows:, cols] = d_output[rows].astype(jnp.bfloat16)
        return carry

    lax.fori_loop(0, groups, merge_group, 0)
    here, near_own, near_other, far, core = (place_ref[k] for k in range(5))
    order = [
        (2 * here, w_own, 0),
        (2 * here + 1, w_own, 1),
        (2 * near_own, w_near_own, 0),
        (2 * near_own + 1, w_near_own, 1),
        (2 * near_other, w_near_other, 0),
        (2 * near_other + 1, w_near_other, 1),
        (2 * far + core, w_far_own, 0),
        (2 * far + 1 - core, w_far_other, 0),
    ]
    step = sum_ref.shape[1] // 4

    def project(n, carry):
        cols = pl.ds(pl.multiple_of(n * step, step), step)
        total = None
        for place, piece, half in order:
            term = jnp.dot(
                held_ref[place],
                piece[half * half_cols : (half + 1) * half_cols, cols],
                preferred_element_type=jnp.float32,
            )
            total = term if total is None else total + term
        sum_ref[:, cols] = total
        return carry

    lax.fori_loop(0, sum_ref.shape[1] // step, project, 0)
    start = pl.multiple_of(here * moe_rows, moe_rows)
    own = pl.ds(start, moe_rows)
    residual = tokens_ref[own].astype(jnp.float32) + sum_ref[:moe_rows]
    d_residual = tangents_ref[own].astype(jnp.float32) + sum_ref[moe_rows:]
    residual_ref[:moe_rows] = residual
    residual_ref[moe_rows:] = d_residual
    gain = gain_ref[...]
    root = lax.rsqrt(jnp.mean(residual * residual, axis=1, keepdims=True) + epsilon)
    slope = jnp.mean(residual * d_residual, axis=1, keepdims=True) * root * root * root
    block_ref[:moe_rows] = (residual * root * gain).astype(jnp.bfloat16)
    d_normed = (d_residual * root - residual * slope) * gain
    block_ref[moe_rows : 2 * moe_rows] = d_normed.astype(jnp.bfloat16)
    block_ref[2 * moe_rows :] = routing_ref[...]


def merge(places, arrived, tokens, tangents, gain, routing, pieces, head_count, moe_rows):
    model_width = tokens.shape[1]
    half_cols = pieces[0].shape[0] // 2
    vmem = pl.BlockSpec(memory_space=pltpu.VMEM)
    return pl.pallas_call(
        merge_kernel,
        in_specs=[pl.BlockSpec(memory_space=pltpu.SMEM)] + [vmem] * (5 + len(pieces)),
        out_specs=(vmem, vmem),
        out_shape=(
            jax.ShapeDtypeStruct((2 * moe_rows, model_width), jnp.float32),
            jax.ShapeDtypeStruct((2 * moe_rows + 8, model_width), jnp.bfloat16),
        ),
        scratch_shapes=[
            pltpu.VMEM((2 * head_count, 2 * moe_rows, half_cols), jnp.bfloat16),
            pltpu.VMEM((2 * moe_rows, model_width), jnp.float32),
        ],
        compiler_params=pltpu.CompilerParams(vmem_limit_bytes=48 << 20),
        name="merge",
    )(places, arrived, tokens, tangents, gain, routing, *pieces)


def norm_kernel(tokens_ref, tangents_ref, gain_ref, out_ref):
    values = tokens_ref[...].astype(jnp.float32)
    tangent = tangents_ref[...].astype(jnp.float32)
    gain = gain_ref[...]
    root = lax.rsqrt(jnp.mean(values * values, axis=1, keepdims=True) + epsilon)
    slope = jnp.mean(values * tangent, axis=1, keepdims=True) * root * root * root
    out_ref[0] = (values * root * gain).astype(jnp.bfloat16)
    out_ref[1] = ((tangent * root - values * slope) * gain).astype(jnp.bfloat16)


def norm_rows(tokens, tangents, gain):
    count, width = tokens.shape
    rows = count // 4
    row_block = pl.BlockSpec((rows, width), lambda i: (i, 0))
    return pl.pallas_call(
        norm_kernel,
        grid=(count // rows,),
        in_specs=[row_block, row_block, pl.BlockSpec((1, width), lambda i: (0, 0))],
        out_specs=pl.BlockSpec((2, rows, width), lambda i: (0, i, 0)),
        out_shape=jax.ShapeDtypeStruct((2, count, width), jnp.bfloat16),
        name="norm_rows",
    )(tokens, tangents, gain)


def table_of(refs, rows, number):
    lanes = slice(128 * number, 128 * (number + 1))
    tiles = [ref[rows : rows + 8, lanes].astype(jnp.float32) for ref in refs]
    pairs = [tiles[k] + pltpu.roll(tiles[k + 1], 64, 1) for k in range(0, len(tiles), 2)]
    return jnp.concatenate(pairs, axis=1)


def placing(first_expert, routes, experts, capacity, slot_rows, moe_rows):
    count, cols = routes.shape
    expert = first_expert + lax.broadcasted_iota(jnp.int32, (experts, cols), 0)
    named = [
        jnp.broadcast_to(routes[k : k + 1], (experts, cols)) == expert.astype(jnp.float32)
        for k in range(count)
    ]
    hit = jnp.zeros((experts, cols), jnp.float32)
    for each in named:
        hit = hit + jnp.where(each, 1.0, 0.0)
    source = lax.broadcasted_iota(jnp.int32, (cols, cols), 0)
    target = lax.broadcasted_iota(jnp.int32, (cols, cols), 1)
    before = (source // moe_rows == target // moe_rows) & (source < target)
    rank = jnp.dot(
        hit.astype(jnp.bfloat16),
        jnp.where(before, 1.0, 0.0).astype(jnp.bfloat16),
        preferred_element_type=jnp.float32,
    )
    block = (lax.broadcasted_iota(jnp.int32, (experts, cols), 1) // (2 * moe_rows)).astype(jnp.float32)
    slot = jnp.where(hit > 0.0, block * capacity + rank, -1.0)
    row = lax.broadcasted_iota(jnp.int32, (slot_rows, cols), 0)
    half = lax.broadcasted_iota(jnp.int32, (slot_rows, cols), 1) // moe_rows % 2
    is_tangent = jnp.where((row // 8 == 1) | (row >= 20), 1, 0)
    row_slot = jnp.where(row < 8, row, jnp.where(row < 20, row - 8, row - 12))
    code = jnp.where(half == is_tangent, row_slot, -2).astype(jnp.float32)
    chosen = [
        jnp.broadcast_to(slot[j : j + 1], (slot_rows, cols)) == code for j in range(experts)
    ]
    return chosen, named


def pack_kernel(experts, capacity, slot_rows, moe_rows, first_ref, *refs):
    blocks, out_ref = refs[:-1], refs[-1]
    rows = 2 * moe_rows
    routes = table_of(blocks, rows, 0)
    chosen, _ = placing(first_ref[0], routes, experts, capacity, slot_rows, moe_rows)
    pick = jnp.concatenate([jnp.where(c, 1.0, 0.0) for c in chosen], axis=0).astype(jnp.bfloat16)
    source = jnp.concatenate([block[:rows] for block in blocks], axis=0)
    out_ref[...] = jnp.dot(pick, source, preferred_element_type=jnp.float32).astype(jnp.bfloat16)


def mix_kernel(experts, capacity, slot_rows, moe_rows, first_ref, returned_ref, *refs):
    tables, out_ref = refs[:-1], refs[-1]
    routes = table_of(tables, 0, 0)
    chosen, named = placing(first_ref[0], routes, experts, capacity, slot_rows, moe_rows)
    shares = table_of(tables, 0, 1)
    share = jnp.zeros(named[0].shape, jnp.float32)
    for k, each in enumerate(named):
        share = share + jnp.where(each, jnp.broadcast_to(shares[k : k + 1], each.shape), 0.0)
    held = jnp.concatenate(
        [
            jnp.where(c, jnp.broadcast_to(share[j : j + 1], c.shape), 0.0)
            for j, c in enumerate(chosen)
        ],
        axis=0,
    )
    out_ref[...] = jnp.dot(
        held.T.astype(jnp.bfloat16), returned_ref[...], preferred_element_type=jnp.float32
    )


def pack(first, blocks, experts, capacity, slot_rows, moe_rows):
    vmem = pl.BlockSpec(memory_space=pltpu.VMEM)
    return pl.pallas_call(
        functools.partial(pack_kernel, experts, capacity, slot_rows, moe_rows),
        in_specs=[pl.BlockSpec(memory_space=pltpu.SMEM)] + [vmem] * len(blocks),
        out_specs=vmem,
        out_shape=jax.ShapeDtypeStruct((experts * slot_rows, blocks[0].shape[1]), jnp.bfloat16),
        compiler_params=pltpu.CompilerParams(vmem_limit_bytes=40 << 20),
        name="pack",
    )(first, *blocks)


def mixed(first, returned, blocks, experts, capacity, slot_rows, moe_rows):
    vmem = pl.BlockSpec(memory_space=pltpu.VMEM)
    table = pl.BlockSpec((8, 256), lambda i: (2 * moe_rows // 8, 0))
    rows = 2 * moe_rows * len(blocks)
    return pl.pallas_call(
        functools.partial(mix_kernel, experts, capacity, slot_rows, moe_rows),
        grid=(1,),
        in_specs=[
            pl.BlockSpec(memory_space=pltpu.SMEM),
            pl.BlockSpec(returned.shape, lambda i: (0, 0)),
            *[table] * len(blocks),
        ],
        out_specs=pl.BlockSpec((rows, returned.shape[1]), lambda i: (0, 0)),
        out_shape=jax.ShapeDtypeStruct((rows, returned.shape[1]), jnp.float32),
        compiler_params=pltpu.CompilerParams(vmem_limit_bytes=40 << 20),
        name="mixed",
    )(first, returned, *blocks)


def expert_kernel(rows_ref, gate_a, up_a, gate_b, up_b, down_a, down_b, out_ref, sum_ref, hidden_ref):
    count, depth = rows_ref.shape
    units = gate_a.shape[1]
    step = depth // 4
    sum_ref[...] = jnp.zeros_like(sum_ref)

    def contract(k, carry):
        part = pl.ds(pl.multiple_of(k * step, step), step)
        for number, weight_ref in enumerate((gate_a, up_a, gate_b, up_b)):
            sum_ref[number] += jnp.dot(
                rows_ref[:, part], weight_ref[part], preferred_element_type=jnp.float32
            )
        return carry

    lax.fori_loop(0, depth // step, contract, 0)

    def pair(gate_value, gate_tangent, up_value, up_tangent):
        sigmoid_gate = jax.nn.sigmoid(gate_value)
        active = gate_value * sigmoid_gate
        active_slope = sigmoid_gate * (1.0 + gate_value * (1.0 - sigmoid_gate))
        primal = active * up_value
        return primal, active_slope * gate_tangent * up_value + active * up_tangent

    groups = 48 if count % 96 else 96

    def activate(number, carry):
        half = number // (count // groups)
        part = pl.ds(pl.multiple_of(number % (count // groups) * groups, groups), groups)
        gate = sum_ref[2 * half, part].reshape(groups // 24, 3, 8, units)
        up = sum_ref[2 * half + 1, part].reshape(groups // 24, 3, 8, units)
        primal, tangent = pair(gate[:, 0], gate[:, 1], up[:, 0], up[:, 1])
        mixed_gate, mixed_up = gate[:, 2], up[:, 2]
        turned_gate = pltpu.roll(mixed_gate, 4, 1)
        turned_up = pltpu.roll(mixed_up, 4, 1)
        first = lax.broadcasted_iota(jnp.int32, mixed_gate.shape, 1) < 4
        last_primal, last_tangent = pair(
            jnp.where(first, mixed_gate, turned_gate),
            jnp.where(first, turned_gate, mixed_gate),
            jnp.where(first, mixed_up, turned_up),
            jnp.where(first, turned_up, mixed_up),
        )
        last = jnp.where(first, last_primal, last_tangent)
        hidden = jnp.stack([primal, tangent, last], 1).reshape(groups, units)
        hidden_ref[half, part] = hidden.astype(jnp.bfloat16)
        return carry

    lax.fori_loop(0, 2 * (count // groups), activate, 0)

    def produce(n, carry):
        part = pl.ds(pl.multiple_of(n * step, step), step)
        across = (((1,), (1,)), ((), ()))
        result = lax.dot_general(
            hidden_ref[0], down_a[part], across, preferred_element_type=jnp.float32
        ) + lax.dot_general(
            hidden_ref[1], down_b[part], across, preferred_element_type=jnp.float32
        )
        out_ref[:, part] = result.astype(out_ref.dtype)
        return carry

    lax.fori_loop(0, depth // step, produce, 0)


def expert_rows(rows, weights):
    gate, up, down, gate_other, up_other, down_other = weights
    count, units = rows.shape[0], gate.shape[1]
    return pl.pallas_call(
        expert_kernel,
        out_shape=jax.ShapeDtypeStruct(rows.shape, jnp.bfloat16),
        scratch_shapes=[
            pltpu.VMEM((4, count, units), jnp.float32),
            pltpu.VMEM((2, count, units), jnp.bfloat16),
        ],
        compiler_params=pltpu.CompilerParams(vmem_limit_bytes=56 << 20),
        name="expert_rows",
    )(rows, gate, up, gate_other, up_other, down, down_other)


def layer(
    tokens,
    tangents,
    attn_gain,
    ffn_gain,
    w_query,
    w_key,
    w_value,
    w_out,
    query_gain,
    key_gain,
    expert_gate,
    expert_up,
    expert_down,
    routes,
    route_weights,
):
    tok_count, model_width = tokens.shape
    head_width = query_gain.shape[0]
    heads_here = w_query.shape[1] // head_width
    head_count = lax.axis_size("head")
    moe_rows = tok_count // head_count
    core = lax.axis_index("dp")
    other_core = [(0, 1), (1, 0)]

    half_rows = w_out.shape[0] // 2
    ring = range(head_count)
    sides = [(i, (i + 1) % head_count) for i in ring]
    sides += [(head_count + i, head_count + (i - 1) % head_count) for i in ring]
    far_rows = lax.dynamic_slice_in_dim(w_out, core * half_rows, half_rows, 0)
    near_own = lax.ppermute(w_out, ("dp", "head"), sides)
    far_own = shifted(far_rows, "head", head_count // 2)
    near_other = lax.ppermute(near_own, "dp", other_core)
    far_other = lax.ppermute(far_own, "dp", other_core)
    out_pieces = (w_out, near_own, near_other, far_own, far_other)

    own_halves = [expert_gate[0], expert_up[0], expert_down[0]]
    expert_halves = own_halves + [lax.ppermute(half, "dp", other_core) for half in own_halves]

    plane = lax.axis_index("seq_0")
    row_in_plane = lax.axis_index("seq_1")
    plane_rows = lax.axis_size("seq_1") * tok_count
    plane_count = lax.axis_size("seq_0")
    first_pos = plane * plane_rows + row_in_plane * tok_count
    positions = first_pos + jnp.arange(tok_count, dtype=jnp.int32)
    turns = turns_of(positions, head_width)
    kv_count = w_key.shape[1] // head_width
    devices_per_kv = lax.axis_size("head") // kv_count
    kv_start = lax.axis_index("head") // devices_per_kv * head_width
    key_cols = lax.dynamic_slice_in_dim(w_key, kv_start, head_width, 1)
    value_cols = lax.dynamic_slice_in_dim(w_value, kv_start, head_width, 1)
    stacked = norm_rows(tokens, tangents, attn_gain[None]).reshape(2 * tok_count, model_width)
    kv_cols = jnp.concatenate([key_cols, value_cols], 1)
    kv_all = jnp.dot(stacked, kv_cols, preferred_element_type=jnp.float32)
    key_all = kv_all[:, :head_width].reshape(2, tok_count, 1, head_width)
    value_all = kv_all[:, head_width:].reshape(2, tok_count, head_width)
    key, d_key = head_pair(key_all[0], key_all[1], key_gain, turns)
    packed = jnp.concatenate(
        [
            key.reshape(tok_count, head_width),
            d_key.reshape(tok_count, head_width),
            value_all[0],
            value_all[1],
        ],
        1,
    ).astype(jnp.bfloat16)
    blocks = ring_blocks(packed, "seq_0")

    top_count = routes.shape[1]
    tables = jnp.stack([routes.astype(jnp.bfloat16), route_weights.astype(jnp.bfloat16)], 0)
    tables = jnp.transpose(tables, (2, 0, 1))
    tables = jnp.concatenate([tables, tables, jnp.zeros_like(tables), jnp.zeros_like(tables)], 2)
    tables = tables.reshape(top_count, 2 * 4 * moe_rows)
    tables = jnp.pad(tables, ((0, 0), (0, model_width - tables.shape[1])))

    query_all = jnp.dot(stacked, w_query, preferred_element_type=jnp.float32)
    query_all = query_all.reshape(2, tok_count, heads_here, head_width)
    query, d_query = head_pair(query_all[0], query_all[1], query_gain, turns)

    def by_receiver(values):
        values = values.astype(jnp.bfloat16).reshape(head_count, moe_rows, heads_here, head_width)
        return jnp.transpose(values, (0, 2, 1, 3)).reshape(tok_count * heads_here, head_width)

    joint_own = jnp.concatenate([by_receiver(d_query), by_receiver(query)], 1)
    own_rows = joint_own.shape[0]
    row_groups = lax.axis_size("seq_1")
    copies = jnp.broadcast_to(joint_own[None], (row_groups, own_rows, 2 * head_width))
    joint_query = lax.all_to_all(copies, "seq_1", 0, 0, tiled=True)
    joint_query = joint_query.reshape(row_groups * own_rows, 2 * head_width)
    order = sorted(blocks)
    spans = jnp.stack(
        [
            (lax.rem(plane + k + plane_count, plane_count) - plane) * plane_rows
            + row_in_plane * tok_count
            for k in order
        ]
    ).astype(jnp.int32)
    receivers = row_groups * head_count
    rows_each = heads_here * moe_rows
    sent = attend(
        spans, joint_query, [blocks[k] for k in order], receivers, rows_each, own_rows, moe_rows
    )
    arrived = lax.all_to_all(sent, ("seq_1", "head"), 0, 0, tiled=True)
    here = lax.axis_index("head")
    side = 1 - 2 * core
    places = jnp.stack(
        [
            here,
            lax.rem(here - side + head_count, head_count),
            lax.rem(here + side + head_count, head_count),
            lax.rem(here + head_count // 2, head_count),
            core,
        ]
    ).astype(jnp.int32)
    residual, moe_in = merge(
        places,
        arrived,
        tokens,
        tangents,
        ffn_gain[None],
        tables,
        out_pieces,
        head_count,
        moe_rows,
    )
    gathered = ring_blocks(moe_in, "seq_0")

    plane_experts = row_groups * head_count
    capacity = 3
    first_expert = (plane * plane_experts).astype(jnp.int32)[None]
    near, far = [0, 1, -1, 2], [-2, 3, -3, -4]
    block_rows = 2 * moe_rows
    slot_rows = 2 * capacity * len(near)
    layout = (plane_experts, capacity, slot_rows, moe_rows)

    results = []
    for group in (near, far):
        outgoing = pack(first_expert, [gathered[k] for k in group], *layout)
        outgoing = outgoing.reshape(plane_experts, slot_rows, model_width)
        received = lax.all_to_all(outgoing, ("seq_1", "head"), 0, 0, tiled=True)
        results.append(
            expert_rows(received.reshape(plane_experts * slot_rows, model_width), expert_halves)
        )
    share_of = {}
    for group, result in ((far, results[1]), (near, results[0])):
        result = result.reshape(plane_experts, slot_rows, model_width)
        returned = lax.all_to_all(result, ("seq_1", "head"), 0, 0, tiled=True)
        returned = returned.reshape(plane_experts * slot_rows, model_width)
        sums = mixed(first_expert, returned, [gathered[k] for k in group], *layout)
        sums = sums.reshape(len(group), block_rows, model_width)
        for number, k in enumerate(group):
            share_of[k] = sums[number]
    low = jnp.bfloat16
    up = shifted(share_of[-4].astype(low), "seq_0", 1)
    down = shifted(share_of[-3].astype(low), "seq_0", -1)
    for k in (3, 2, 1):
        up = shifted((share_of[k] + up.astype(jnp.float32)).astype(low), "seq_0", 1)
    for k in (-2, -1):
        down = shifted((share_of[k] + down.astype(jnp.float32)).astype(low), "seq_0", -1)
    moe_sum = share_of[0] + up.astype(jnp.float32) + down.astype(jnp.float32)
    result = (residual + moe_sum).astype(jnp.bfloat16)
    layer_out, layer_tangent = result[:moe_rows], result[moe_rows:]
    return (layer_out, layer_tangent)


def solution(mesh):
    split = Mesh(
        mesh.devices.reshape(mesh.shape["dp"], 8, 4, mesh.shape["head"]),
        ("dp", "seq_0", "seq_1", "head"),
    )
    return jax.shard_map(
        layer,
        mesh=split,
        in_specs=(
            P(DP_SEQ, None),
            P(DP_SEQ, None),
            P(),
            P(),
            P(None, "head"),
            P(),
            P(),
            P("head", None),
            P(),
            P(),
            P(SEQ_HEAD, None, "dp"),
            P(SEQ_HEAD, None, "dp"),
            P(SEQ_HEAD, None, "dp"),
            P(DP_SEQ_HEAD, None),
            P(DP_SEQ_HEAD, None),
        ),
        out_specs=(P(DP_SEQ_HEAD, None), P(DP_SEQ_HEAD, None)),
        check_vma=False,
    )
```

```python
import functools

import jax
import jax.numpy as jnp
from jax import lax
from jax.experimental import pallas as pl
from jax.experimental.pallas import tpu as pltpu
from jax.sharding import Mesh
from jax.sharding import PartitionSpec as P


SEQ_HEAD = ("seq_0", "seq_1", "head")
DP_SEQ = ("dp", "seq_0", "seq_1")
DP_SEQ_HEAD = ("dp", "seq_0", "seq_1", "head")


epsilon = 1e-06
rope_base = 1000000.0
masked_score = -1e30


def turns_of(positions, head_width):
    half_width = head_width // 2
    exponent = jnp.arange(half_width, dtype=jnp.float32) * (2.0 / head_width)
    frequency = jnp.power(jnp.float32(rope_base), -exponent)
    angle = positions.astype(jnp.float32)[:, None] * frequency[None, :]
    cosine, sine = jnp.cos(angle), jnp.sin(angle)
    return jnp.concatenate([cosine, cosine], 1), jnp.concatenate([-sine, sine], 1)


def shifted(array, axis, offset):
    size = lax.axis_size(axis)
    return lax.ppermute(array, axis, [(i, (i + offset) % size) for i in range(size)])


def ring_blocks(block, axis):
    size = lax.axis_size(axis)
    found = {0: block}
    up = down = block
    for step in range(1, size // 2 + 1):
        up = shifted(up, axis, 1)
        found[-step] = up
        if 2 * step < size:
            down = shifted(down, axis, -1)
            found[step] = down
    return found


def three_parts(values):
    high = values.astype(jnp.bfloat16).astype(jnp.float32)
    rest = values - high
    middle = rest.astype(jnp.bfloat16).astype(jnp.float32)
    low = rest - middle
    row = lax.broadcasted_iota(jnp.int32, values.shape, 0)
    return jnp.where(row == 0, high, jnp.where(row == 1, middle, jnp.where(row == 2, low, 0.0)))


def attend_kernel(scale, group_rows, moe_rows, span_ref, joint_ref, *refs):
    blocks, (out_ref, held_ref, score_ref) = refs[:-3], refs[-3:]
    rows, width = joint_ref.shape[0], joint_ref.shape[1] // 2
    keys = blocks[0].shape[0]
    chunk = held_ref.shape[1]
    each_chunk = chunk // keys

    @pl.when(pl.program_id(0) == 0)
    def _():
        for number, block in enumerate(blocks):
            start = number % each_chunk * keys
            held_ref[number // each_chunk, start : start + keys] = block[...]

    joint = joint_ref[...]
    query = joint[:, width:]
    contract = (((1,), (1,)), ((), ()))
    shape = (rows, chunk)
    row = pl.program_id(0) * rows + lax.broadcasted_iota(jnp.int32, shape, 0)
    own = row // group_rows * keys + row % group_rows // keys * moe_rows + row % moe_rows
    lane = lax.broadcasted_iota(jnp.int32, shape, 1)
    own = own - lane % keys
    top = jnp.full(shape, masked_score, jnp.float32)
    for number in range(held_ref.shape[0]):
        score = lax.dot_general(
            query, held_ref[number, :, :width], contract, preferred_element_type=jnp.float32
        )
        first = number * each_chunk
        span = jnp.where(lane < keys, span_ref[first], span_ref[first + 1])
        score = jnp.where(span <= own, score * scale, masked_score)
        score_ref[number] = score
        top = jnp.maximum(top, score)
    top = jnp.max(top, axis=1, keepdims=True)
    total = jnp.zeros(shape, jnp.float32)
    slope = jnp.zeros(shape, jnp.float32)
    sums = jnp.zeros((rows, 2 * width), jnp.float32)
    tilted = jnp.zeros((rows, width), jnp.float32)
    for number in range(held_ref.shape[0]):
        score = score_ref[number]
        d_score = lax.dot_general(
            joint, held_ref[number, :, : 2 * width], contract, preferred_element_type=jnp.float32
        ) * scale
        weight = jnp.where(score > 0.5 * masked_score, jnp.exp(score - top), 0.0)
        tilt = weight * d_score
        total = total + weight
        slope = slope + tilt
        sums = sums + jnp.dot(
            weight.astype(jnp.bfloat16),
            held_ref[number, :, 2 * width :],
            preferred_element_type=jnp.float32,
        )
        tilted = tilted + jnp.dot(
            tilt.astype(jnp.bfloat16),
            held_ref[number, :, 2 * width : 3 * width],
            preferred_element_type=jnp.float32,
        )
    total = jnp.sum(total, axis=1, keepdims=True)
    slope = jnp.sum(slope, axis=1, keepdims=True)
    some = total > 0.0
    share = jnp.where(some, 1.0 / jnp.where(some, total, 1.0), 0.0)
    output = sums[:, :width] * share
    mean_slope = slope * share
    d_output = (sums[:, width:] + tilted) * share - mean_slope * output
    level = jnp.where(some, top + jnp.log(jnp.where(some, total, 1.0)), masked_score)
    both = jnp.concatenate([output, d_output], axis=1).astype(jnp.bfloat16)
    lane = lax.broadcasted_iota(jnp.int32, (rows, width), 1)
    figures = jnp.where(lane < width // 2, level, mean_slope)
    each = out_ref.shape[1] - 8
    for number in range(out_ref.shape[0]):
        out_ref[number, :each] = both[number * each : (number + 1) * each]
        turned = figures[number * each : (number + 1) * each].T
        stats = jnp.concatenate(
            [three_parts(turned[:8]), three_parts(turned[width // 2 : width // 2 + 8])], axis=1
        )
        out_ref[number, each:] = stats.astype(jnp.bfloat16)


def attend(spans, joint_query, blocks, receivers, rows_each, group_rows, moe_rows):
    width = joint_query.shape[1]
    count = 2
    rows = count * rows_each
    whole = pl.BlockSpec(blocks[0].shape, lambda i: (0, 0))
    return pl.pallas_call(
        functools.partial(attend_kernel, (width // 2) ** (-0.5), group_rows, moe_rows),
        grid=(receivers // count,),
        in_specs=[
            pl.BlockSpec(memory_space=pltpu.SMEM),
            pl.BlockSpec((rows, width), lambda i: (i, 0)),
            *[whole] * len(blocks),
        ],
        out_specs=pl.BlockSpec((count, rows_each + 8, width), lambda i: (i, 0, 0)),
        out_shape=jax.ShapeDtypeStruct((receivers, rows_each + 8, width), jnp.bfloat16),
        scratch_shapes=[
            pltpu.VMEM((len(blocks) // 2, 2 * blocks[0].shape[0], blocks[0].shape[1]), jnp.bfloat16),
            pltpu.VMEM((len(blocks) // 2, rows, 2 * blocks[0].shape[0]), jnp.float32),
        ],
        compiler_params=pltpu.CompilerParams(vmem_limit_bytes=40 << 20),
        name="attend",
    )(spans, joint_query, *blocks)


def merge_kernel(
    place_ref,
    arrived_ref,
    tokens_ref,
    tangents_ref,
    gain_ref,
    routing_ref,
    w_own,
    w_near_own,
    w_near_other,
    w_far_own,
    w_far_other,
    residual_ref,
    block_ref,
    held_ref,
    sum_ref,
):
    parts, each = arrived_ref.shape[0], arrived_ref.shape[1] - 8
    width = arrived_ref.shape[2] // 2
    groups = held_ref.shape[0] // 2
    row_groups = parts // groups
    moe_rows = held_ref.shape[1] // 2
    half_cols = held_ref.shape[2]

    def merge_group(group, carry):
        stats = [
            jnp.sum(
                arrived_ref[part * groups + group, each:].astype(jnp.float32),
                axis=0,
                keepdims=True,
            )
            for part in range(row_groups)
        ]
        level = jnp.concatenate([v[:, :width] for v in stats], axis=0)
        slopes = jnp.concatenate([v[:, width:] for v in stats], axis=0)
        raw = jnp.exp(level - jnp.max(level, axis=0, keepdims=True))
        mix = raw / jnp.sum(raw, axis=0, keepdims=True)
        slope = jnp.sum(mix * slopes, axis=0, keepdims=True)
        turned = jnp.concatenate([mix, mix * (slopes - slope)], axis=0).T
        output = d_output = None
        for part in range(row_groups):
            data = arrived_ref[part * groups + group, :each].astype(jnp.float32)
            share = turned[:, part : part + 1]
            tilt = turned[:, row_groups + part : row_groups + part + 1]
            term = share * data[:, :width]
            d_term = share * data[:, width:] + tilt * data[:, :width]
            output = term if output is None else output + term
            d_output = d_term if d_output is None else d_output + d_term
        per_half = half_cols // width
        for head in range(each // moe_rows):
            place = 2 * group + head // per_half
            cols = slice(head % per_half * width, (head % per_half + 1) * width)
            rows = slice(head * moe_rows, (head + 1) * moe_rows)
            held_ref[place, :moe_rows, cols] = output[rows].astype(jnp.bfloat16)
            held_ref[place, moe_rows:, cols] = d_output[rows].astype(jnp.bfloat16)
        return carry

    lax.fori_loop(0, groups, merge_group, 0)
    here, near_own, near_other, far, core = (place_ref[k] for k in range(5))
    order = [
        (2 * here, w_own, 0),
        (2 * here + 1, w_own, 1),
        (2 * near_own, w_near_own, 0),
        (2 * near_own + 1, w_near_own, 1),
        (2 * near_other, w_near_other, 0),
        (2 * near_other + 1, w_near_other, 1),
        (2 * far + core, w_far_own, 0),
        (2 * far + 1 - core, w_far_other, 0),
    ]
    step = sum_ref.shape[1] // 4

    def project(n, carry):
        cols = pl.ds(pl.multiple_of(n * step, step), step)
        total = None
        for place, piece, half in order:
            term = jnp.dot(
                held_ref[place],
                piece[half * half_cols : (half + 1) * half_cols, cols],
                preferred_element_type=jnp.float32,
            )
            total = term if total is None else total + term
        sum_ref[:, cols] = total
        return carry

    lax.fori_loop(0, sum_ref.shape[1] // step, project, 0)
    start = pl.multiple_of(here * moe_rows, moe_rows)
    own = pl.ds(start, moe_rows)
    residual = tokens_ref[own].astype(jnp.float32) + sum_ref[:moe_rows]
    d_residual = tangents_ref[own].astype(jnp.float32) + sum_ref[moe_rows:]
    residual_ref[:moe_rows] = residual
    residual_ref[moe_rows:] = d_residual
    gain = gain_ref[...]
    root = lax.rsqrt(jnp.mean(residual * residual, axis=1, keepdims=True) + epsilon)
    slope = jnp.mean(residual * d_residual, axis=1, keepdims=True) * root * root * root
    block_ref[:moe_rows] = (residual * root * gain).astype(jnp.bfloat16)
    d_normed = (d_residual * root - residual * slope) * gain
    block_ref[moe_rows : 2 * moe_rows] = d_normed.astype(jnp.bfloat16)
    block_ref[2 * moe_rows :] = routing_ref[...]


def merge(places, arrived, tokens, tangents, gain, routing, pieces, head_count, moe_rows):
    model_width = tokens.shape[1]
    half_cols = pieces[0].shape[0] // 2
    vmem = pl.BlockSpec(memory_space=pltpu.VMEM)
    return pl.pallas_call(
        merge_kernel,
        in_specs=[pl.BlockSpec(memory_space=pltpu.SMEM)] + [vmem] * (5 + len(pieces)),
        out_specs=(vmem, vmem),
        out_shape=(
            jax.ShapeDtypeStruct((2 * moe_rows, model_width), jnp.float32),
            jax.ShapeDtypeStruct((2 * moe_rows + 8, model_width), jnp.bfloat16),
        ),
        scratch_shapes=[
            pltpu.VMEM((2 * head_count, 2 * moe_rows, half_cols), jnp.bfloat16),
            pltpu.VMEM((2 * moe_rows, model_width), jnp.float32),
        ],
        compiler_params=pltpu.CompilerParams(vmem_limit_bytes=48 << 20),
        name="merge",
    )(places, arrived, tokens, tangents, gain, routing, *pieces)


def turned_pair(values, tangent, gain, cosine, sine):
    root = lax.rsqrt(jnp.mean(values * values, axis=1, keepdims=True) + epsilon)
    slope = jnp.mean(values * tangent, axis=1, keepdims=True) * root * root * root
    normed = values * root * gain
    d_normed = (tangent * root - values * slope) * gain
    half = values.shape[1] // 2
    return (
        normed * cosine + pltpu.roll(normed, half, 1) * sine,
        d_normed * cosine + pltpu.roll(d_normed, half, 1) * sine,
    )


def keys_kernel(
    head_ref,
    tokens_ref,
    tangents_ref,
    gain_ref,
    w_key_ref,
    w_value_ref,
    key_gain_ref,
    cosine_ref,
    sine_ref,
    stacked_ref,
    packed_ref,
):
    count = tokens_ref.shape[0]
    step = count // 4
    gain = gain_ref[...]

    def norm(number, carry):
        start = pl.multiple_of(number * step, step)
        part = pl.ds(start, step)
        values = tokens_ref[part].astype(jnp.float32)
        tangent = tangents_ref[part].astype(jnp.float32)
        root = lax.rsqrt(jnp.mean(values * values, axis=1, keepdims=True) + epsilon)
        slope = jnp.mean(values * tangent, axis=1, keepdims=True) * root * root * root
        stacked_ref[part] = (values * root * gain).astype(jnp.bfloat16)
        d_normed = (tangent * root - values * slope) * gain
        stacked_ref[pl.ds(count + start, step)] = d_normed.astype(jnp.bfloat16)
        return carry

    lax.fori_loop(0, count // step, norm, 0)
    stacked = stacked_ref[...]
    width = w_key_ref.shape[1]
    key = jnp.dot(stacked, w_key_ref[...], preferred_element_type=jnp.float32)
    value = jnp.dot(stacked, w_value_ref[...], preferred_element_type=jnp.float32)
    key, d_key = turned_pair(
        key[:count], key[count:], key_gain_ref[...], cosine_ref[...], sine_ref[...]
    )
    for number, part in enumerate((key, d_key, value[:count], value[count:])):
        packed_ref[:, number * width : (number + 1) * width] = part.astype(jnp.bfloat16)


def keys_of(head, tokens, tangents, gain, w_key, w_value, key_gain, cosine, sine):
    count, model_width = tokens.shape
    width = key_gain.shape[1]
    whole = lambda array: pl.BlockSpec(array.shape, lambda i, head: (0, 0))
    column = pl.BlockSpec((model_width, width), lambda i, head: (0, head[0]))
    return pl.pallas_call(
        keys_kernel,
        grid_spec=pltpu.PrefetchScalarGridSpec(
            num_scalar_prefetch=1,
            grid=(1,),
            in_specs=[
                whole(tokens),
                whole(tangents),
                whole(gain),
                column,
                column,
                whole(key_gain),
                whole(cosine),
                whole(sine),
            ],
            out_specs=(
                pl.BlockSpec((2 * count, model_width), lambda i, head: (0, 0)),
                pl.BlockSpec((count, 4 * width), lambda i, head: (0, 0)),
            ),
        ),
        out_shape=(
            jax.ShapeDtypeStruct((2 * count, model_width), jnp.bfloat16),
            jax.ShapeDtypeStruct((count, 4 * width), jnp.bfloat16),
        ),
        name="keys_of",
    )(head, tokens, tangents, gain, w_key, w_value, key_gain, cosine, sine)


def queries_kernel(moe_rows, stacked_ref, weight_ref, gain_ref, cosine_ref, sine_ref, out_ref):
    count = stacked_ref.shape[0] // 2
    width = gain_ref.shape[1]
    heads = weight_ref.shape[1] // width
    query_all = jnp.dot(stacked_ref[...], weight_ref[...], preferred_element_type=jnp.float32)
    for head in range(heads):
        column = query_all[:, head * width : (head + 1) * width]
        query, d_query = turned_pair(
            column[:count], column[count:], gain_ref[...], cosine_ref[...], sine_ref[...]
        )
        joint = jnp.concatenate([d_query, query], axis=1).astype(jnp.bfloat16)
        for receiver in range(count // moe_rows):
            start = (receiver * heads + head) * moe_rows
            for copy in range(out_ref.shape[0]):
                out_ref[copy, start : start + moe_rows] = joint[
                    receiver * moe_rows : (receiver + 1) * moe_rows
                ]


def queries_of(stacked, weight, gain, cosine, sine, copies, moe_rows):
    width = gain.shape[1]
    rows = stacked.shape[0] // 2 * (weight.shape[1] // width)
    return pl.pallas_call(
        functools.partial(queries_kernel, moe_rows),
        out_shape=jax.ShapeDtypeStruct((copies, rows, 2 * width), jnp.bfloat16),
        name="queries_of",
    )(stacked, weight, gain, cosine, sine)


def table_of(refs, rows, number):
    lanes = slice(128 * number, 128 * (number + 1))
    tiles = [ref[rows : rows + 8, lanes].astype(jnp.float32) for ref in refs]
    pairs = [tiles[k] + pltpu.roll(tiles[k + 1], 64, 1) for k in range(0, len(tiles), 2)]
    return jnp.concatenate(pairs, axis=1)


def placing(first_expert, routes, experts, capacity, slot_rows, moe_rows):
    count, cols = routes.shape
    expert = first_expert + lax.broadcasted_iota(jnp.int32, (experts, cols), 0)
    named = [
        jnp.broadcast_to(routes[k : k + 1], (experts, cols)) == expert.astype(jnp.float32)
        for k in range(count)
    ]
    hit = jnp.zeros((experts, cols), jnp.float32)
    for each in named:
        hit = hit + jnp.where(each, 1.0, 0.0)
    source = lax.broadcasted_iota(jnp.int32, (cols, cols), 0)
    target = lax.broadcasted_iota(jnp.int32, (cols, cols), 1)
    before = (source // moe_rows == target // moe_rows) & (source < target)
    rank = jnp.dot(
        hit.astype(jnp.bfloat16),
        jnp.where(before, 1.0, 0.0).astype(jnp.bfloat16),
        preferred_element_type=jnp.float32,
    )
    block = (lax.broadcasted_iota(jnp.int32, (experts, cols), 1) // (2 * moe_rows)).astype(jnp.float32)
    slot = jnp.where(hit > 0.0, block * capacity + rank, -1.0)
    row = lax.broadcasted_iota(jnp.int32, (slot_rows, cols), 0)
    half = lax.broadcasted_iota(jnp.int32, (slot_rows, cols), 1) // moe_rows % 2
    is_tangent = jnp.where((row // 8 == 1) | (row >= 20), 1, 0)
    row_slot = jnp.where(row < 8, row, jnp.where(row < 20, row - 8, row - 12))
    code = jnp.where(half == is_tangent, row_slot, -2).astype(jnp.float32)
    chosen = [
        jnp.broadcast_to(slot[j : j + 1], (slot_rows, cols)) == code for j in range(experts)
    ]
    return chosen, named


def pack_kernel(experts, capacity, slot_rows, moe_rows, first_ref, *refs):
    blocks, out_ref, table_ref = refs[:-2], refs[-2], refs[-1]
    rows = 2 * moe_rows
    routes = table_of(blocks, rows, 0)
    table_ref[:8] = routes
    table_ref[8:] = table_of(blocks, rows, 1)
    chosen, _ = placing(first_ref[0], routes, experts, capacity, slot_rows, moe_rows)
    pick = jnp.concatenate([jnp.where(c, 1.0, 0.0) for c in chosen], axis=0).astype(jnp.bfloat16)
    source = jnp.concatenate([block[:rows] for block in blocks], axis=0)
    out_ref[...] = jnp.dot(pick, source, preferred_element_type=jnp.float32).astype(jnp.bfloat16)


def mix_kernel(
    experts, capacity, slot_rows, moe_rows, first_ref, returned_ref, table_ref, out_ref
):
    routes = table_ref[:8]
    chosen, named = placing(first_ref[0], routes, experts, capacity, slot_rows, moe_rows)
    shares = table_ref[8:]
    share = jnp.zeros(named[0].shape, jnp.float32)
    for k, each in enumerate(named):
        share = share + jnp.where(each, jnp.broadcast_to(shares[k : k + 1], each.shape), 0.0)
    held = jnp.concatenate(
        [
            jnp.where(c, jnp.broadcast_to(share[j : j + 1], c.shape), 0.0)
            for j, c in enumerate(chosen)
        ],
        axis=0,
    )
    out_ref[...] = jnp.dot(
        held.T.astype(jnp.bfloat16), returned_ref[...], preferred_element_type=jnp.float32
    )


def pack(first, blocks, experts, capacity, slot_rows, moe_rows):
    vmem = pl.BlockSpec(memory_space=pltpu.VMEM)
    return pl.pallas_call(
        functools.partial(pack_kernel, experts, capacity, slot_rows, moe_rows),
        in_specs=[pl.BlockSpec(memory_space=pltpu.SMEM)] + [vmem] * len(blocks),
        out_specs=(vmem, vmem),
        out_shape=(
            jax.ShapeDtypeStruct((experts * slot_rows, blocks[0].shape[1]), jnp.bfloat16),
            jax.ShapeDtypeStruct((16, 2 * moe_rows * len(blocks)), jnp.float32),
        ),
        compiler_params=pltpu.CompilerParams(vmem_limit_bytes=40 << 20),
        name="pack",
    )(first, *blocks)


def mixed(first, returned, table, experts, capacity, slot_rows, moe_rows):
    vmem = pl.BlockSpec(memory_space=pltpu.VMEM)
    return pl.pallas_call(
        functools.partial(mix_kernel, experts, capacity, slot_rows, moe_rows),
        in_specs=[pl.BlockSpec(memory_space=pltpu.SMEM), vmem, vmem],
        out_specs=vmem,
        out_shape=jax.ShapeDtypeStruct((table.shape[1], returned.shape[1]), jnp.float32),
        compiler_params=pltpu.CompilerParams(vmem_limit_bytes=40 << 20),
        name="mixed",
    )(first, returned, table)


def expert_kernel(rows_ref, *refs):
    sources, out_ref, held, (sum_ref, hidden_ref, sems) = refs[:6], refs[6], refs[7:13], refs[13:]
    down_a, down_b = held[4:]
    count, depth = rows_ref.shape
    units = held[0].shape[1]
    step = depth // 4

    def copy(number, k):
        part = pl.ds(pl.multiple_of(k * step, step), step)
        return pltpu.make_async_copy(
            sources[number].at[part], held[number].at[part], sems.at[number, k]
        )

    for numbers in (range(4), range(4, 6)):
        for k in range(depth // step):
            for number in numbers:
                copy(number, k).start()
    sum_ref[...] = jnp.zeros_like(sum_ref)

    def contract(k, carry):
        part = pl.ds(pl.multiple_of(k * step, step), step)
        for number in range(4):
            copy(number, k).wait()
            sum_ref[number] += jnp.dot(
                rows_ref[:, part], held[number][part], preferred_element_type=jnp.float32
            )
        return carry

    lax.fori_loop(0, depth // step, contract, 0)

    def pair(gate_value, gate_tangent, up_value, up_tangent):
        sigmoid_gate = jax.nn.sigmoid(gate_value)
        active = gate_value * sigmoid_gate
        active_slope = sigmoid_gate * (1.0 + gate_value * (1.0 - sigmoid_gate))
        primal = active * up_value
        return primal, active_slope * gate_tangent * up_value + active * up_tangent

    groups = 48 if count % 96 else 96

    def activate(number, carry):
        half = number // (count // groups)
        part = pl.ds(pl.multiple_of(number % (count // groups) * groups, groups), groups)
        gate = sum_ref[2 * half, part].reshape(groups // 24, 3, 8, units)
        up = sum_ref[2 * half + 1, part].reshape(groups // 24, 3, 8, units)
        primal, tangent = pair(gate[:, 0], gate[:, 1], up[:, 0], up[:, 1])
        mixed_gate, mixed_up = gate[:, 2], up[:, 2]
        turned_gate = pltpu.roll(mixed_gate, 4, 1)
        turned_up = pltpu.roll(mixed_up, 4, 1)
        first = lax.broadcasted_iota(jnp.int32, mixed_gate.shape, 1) < 4
        last_primal, last_tangent = pair(
            jnp.where(first, mixed_gate, turned_gate),
            jnp.where(first, turned_gate, mixed_gate),
            jnp.where(first, mixed_up, turned_up),
            jnp.where(first, turned_up, mixed_up),
        )
        last = jnp.where(first, last_primal, last_tangent)
        hidden = jnp.stack([primal, tangent, last], 1).reshape(groups, units)
        hidden_ref[half, part] = hidden.astype(jnp.bfloat16)
        return carry

    lax.fori_loop(0, 2 * (count // groups), activate, 0)

    def produce(n, carry):
        part = pl.ds(pl.multiple_of(n * step, step), step)
        copy(4, n).wait()
        copy(5, n).wait()
        across = (((1,), (1,)), ((), ()))
        result = lax.dot_general(
            hidden_ref[0], down_a[part], across, preferred_element_type=jnp.float32
        ) + lax.dot_general(
            hidden_ref[1], down_b[part], across, preferred_element_type=jnp.float32
        )
        out_ref[:, part] = result.astype(out_ref.dtype)
        return carry

    lax.fori_loop(0, depth // step, produce, 0)


def expert_rows(rows, weights):
    gate, up, down, gate_other, up_other, down_other = weights
    count, (depth, units) = rows.shape[0], gate.shape
    vmem, hbm = (pl.BlockSpec(memory_space=space) for space in (pltpu.VMEM, pl.ANY))
    return pl.pallas_call(
        expert_kernel,
        in_specs=[vmem] + [hbm] * 6,
        out_specs=vmem,
        out_shape=jax.ShapeDtypeStruct(rows.shape, jnp.bfloat16),
        scratch_shapes=[
            *[pltpu.VMEM((depth, units), jnp.bfloat16)] * 6,
            pltpu.VMEM((4, count, units), jnp.float32),
            pltpu.VMEM((2, count, units), jnp.bfloat16),
            pltpu.SemaphoreType.DMA((6, 4)),
        ],
        compiler_params=pltpu.CompilerParams(vmem_limit_bytes=56 << 20),
        name="expert_rows",
    )(rows, gate, up, gate_other, up_other, down, down_other)


def layer(
    tokens,
    tangents,
    attn_gain,
    ffn_gain,
    w_query,
    w_key,
    w_value,
    w_out,
    query_gain,
    key_gain,
    expert_gate,
    expert_up,
    expert_down,
    routes,
    route_weights,
):
    tok_count, model_width = tokens.shape
    head_width = query_gain.shape[0]
    heads_here = w_query.shape[1] // head_width
    head_count = lax.axis_size("head")
    moe_rows = tok_count // head_count
    core = lax.axis_index("dp")
    other_core = [(0, 1), (1, 0)]

    half_rows = w_out.shape[0] // 2
    ring = range(head_count)
    sides = [(i, (i + 1) % head_count) for i in ring]
    sides += [(head_count + i, head_count + (i - 1) % head_count) for i in ring]
    far_rows = lax.dynamic_slice_in_dim(w_out, core * half_rows, half_rows, 0)
    near_own = lax.ppermute(w_out, ("dp", "head"), sides)
    far_own = shifted(far_rows, "head", head_count // 2)
    near_other = lax.ppermute(near_own, "dp", other_core)
    far_other = lax.ppermute(far_own, "dp", other_core)
    out_pieces = (w_out, near_own, near_other, far_own, far_other)

    own_halves = [expert_gate[0], expert_up[0], expert_down[0]]
    expert_halves = own_halves + [lax.ppermute(half, "dp", other_core) for half in own_halves]

    plane = lax.axis_index("seq_0")
    row_in_plane = lax.axis_index("seq_1")
    plane_rows = lax.axis_size("seq_1") * tok_count
    plane_count = lax.axis_size("seq_0")
    first_pos = plane * plane_rows + row_in_plane * tok_count
    positions = first_pos + jnp.arange(tok_count, dtype=jnp.int32)
    cosine, sine = turns_of(positions, head_width)
    kv_count = w_key.shape[1] // head_width
    devices_per_kv = lax.axis_size("head") // kv_count
    kv_head = (lax.axis_index("head") // devices_per_kv).astype(jnp.int32)[None]
    stacked, packed = keys_of(
        kv_head,
        tokens,
        tangents,
        attn_gain[None],
        w_key,
        w_value,
        key_gain[None],
        cosine,
        sine,
    )
    blocks = ring_blocks(packed, "seq_0")

    top_count = routes.shape[1]
    tables = jnp.stack([routes.astype(jnp.bfloat16), route_weights.astype(jnp.bfloat16)], 0)
    tables = jnp.transpose(tables, (2, 0, 1))
    tables = jnp.concatenate([tables, tables, jnp.zeros_like(tables), jnp.zeros_like(tables)], 2)
    tables = tables.reshape(top_count, 2 * 4 * moe_rows)
    tables = jnp.pad(tables, ((0, 0), (0, model_width - tables.shape[1])))

    row_groups = lax.axis_size("seq_1")
    copies = queries_of(stacked, w_query, query_gain[None], cosine, sine, row_groups, moe_rows)
    own_rows = copies.shape[1]
    joint_query = lax.all_to_all(copies, "seq_1", 0, 0, tiled=True)
    joint_query = joint_query.reshape(row_groups * own_rows, 2 * head_width)
    order = sorted(blocks)
    spans = jnp.stack(
        [
            (lax.rem(plane + k + plane_count, plane_count) - plane) * plane_rows
            + row_in_plane * tok_count
            for k in order
        ]
    ).astype(jnp.int32)
    receivers = row_groups * head_count
    rows_each = heads_here * moe_rows
    sent = attend(
        spans, joint_query, [blocks[k] for k in order], receivers, rows_each, own_rows, moe_rows
    )
    arrived = lax.all_to_all(sent, ("seq_1", "head"), 0, 0, tiled=True)
    here = lax.axis_index("head")
    side = 1 - 2 * core
    places = jnp.stack(
        [
            here,
            lax.rem(here - side + head_count, head_count),
            lax.rem(here + side + head_count, head_count),
            lax.rem(here + head_count // 2, head_count),
            core,
        ]
    ).astype(jnp.int32)
    residual, moe_in = merge(
        places,
        arrived,
        tokens,
        tangents,
        ffn_gain[None],
        tables,
        out_pieces,
        head_count,
        moe_rows,
    )
    gathered = ring_blocks(moe_in, "seq_0")

    plane_experts = row_groups * head_count
    capacity = 3
    first_expert = (plane * plane_experts).astype(jnp.int32)[None]
    near, far = [0, 1, -1, 2], [-2, 3, -3, -4]
    block_rows = 2 * moe_rows
    slot_rows = 2 * capacity * len(near)
    layout = (plane_experts, capacity, slot_rows, moe_rows)

    results, lists = [], {}
    for name, group in (("near", near), ("far", far)):
        outgoing, lists[name] = pack(first_expert, [gathered[k] for k in group], *layout)
        outgoing = outgoing.reshape(plane_experts, slot_rows, model_width)
        received = lax.all_to_all(outgoing, ("seq_1", "head"), 0, 0, tiled=True)
        results.append(
            expert_rows(received.reshape(plane_experts * slot_rows, model_width), expert_halves)
        )
    share_of = {}
    for name, group, result in (("far", far, results[1]), ("near", near, results[0])):
        result = result.reshape(plane_experts, slot_rows, model_width)
        returned = lax.all_to_all(result, ("seq_1", "head"), 0, 0, tiled=True)
        returned = returned.reshape(plane_experts * slot_rows, model_width)
        sums = mixed(first_expert, returned, lists[name], *layout)
        sums = sums.reshape(len(group), block_rows, model_width)
        for number, k in enumerate(group):
            share_of[k] = sums[number]
    low = jnp.bfloat16
    up = shifted(share_of[-4].astype(low), "seq_0", 1)
    down = shifted(share_of[-3].astype(low), "seq_0", -1)
    for k in (3, 2, 1):
        up = shifted((share_of[k] + up.astype(jnp.float32)).astype(low), "seq_0", 1)
    for k in (-2, -1):
        down = shifted((share_of[k] + down.astype(jnp.float32)).astype(low), "seq_0", -1)
    moe_sum = share_of[0] + up.astype(jnp.float32) + down.astype(jnp.float32)
    result = (residual + moe_sum).astype(jnp.bfloat16)
    layer_out, layer_tangent = result[:moe_rows], result[moe_rows:]
    return (layer_out, layer_tangent)


def solution(mesh):
    split = Mesh(
        mesh.devices.reshape(mesh.shape["dp"], 8, 4, mesh.shape["head"]),
        ("dp", "seq_0", "seq_1", "head"),
    )
    return jax.shard_map(
        layer,
        mesh=split,
        in_specs=(
            P(DP_SEQ, None),
            P(DP_SEQ, None),
            P(),
            P(),
            P(None, "head"),
            P(),
            P(),
            P("head", None),
            P(),
            P(),
            P(SEQ_HEAD, None, "dp"),
            P(SEQ_HEAD, None, "dp"),
            P(SEQ_HEAD, None, "dp"),
            P(DP_SEQ_HEAD, None),
            P(DP_SEQ_HEAD, None),
        ),
        out_specs=(P(DP_SEQ_HEAD, None), P(DP_SEQ_HEAD, None)),
        check_vma=False,
    )
```

```python
import functools

import jax
import jax.numpy as jnp
from jax import lax
from jax.experimental import pallas as pl
from jax.experimental.pallas import tpu as pltpu
from jax.sharding import Mesh
from jax.sharding import PartitionSpec as P


SEQ_HEAD = ("seq_0", "seq_1", "head")
DP_SEQ = ("dp", "seq_0", "seq_1")
DP_SEQ_HEAD = ("dp", "seq_0", "seq_1", "head")


epsilon = 1e-06
rope_base = 1000000.0
masked_score = -1e30


def turns_of(positions, head_width):
    half_width = head_width // 2
    exponent = jnp.arange(half_width, dtype=jnp.float32) * (2.0 / head_width)
    frequency = jnp.power(jnp.float32(rope_base), -exponent)
    angle = positions.astype(jnp.float32)[:, None] * frequency[None, :]
    cosine, sine = jnp.cos(angle), jnp.sin(angle)
    return jnp.concatenate([cosine, cosine], 1), jnp.concatenate([-sine, sine], 1)


def shifted(array, axis, offset):
    size = lax.axis_size(axis)
    return lax.ppermute(array, axis, [(i, (i + offset) % size) for i in range(size)])


def ring_blocks(block, axis):
    size = lax.axis_size(axis)
    found = {0: block}
    up = down = block
    for step in range(1, size // 2 + 1):
        up = shifted(up, axis, 1)
        found[-step] = up
        if 2 * step < size:
            down = shifted(down, axis, -1)
            found[step] = down
    return found


def three_parts(values):
    high = values.astype(jnp.bfloat16).astype(jnp.float32)
    rest = values - high
    middle = rest.astype(jnp.bfloat16).astype(jnp.float32)
    low = rest - middle
    row = lax.broadcasted_iota(jnp.int32, values.shape, 0)
    return jnp.where(row == 0, high, jnp.where(row == 1, middle, jnp.where(row == 2, low, 0.0)))


def attend_kernel(scale, group_rows, moe_rows, first, count, span_ref, joint_ref, *refs):
    blocks, refs = refs[:count], refs[count:]
    if first:
        sums_ref, figures_ref, held_ref, score_ref = refs
    else:
        old_sums_ref, old_figures_ref, out_ref, held_ref, score_ref = refs
    rows, width = joint_ref.shape[0], joint_ref.shape[1] // 2
    keys = blocks[0].shape[0]
    chunk = held_ref.shape[1]
    each_chunk = chunk // keys

    @pl.when(pl.program_id(0) == 0)
    def _():
        for number, block in enumerate(blocks):
            start = number % each_chunk * keys
            held_ref[number // each_chunk, start : start + keys] = block[...]

    joint = joint_ref[...]
    query = joint[:, width:]
    contract = (((1,), (1,)), ((), ()))
    shape = (rows, chunk)
    row = pl.program_id(0) * rows + lax.broadcasted_iota(jnp.int32, shape, 0)
    own = row // group_rows * keys + row % group_rows // keys * moe_rows + row % moe_rows
    lane = lax.broadcasted_iota(jnp.int32, shape, 1)
    own = own - lane % keys
    top = jnp.full(shape, masked_score, jnp.float32)
    for number in range(held_ref.shape[0]):
        score = lax.dot_general(
            query, held_ref[number, :, :width], contract, preferred_element_type=jnp.float32
        )
        lead = number * each_chunk
        span = jnp.where(lane < keys, span_ref[lead], span_ref[lead + 1])
        score = jnp.where(span <= own, score * scale, masked_score)
        score_ref[number] = score
        top = jnp.maximum(top, score)
    top = jnp.max(top, axis=1, keepdims=True)
    if not first:
        old_top = old_figures_ref[:, :1]
        top = jnp.maximum(top, old_top)
    total = jnp.zeros(shape, jnp.float32)
    slope = jnp.zeros(shape, jnp.float32)
    sums = jnp.zeros((rows, 2 * width), jnp.float32)
    tilted = jnp.zeros((rows, width), jnp.float32)
    for number in range(held_ref.shape[0]):
        score = score_ref[number]
        d_score = lax.dot_general(
            joint, held_ref[number, :, : 2 * width], contract, preferred_element_type=jnp.float32
        ) * scale
        weight = jnp.where(score > 0.5 * masked_score, jnp.exp(score - top), 0.0)
        tilt = weight * d_score
        total = total + weight
        slope = slope + tilt
        sums = sums + jnp.dot(
            weight.astype(jnp.bfloat16),
            held_ref[number, :, 2 * width :],
            preferred_element_type=jnp.float32,
        )
        tilted = tilted + jnp.dot(
            tilt.astype(jnp.bfloat16),
            held_ref[number, :, 2 * width : 3 * width],
            preferred_element_type=jnp.float32,
        )
    total = jnp.sum(total, axis=1, keepdims=True)
    slope = jnp.sum(slope, axis=1, keepdims=True)
    lane = lax.broadcasted_iota(jnp.int32, (rows, width), 1)
    if first:
        sums_ref[:, :width] = sums[:, :width]
        sums_ref[:, width:] = sums[:, width:] + tilted
        figures_ref[...] = jnp.where(lane == 0, top, jnp.where(lane == 1, total, slope))
        return
    fade = jnp.exp(old_top - top)
    total = total + fade * old_figures_ref[:, 1:2]
    slope = slope + fade * old_figures_ref[:, 2:3]
    primal = sums[:, :width] + fade * old_sums_ref[:, :width]
    tangent = sums[:, width:] + tilted + fade * old_sums_ref[:, width:]
    some = total > 0.0
    share = jnp.where(some, 1.0 / jnp.where(some, total, 1.0), 0.0)
    output = primal * share
    mean_slope = slope * share
    d_output = tangent * share - mean_slope * output
    level = jnp.where(some, top + jnp.log(jnp.where(some, total, 1.0)), masked_score)
    both = jnp.concatenate([output, d_output], axis=1).astype(jnp.bfloat16)
    figures = jnp.where(lane < width // 2, level, mean_slope)
    each = out_ref.shape[1] - 8
    for number in range(out_ref.shape[0]):
        out_ref[number, :each] = both[number * each : (number + 1) * each]
        turned = figures[number * each : (number + 1) * each].T
        stats = jnp.concatenate(
            [three_parts(turned[:8]), three_parts(turned[width // 2 : width // 2 + 8])], axis=1
        )
        out_ref[number, each:] = stats.astype(jnp.bfloat16)


def attend(spans, joint_query, blocks, state, receivers, rows_each, group_rows, moe_rows):
    width = joint_query.shape[1]
    count = 2
    rows = count * rows_each
    whole = pl.BlockSpec(blocks[0].shape, lambda i: (0, 0))
    row_block = pl.BlockSpec((rows, width), lambda i: (i, 0))
    half_block = pl.BlockSpec((rows, width // 2), lambda i: (i, 0))
    first = not state
    if first:
        out_specs = (row_block, half_block)
        out_shape = (
            jax.ShapeDtypeStruct((joint_query.shape[0], width), jnp.float32),
            jax.ShapeDtypeStruct((joint_query.shape[0], width // 2), jnp.float32),
        )
    else:
        out_specs = pl.BlockSpec((count, rows_each + 8, width), lambda i: (i, 0, 0))
        out_shape = jax.ShapeDtypeStruct((receivers, rows_each + 8, width), jnp.bfloat16)
    scale = (width // 2) ** (-0.5)
    return pl.pallas_call(
        functools.partial(attend_kernel, scale, group_rows, moe_rows, first, len(blocks)),
        grid=(receivers // count,),
        in_specs=[
            pl.BlockSpec(memory_space=pltpu.SMEM),
            row_block,
            *[whole] * len(blocks),
            *([] if first else [row_block, half_block]),
        ],
        out_specs=out_specs,
        out_shape=out_shape,
        scratch_shapes=[
            pltpu.VMEM((len(blocks) // 2, 2 * blocks[0].shape[0], blocks[0].shape[1]), jnp.bfloat16),
            pltpu.VMEM((len(blocks) // 2, rows, 2 * blocks[0].shape[0]), jnp.float32),
        ],
        compiler_params=pltpu.CompilerParams(vmem_limit_bytes=40 << 20),
        name="attend",
    )(spans, joint_query, *blocks, *state)


def merge_kernel(
    place_ref,
    arrived_ref,
    tokens_ref,
    tangents_ref,
    gain_ref,
    routing_ref,
    w_own,
    w_near_own,
    w_near_other,
    w_far_own,
    w_far_other,
    residual_ref,
    block_ref,
    held_ref,
    sum_ref,
):
    parts, each = arrived_ref.shape[0], arrived_ref.shape[1] - 8
    width = arrived_ref.shape[2] // 2
    groups = held_ref.shape[0] // 2
    row_groups = parts // groups
    moe_rows = held_ref.shape[1] // 2
    half_cols = held_ref.shape[2]

    def merge_group(group, carry):
        stats = [
            jnp.sum(
                arrived_ref[part * groups + group, each:].astype(jnp.float32),
                axis=0,
                keepdims=True,
            )
            for part in range(row_groups)
        ]
        level = jnp.concatenate([v[:, :width] for v in stats], axis=0)
        slopes = jnp.concatenate([v[:, width:] for v in stats], axis=0)
        raw = jnp.exp(level - jnp.max(level, axis=0, keepdims=True))
        mix = raw / jnp.sum(raw, axis=0, keepdims=True)
        slope = jnp.sum(mix * slopes, axis=0, keepdims=True)
        turned = jnp.concatenate([mix, mix * (slopes - slope)], axis=0).T
        output = d_output = None
        for part in range(row_groups):
            data = arrived_ref[part * groups + group, :each].astype(jnp.float32)
            share = turned[:, part : part + 1]
            tilt = turned[:, row_groups + part : row_groups + part + 1]
            term = share * data[:, :width]
            d_term = share * data[:, width:] + tilt * data[:, :width]
            output = term if output is None else output + term
            d_output = d_term if d_output is None else d_output + d_term
        per_half = half_cols // width
        for head in range(each // moe_rows):
            place = 2 * group + head // per_half
            cols = slice(head % per_half * width, (head % per_half + 1) * width)
            rows = slice(head * moe_rows, (head + 1) * moe_rows)
            held_ref[place, :moe_rows, cols] = output[rows].astype(jnp.bfloat16)
            held_ref[place, moe_rows:, cols] = d_output[rows].astype(jnp.bfloat16)
        return carry

    lax.fori_loop(0, groups, merge_group, 0)
    here, near_own, near_other, far, core = (place_ref[k] for k in range(5))
    order = [
        (2 * here, w_own, 0),
        (2 * here + 1, w_own, 1),
        (2 * near_own, w_near_own, 0),
        (2 * near_own + 1, w_near_own, 1),
        (2 * near_other, w_near_other, 0),
        (2 * near_other + 1, w_near_other, 1),
        (2 * far + core, w_far_own, 0),
        (2 * far + 1 - core, w_far_other, 0),
    ]
    step = sum_ref.shape[1] // 4

    def project(n, carry):
        cols = pl.ds(pl.multiple_of(n * step, step), step)
        total = None
        for place, piece, half in order:
            term = jnp.dot(
                held_ref[place],
                piece[half * half_cols : (half + 1) * half_cols, cols],
                preferred_element_type=jnp.float32,
            )
            total = term if total is None else total + term
        sum_ref[:, cols] = total
        return carry

    lax.fori_loop(0, sum_ref.shape[1] // step, project, 0)
    start = pl.multiple_of(here * moe_rows, moe_rows)
    own = pl.ds(start, moe_rows)
    residual = tokens_ref[own].astype(jnp.float32) + sum_ref[:moe_rows]
    d_residual = tangents_ref[own].astype(jnp.float32) + sum_ref[moe_rows:]
    residual_ref[:moe_rows] = residual
    residual_ref[moe_rows:] = d_residual
    gain = gain_ref[...]
    root = lax.rsqrt(jnp.mean(residual * residual, axis=1, keepdims=True) + epsilon)
    slope = jnp.mean(residual * d_residual, axis=1, keepdims=True) * root * root * root
    block_ref[:moe_rows] = (residual * root * gain).astype(jnp.bfloat16)
    d_normed = (d_residual * root - residual * slope) * gain
    block_ref[moe_rows : 2 * moe_rows] = d_normed.astype(jnp.bfloat16)
    block_ref[2 * moe_rows :] = routing_ref[...]


def merge(places, arrived, tokens, tangents, gain, routing, pieces, head_count, moe_rows):
    model_width = tokens.shape[1]
    half_cols = pieces[0].shape[0] // 2
    vmem = pl.BlockSpec(memory_space=pltpu.VMEM)
    return pl.pallas_call(
        merge_kernel,
        in_specs=[pl.BlockSpec(memory_space=pltpu.SMEM)] + [vmem] * (5 + len(pieces)),
        out_specs=(vmem, vmem),
        out_shape=(
            jax.ShapeDtypeStruct((2 * moe_rows, model_width), jnp.float32),
            jax.ShapeDtypeStruct((2 * moe_rows + 8, model_width), jnp.bfloat16),
        ),
        scratch_shapes=[
            pltpu.VMEM((2 * head_count, 2 * moe_rows, half_cols), jnp.bfloat16),
            pltpu.VMEM((2 * moe_rows, model_width), jnp.float32),
        ],
        compiler_params=pltpu.CompilerParams(vmem_limit_bytes=48 << 20),
        name="merge",
    )(places, arrived, tokens, tangents, gain, routing, *pieces)


def turned_pair(values, tangent, gain, cosine, sine):
    root = lax.rsqrt(jnp.mean(values * values, axis=1, keepdims=True) + epsilon)
    slope = jnp.mean(values * tangent, axis=1, keepdims=True) * root * root * root
    normed = values * root * gain
    d_normed = (tangent * root - values * slope) * gain
    half = values.shape[1] // 2
    return (
        normed * cosine + pltpu.roll(normed, half, 1) * sine,
        d_normed * cosine + pltpu.roll(d_normed, half, 1) * sine,
    )


def keys_kernel(
    head_ref,
    tokens_ref,
    tangents_ref,
    gain_ref,
    w_key_ref,
    w_value_ref,
    key_gain_ref,
    cosine_ref,
    sine_ref,
    stacked_ref,
    packed_ref,
):
    count = tokens_ref.shape[0]
    step = count // 4
    gain = gain_ref[...]

    def norm(number, carry):
        start = pl.multiple_of(number * step, step)
        part = pl.ds(start, step)
        values = tokens_ref[part].astype(jnp.float32)
        tangent = tangents_ref[part].astype(jnp.float32)
        root = lax.rsqrt(jnp.mean(values * values, axis=1, keepdims=True) + epsilon)
        slope = jnp.mean(values * tangent, axis=1, keepdims=True) * root * root * root
        stacked_ref[part] = (values * root * gain).astype(jnp.bfloat16)
        d_normed = (tangent * root - values * slope) * gain
        stacked_ref[pl.ds(count + start, step)] = d_normed.astype(jnp.bfloat16)
        return carry

    lax.fori_loop(0, count // step, norm, 0)
    stacked = stacked_ref[...]
    width = w_key_ref.shape[1]
    key = jnp.dot(stacked, w_key_ref[...], preferred_element_type=jnp.float32)
    value = jnp.dot(stacked, w_value_ref[...], preferred_element_type=jnp.float32)
    key, d_key = turned_pair(
        key[:count], key[count:], key_gain_ref[...], cosine_ref[...], sine_ref[...]
    )
    for number, part in enumerate((key, d_key, value[:count], value[count:])):
        packed_ref[:, number * width : (number + 1) * width] = part.astype(jnp.bfloat16)


def keys_of(head, tokens, tangents, gain, w_key, w_value, key_gain, cosine, sine):
    count, model_width = tokens.shape
    width = key_gain.shape[1]
    whole = lambda array: pl.BlockSpec(array.shape, lambda i, head: (0, 0))
    column = pl.BlockSpec((model_width, width), lambda i, head: (0, head[0]))
    return pl.pallas_call(
        keys_kernel,
        grid_spec=pltpu.PrefetchScalarGridSpec(
            num_scalar_prefetch=1,
            grid=(1,),
            in_specs=[
                whole(tokens),
                whole(tangents),
                whole(gain),
                column,
                column,
                whole(key_gain),
                whole(cosine),
                whole(sine),
            ],
            out_specs=(
                pl.BlockSpec((2 * count, model_width), lambda i, head: (0, 0)),
                pl.BlockSpec((count, 4 * width), lambda i, head: (0, 0)),
            ),
        ),
        out_shape=(
            jax.ShapeDtypeStruct((2 * count, model_width), jnp.bfloat16),
            jax.ShapeDtypeStruct((count, 4 * width), jnp.bfloat16),
        ),
        name="keys_of",
    )(head, tokens, tangents, gain, w_key, w_value, key_gain, cosine, sine)


def queries_kernel(moe_rows, stacked_ref, weight_ref, gain_ref, cosine_ref, sine_ref, out_ref):
    count = stacked_ref.shape[0] // 2
    width = gain_ref.shape[1]
    heads = weight_ref.shape[1] // width
    query_all = jnp.dot(stacked_ref[...], weight_ref[...], preferred_element_type=jnp.float32)
    for head in range(heads):
        column = query_all[:, head * width : (head + 1) * width]
        query, d_query = turned_pair(
            column[:count], column[count:], gain_ref[...], cosine_ref[...], sine_ref[...]
        )
        joint = jnp.concatenate([d_query, query], axis=1).astype(jnp.bfloat16)
        for receiver in range(count // moe_rows):
            start = (receiver * heads + head) * moe_rows
            for copy in range(out_ref.shape[0]):
                out_ref[copy, start : start + moe_rows] = joint[
                    receiver * moe_rows : (receiver + 1) * moe_rows
                ]


def queries_of(stacked, weight, gain, cosine, sine, copies, moe_rows):
    width = gain.shape[1]
    rows = stacked.shape[0] // 2 * (weight.shape[1] // width)
    return pl.pallas_call(
        functools.partial(queries_kernel, moe_rows),
        out_shape=jax.ShapeDtypeStruct((copies, rows, 2 * width), jnp.bfloat16),
        name="queries_of",
    )(stacked, weight, gain, cosine, sine)


def table_of(refs, rows, number):
    lanes = slice(128 * number, 128 * (number + 1))
    tiles = [ref[rows : rows + 8, lanes].astype(jnp.float32) for ref in refs]
    pairs = [tiles[k] + pltpu.roll(tiles[k + 1], 64, 1) for k in range(0, len(tiles), 2)]
    return jnp.concatenate(pairs, axis=1)


def placing(first_expert, routes, experts, capacity, slot_rows, moe_rows):
    count, cols = routes.shape
    expert = first_expert + lax.broadcasted_iota(jnp.int32, (experts, cols), 0)
    named = [
        jnp.broadcast_to(routes[k : k + 1], (experts, cols)) == expert.astype(jnp.float32)
        for k in range(count)
    ]
    hit = jnp.zeros((experts, cols), jnp.float32)
    for each in named:
        hit = hit + jnp.where(each, 1.0, 0.0)
    source = lax.broadcasted_iota(jnp.int32, (cols, cols), 0)
    target = lax.broadcasted_iota(jnp.int32, (cols, cols), 1)
    before = (source // moe_rows == target // moe_rows) & (source < target)
    rank = jnp.dot(
        hit.astype(jnp.bfloat16),
        jnp.where(before, 1.0, 0.0).astype(jnp.bfloat16),
        preferred_element_type=jnp.float32,
    )
    block = (lax.broadcasted_iota(jnp.int32, (experts, cols), 1) // (2 * moe_rows)).astype(jnp.float32)
    slot = jnp.where(hit > 0.0, block * capacity + rank, -1.0)
    row = lax.broadcasted_iota(jnp.int32, (slot_rows, cols), 0)
    half = lax.broadcasted_iota(jnp.int32, (slot_rows, cols), 1) // moe_rows % 2
    is_tangent = jnp.where((row // 8 == 1) | (row >= 20), 1, 0)
    row_slot = jnp.where(row < 8, row, jnp.where(row < 20, row - 8, row - 12))
    code = jnp.where(half == is_tangent, row_slot, -2).astype(jnp.float32)
    chosen = [
        jnp.broadcast_to(slot[j : j + 1], (slot_rows, cols)) == code for j in range(experts)
    ]
    return chosen, named


def pack_kernel(experts, capacity, slot_rows, moe_rows, first_ref, *refs):
    blocks, out_ref, table_ref = refs[:-2], refs[-2], refs[-1]
    rows = 2 * moe_rows
    routes = table_of(blocks, rows, 0)
    table_ref[:8] = routes
    table_ref[8:] = table_of(blocks, rows, 1)
    chosen, _ = placing(first_ref[0], routes, experts, capacity, slot_rows, moe_rows)
    pick = jnp.concatenate([jnp.where(c, 1.0, 0.0) for c in chosen], axis=0).astype(jnp.bfloat16)
    source = jnp.concatenate([block[:rows] for block in blocks], axis=0)
    out_ref[...] = jnp.dot(pick, source, preferred_element_type=jnp.float32).astype(jnp.bfloat16)


def mix_kernel(
    experts, capacity, slot_rows, moe_rows, first_ref, returned_ref, table_ref, out_ref
):
    routes = table_ref[:8]
    chosen, named = placing(first_ref[0], routes, experts, capacity, slot_rows, moe_rows)
    shares = table_ref[8:]
    share = jnp.zeros(named[0].shape, jnp.float32)
    for k, each in enumerate(named):
        share = share + jnp.where(each, jnp.broadcast_to(shares[k : k + 1], each.shape), 0.0)
    held = jnp.concatenate(
        [
            jnp.where(c, jnp.broadcast_to(share[j : j + 1], c.shape), 0.0)
            for j, c in enumerate(chosen)
        ],
        axis=0,
    )
    out_ref[...] = jnp.dot(
        held.T.astype(jnp.bfloat16), returned_ref[...], preferred_element_type=jnp.float32
    )


def pack(first, blocks, experts, capacity, slot_rows, moe_rows):
    vmem = pl.BlockSpec(memory_space=pltpu.VMEM)
    return pl.pallas_call(
        functools.partial(pack_kernel, experts, capacity, slot_rows, moe_rows),
        in_specs=[pl.BlockSpec(memory_space=pltpu.SMEM)] + [vmem] * len(blocks),
        out_specs=(vmem, vmem),
        out_shape=(
            jax.ShapeDtypeStruct((experts * slot_rows, blocks[0].shape[1]), jnp.bfloat16),
            jax.ShapeDtypeStruct((16, 2 * moe_rows * len(blocks)), jnp.float32),
        ),
        compiler_params=pltpu.CompilerParams(vmem_limit_bytes=40 << 20),
        name="pack",
    )(first, *blocks)


def mixed(first, returned, table, experts, capacity, slot_rows, moe_rows):
    vmem = pl.BlockSpec(memory_space=pltpu.VMEM)
    return pl.pallas_call(
        functools.partial(mix_kernel, experts, capacity, slot_rows, moe_rows),
        in_specs=[pl.BlockSpec(memory_space=pltpu.SMEM), vmem, vmem],
        out_specs=vmem,
        out_shape=jax.ShapeDtypeStruct((table.shape[1], returned.shape[1]), jnp.float32),
        compiler_params=pltpu.CompilerParams(vmem_limit_bytes=40 << 20),
        name="mixed",
    )(first, returned, table)


def expert_kernel(rows_ref, *refs):
    sources, out_ref, held, (sum_ref, hidden_ref, sems) = refs[:6], refs[6], refs[7:10], refs[10:]
    count, depth = rows_ref.shape
    units = sources[0].shape[1]
    step = depth // 4

    def copy(number, k):
        part = pl.ds(pl.multiple_of(k * step, step), step)
        side = number % 2 * units
        return pltpu.make_async_copy(
            sources[number].at[part],
            held[number // 2].at[part, side : side + units],
            sems.at[number, k],
        )

    for numbers in (range(4), range(4, 6)):
        for k in range(depth // step):
            for number in numbers:
                copy(number, k).start()
    sum_ref[...] = jnp.zeros_like(sum_ref)

    def contract(k, carry):
        part = pl.ds(pl.multiple_of(k * step, step), step)
        for number in range(2):
            copy(2 * number, k).wait()
            copy(2 * number + 1, k).wait()
            sum_ref[number] += jnp.dot(
                rows_ref[:, part], held[number][part], preferred_element_type=jnp.float32
            )
        return carry

    lax.fori_loop(0, depth // step, contract, 0)

    def pair(gate_value, gate_tangent, up_value, up_tangent):
        sigmoid_gate = jax.nn.sigmoid(gate_value)
        active = gate_value * sigmoid_gate
        active_slope = sigmoid_gate * (1.0 + gate_value * (1.0 - sigmoid_gate))
        primal = active * up_value
        return primal, active_slope * gate_tangent * up_value + active * up_tangent

    groups = 48

    def activate(number, carry):
        part = pl.ds(pl.multiple_of(number * groups, groups), groups)
        gate = sum_ref[0, part].reshape(groups // 24, 3, 8, 2 * units)
        up = sum_ref[1, part].reshape(groups // 24, 3, 8, 2 * units)
        primal, tangent = pair(gate[:, 0], gate[:, 1], up[:, 0], up[:, 1])
        mixed_gate, mixed_up = gate[:, 2], up[:, 2]
        turned_gate = pltpu.roll(mixed_gate, 4, 1)
        turned_up = pltpu.roll(mixed_up, 4, 1)
        first = lax.broadcasted_iota(jnp.int32, mixed_gate.shape, 1) < 4
        last_primal, last_tangent = pair(
            jnp.where(first, mixed_gate, turned_gate),
            jnp.where(first, turned_gate, mixed_gate),
            jnp.where(first, mixed_up, turned_up),
            jnp.where(first, turned_up, mixed_up),
        )
        last = jnp.where(first, last_primal, last_tangent)
        hidden = jnp.stack([primal, tangent, last], 1).reshape(groups, 2 * units)
        hidden_ref[part] = hidden.astype(jnp.bfloat16)
        return carry

    lax.fori_loop(0, count // groups, activate, 0)

    def produce(n, carry):
        part = pl.ds(pl.multiple_of(n * step, step), step)
        copy(4, n).wait()
        copy(5, n).wait()
        across = (((1,), (1,)), ((), ()))
        result = lax.dot_general(
            hidden_ref[...], held[2][part], across, preferred_element_type=jnp.float32
        )
        out_ref[:, part] = result.astype(out_ref.dtype)
        return carry

    lax.fori_loop(0, depth // step, produce, 0)


def expert_rows(rows, weights):
    gate, up, down, gate_other, up_other, down_other = weights
    count, (depth, units) = rows.shape[0], gate.shape
    vmem, hbm = (pl.BlockSpec(memory_space=space) for space in (pltpu.VMEM, pl.ANY))
    return pl.pallas_call(
        expert_kernel,
        in_specs=[vmem] + [hbm] * 6,
        out_specs=vmem,
        out_shape=jax.ShapeDtypeStruct(rows.shape, jnp.bfloat16),
        scratch_shapes=[
            *[pltpu.VMEM((depth, 2 * units), jnp.bfloat16)] * 3,
            pltpu.VMEM((2, count, 2 * units), jnp.float32),
            pltpu.VMEM((count, 2 * units), jnp.bfloat16),
            pltpu.SemaphoreType.DMA((6, 4)),
        ],
        compiler_params=pltpu.CompilerParams(vmem_limit_bytes=56 << 20),
        name="expert_rows",
    )(rows, gate, gate_other, up, up_other, down, down_other)


def layer(
    tokens,
    tangents,
    attn_gain,
    ffn_gain,
    w_query,
    w_key,
    w_value,
    w_out,
    query_gain,
    key_gain,
    expert_gate,
    expert_up,
    expert_down,
    routes,
    route_weights,
):
    tok_count, model_width = tokens.shape
    head_width = query_gain.shape[0]
    heads_here = w_query.shape[1] // head_width
    head_count = lax.axis_size("head")
    moe_rows = tok_count // head_count
    core = lax.axis_index("dp")
    other_core = [(0, 1), (1, 0)]

    half_rows = w_out.shape[0] // 2
    ring = range(head_count)
    sides = [(i, (i + 1) % head_count) for i in ring]
    sides += [(head_count + i, head_count + (i - 1) % head_count) for i in ring]
    far_rows = lax.dynamic_slice_in_dim(w_out, core * half_rows, half_rows, 0)
    near_own = lax.ppermute(w_out, ("dp", "head"), sides)
    far_own = shifted(far_rows, "head", head_count // 2)
    near_other = lax.ppermute(near_own, "dp", other_core)
    far_other = lax.ppermute(far_own, "dp", other_core)
    out_pieces = (w_out, near_own, near_other, far_own, far_other)

    own_halves = [expert_gate[0], expert_up[0], expert_down[0]]
    expert_halves = own_halves + [lax.ppermute(half, "dp", other_core) for half in own_halves]

    plane = lax.axis_index("seq_0")
    row_in_plane = lax.axis_index("seq_1")
    plane_rows = lax.axis_size("seq_1") * tok_count
    plane_count = lax.axis_size("seq_0")
    first_pos = plane * plane_rows + row_in_plane * tok_count
    positions = first_pos + jnp.arange(tok_count, dtype=jnp.int32)
    cosine, sine = turns_of(positions, head_width)
    kv_count = w_key.shape[1] // head_width
    devices_per_kv = lax.axis_size("head") // kv_count
    kv_head = (lax.axis_index("head") // devices_per_kv).astype(jnp.int32)[None]
    stacked, packed = keys_of(
        kv_head,
        tokens,
        tangents,
        attn_gain[None],
        w_key,
        w_value,
        key_gain[None],
        cosine,
        sine,
    )
    blocks = ring_blocks(packed, "seq_0")

    top_count = routes.shape[1]
    tables = jnp.stack([routes.astype(jnp.bfloat16), route_weights.astype(jnp.bfloat16)], 0)
    tables = jnp.transpose(tables, (2, 0, 1))
    tables = jnp.concatenate([tables, tables, jnp.zeros_like(tables), jnp.zeros_like(tables)], 2)
    tables = tables.reshape(top_count, 2 * 4 * moe_rows)
    tables = jnp.pad(tables, ((0, 0), (0, model_width - tables.shape[1])))

    row_groups = lax.axis_size("seq_1")
    copies = queries_of(stacked, w_query, query_gain[None], cosine, sine, row_groups, moe_rows)
    own_rows = copies.shape[1]
    joint_query = lax.all_to_all(copies, "seq_1", 0, 0, tiled=True)
    joint_query = joint_query.reshape(row_groups * own_rows, 2 * head_width)
    receivers = row_groups * head_count
    rows_each = heads_here * moe_rows
    state = ()
    for order in ((0, -1, 1, -2), (2, -3, 3, -4)):
        spans = [
            (lax.rem(plane + k + plane_count, plane_count) - plane) * plane_rows
            + row_in_plane * tok_count
            for k in order
        ]
        state = attend(
            jnp.stack(spans).astype(jnp.int32),
            joint_query,
            [blocks[k] for k in order],
            state,
            receivers,
            rows_each,
            own_rows,
            moe_rows,
        )
    sent = state
    arrived = lax.all_to_all(sent, ("seq_1", "head"), 0, 0, tiled=True)
    here = lax.axis_index("head")
    side = 1 - 2 * core
    places = jnp.stack(
        [
            here,
            lax.rem(here - side + head_count, head_count),
            lax.rem(here + side + head_count, head_count),
            lax.rem(here + head_count // 2, head_count),
            core,
        ]
    ).astype(jnp.int32)
    residual, moe_in = merge(
        places,
        arrived,
        tokens,
        tangents,
        ffn_gain[None],
        tables,
        out_pieces,
        head_count,
        moe_rows,
    )
    gathered = ring_blocks(moe_in, "seq_0")

    plane_experts = row_groups * head_count
    capacity = 3
    first_expert = (plane * plane_experts).astype(jnp.int32)[None]
    near, far = [0, 1, -1, 2], [-2, 3, -3, -4]
    block_rows = 2 * moe_rows
    slot_rows = 2 * capacity * len(near)
    layout = (plane_experts, capacity, slot_rows, moe_rows)

    results, lists = [], {}
    for name, group in (("near", near), ("far", far)):
        outgoing, lists[name] = pack(first_expert, [gathered[k] for k in group], *layout)
        outgoing = outgoing.reshape(plane_experts, slot_rows, model_width)
        received = lax.all_to_all(outgoing, ("seq_1", "head"), 0, 0, tiled=True)
        results.append(
            expert_rows(received.reshape(plane_experts * slot_rows, model_width), expert_halves)
        )
    share_of = {}
    for name, group, result in (("far", far, results[1]), ("near", near, results[0])):
        result = result.reshape(plane_experts, slot_rows, model_width)
        returned = lax.all_to_all(result, ("seq_1", "head"), 0, 0, tiled=True)
        returned = returned.reshape(plane_experts * slot_rows, model_width)
        sums = mixed(first_expert, returned, lists[name], *layout)
        sums = sums.reshape(len(group), block_rows, model_width)
        for number, k in enumerate(group):
            share_of[k] = sums[number]
    low = jnp.bfloat16
    up = shifted(share_of[-4].astype(low), "seq_0", 1)
    down = shifted(share_of[-3].astype(low), "seq_0", -1)
    for k in (3, 2, 1):
        up = shifted((share_of[k] + up.astype(jnp.float32)).astype(low), "seq_0", 1)
    for k in (-2, -1):
        down = shifted((share_of[k] + down.astype(jnp.float32)).astype(low), "seq_0", -1)
    moe_sum = share_of[0] + up.astype(jnp.float32) + down.astype(jnp.float32)
    result = (residual + moe_sum).astype(jnp.bfloat16)
    layer_out, layer_tangent = result[:moe_rows], result[moe_rows:]
    return (layer_out, layer_tangent)


def solution(mesh):
    split = Mesh(
        mesh.devices.reshape(mesh.shape["dp"], 8, 4, mesh.shape["head"]),
        ("dp", "seq_0", "seq_1", "head"),
    )
    return jax.shard_map(
        layer,
        mesh=split,
        in_specs=(
            P(DP_SEQ, None),
            P(DP_SEQ, None),
            P(),
            P(),
            P(None, "head"),
            P(),
            P(),
            P("head", None),
            P(),
            P(),
            P(SEQ_HEAD, None, "dp"),
            P(SEQ_HEAD, None, "dp"),
            P(SEQ_HEAD, None, "dp"),
            P(DP_SEQ_HEAD, None),
            P(DP_SEQ_HEAD, None),
        ),
        out_specs=(P(DP_SEQ_HEAD, None), P(DP_SEQ_HEAD, None)),
        check_vma=False,
    )
```

```python
import functools

import jax
import jax.numpy as jnp
from jax import lax
from jax.experimental import pallas as pl
from jax.experimental.pallas import tpu as pltpu
from jax.sharding import Mesh
from jax.sharding import PartitionSpec as P


SEQ_HEAD = ("seq_0", "seq_1", "head")
DP_SEQ = ("dp", "seq_0", "seq_1")
DP_SEQ_HEAD = ("dp", "seq_0", "seq_1", "head")


epsilon = 1e-06
rope_base = 1000000.0
masked_score = -1e30


def turns_of(positions, head_width):
    half_width = head_width // 2
    exponent = jnp.arange(half_width, dtype=jnp.float32) * (2.0 / head_width)
    frequency = jnp.power(jnp.float32(rope_base), -exponent)
    angle = positions.astype(jnp.float32)[:, None] * frequency[None, :]
    cosine, sine = jnp.cos(angle), jnp.sin(angle)
    return jnp.concatenate([cosine, cosine], 1), jnp.concatenate([-sine, sine], 1)


def shifted(array, axis, offset):
    size = lax.axis_size(axis)
    return lax.ppermute(array, axis, [(i, (i + offset) % size) for i in range(size)])


def ring_blocks(block, axis):
    size = lax.axis_size(axis)
    found = {0: block}
    up = down = block
    for step in range(1, size // 2 + 1):
        up = shifted(up, axis, 1)
        found[-step] = up
        if 2 * step < size:
            down = shifted(down, axis, -1)
            found[step] = down
    return found


def three_parts(values):
    high = values.astype(jnp.bfloat16).astype(jnp.float32)
    rest = values - high
    middle = rest.astype(jnp.bfloat16).astype(jnp.float32)
    low = rest - middle
    row = lax.broadcasted_iota(jnp.int32, values.shape, 0)
    return jnp.where(row == 0, high, jnp.where(row == 1, middle, jnp.where(row == 2, low, 0.0)))


def attend_kernel(scale, group_rows, moe_rows, first, count, span_ref, joint_ref, *refs):
    blocks, refs = refs[:count], refs[count:]
    if first:
        sums_ref, figures_ref, held_ref, score_ref = refs
    else:
        old_sums_ref, old_figures_ref, out_ref, held_ref, score_ref = refs
    rows, width = joint_ref.shape[0], joint_ref.shape[1] // 2
    keys = blocks[0].shape[0]
    chunk = held_ref.shape[1]
    each_chunk = chunk // keys

    @pl.when(pl.program_id(0) == 0)
    def _():
        for number, block in enumerate(blocks):
            start = number % each_chunk * keys
            held_ref[number // each_chunk, start : start + keys] = block[...]

    joint = joint_ref[...]
    query = joint[:, width:]
    contract = (((1,), (1,)), ((), ()))
    shape = (rows, chunk)
    row = pl.program_id(0) * rows + lax.broadcasted_iota(jnp.int32, shape, 0)
    own = row // group_rows * keys + row % group_rows // keys * moe_rows + row % moe_rows
    lane = lax.broadcasted_iota(jnp.int32, shape, 1)
    own = own - lane % keys
    top = jnp.full(shape, masked_score, jnp.float32)
    for number in range(held_ref.shape[0]):
        score = lax.dot_general(
            query, held_ref[number, :, :width], contract, preferred_element_type=jnp.float32
        )
        lead = number * each_chunk
        span = jnp.where(lane < keys, span_ref[lead], span_ref[lead + 1])
        score = jnp.where(span <= own, score * scale, masked_score)
        score_ref[number] = score
        top = jnp.maximum(top, score)
    top = jnp.max(top, axis=1, keepdims=True)
    if not first:
        old_top = old_figures_ref[:, :1]
        top = jnp.maximum(top, old_top)
    total = jnp.zeros(shape, jnp.float32)
    slope = jnp.zeros(shape, jnp.float32)
    sums = jnp.zeros((rows, 2 * width), jnp.float32)
    tilted = jnp.zeros((rows, width), jnp.float32)
    for number in range(held_ref.shape[0]):
        score = score_ref[number]
        d_score = lax.dot_general(
            joint, held_ref[number, :, : 2 * width], contract, preferred_element_type=jnp.float32
        ) * scale
        weight = jnp.where(score > 0.5 * masked_score, jnp.exp(score - top), 0.0)
        tilt = weight * d_score
        total = total + weight
        slope = slope + tilt
        sums = sums + jnp.dot(
            weight.astype(jnp.bfloat16),
            held_ref[number, :, 2 * width :],
            preferred_element_type=jnp.float32,
        )
        tilted = tilted + jnp.dot(
            tilt.astype(jnp.bfloat16),
            held_ref[number, :, 2 * width : 3 * width],
            preferred_element_type=jnp.float32,
        )
    total = jnp.sum(total, axis=1, keepdims=True)
    slope = jnp.sum(slope, axis=1, keepdims=True)
    lane = lax.broadcasted_iota(jnp.int32, (rows, width), 1)
    if first:
        sums_ref[:, :width] = sums[:, :width]
        sums_ref[:, width:] = sums[:, width:] + tilted
        figures_ref[...] = jnp.where(lane == 0, top, jnp.where(lane == 1, total, slope))
        return
    fade = jnp.exp(old_top - top)
    total = total + fade * old_figures_ref[:, 1:2]
    slope = slope + fade * old_figures_ref[:, 2:3]
    primal = sums[:, :width] + fade * old_sums_ref[:, :width]
    tangent = sums[:, width:] + tilted + fade * old_sums_ref[:, width:]
    some = total > 0.0
    share = jnp.where(some, 1.0 / jnp.where(some, total, 1.0), 0.0)
    output = primal * share
    mean_slope = slope * share
    d_output = tangent * share - mean_slope * output
    level = jnp.where(some, top + jnp.log(jnp.where(some, total, 1.0)), masked_score)
    both = jnp.concatenate([output, d_output], axis=1).astype(jnp.bfloat16)
    figures = jnp.where(lane < width // 2, level, mean_slope)
    each = out_ref.shape[1] - 8
    for number in range(out_ref.shape[0]):
        out_ref[number, :each] = both[number * each : (number + 1) * each]
        turned = figures[number * each : (number + 1) * each].T
        stats = jnp.concatenate(
            [three_parts(turned[:8]), three_parts(turned[width // 2 : width // 2 + 8])], axis=1
        )
        out_ref[number, each:] = stats.astype(jnp.bfloat16)


def attend(spans, joint_query, blocks, state, receivers, rows_each, group_rows, moe_rows):
    width = joint_query.shape[1]
    count = 4 if state else 2
    rows = count * rows_each
    whole = pl.BlockSpec(blocks[0].shape, lambda i: (0, 0))
    row_block = pl.BlockSpec((rows, width), lambda i: (i, 0))
    half_block = pl.BlockSpec((rows, width // 2), lambda i: (i, 0))
    first = not state
    if first:
        out_specs = (row_block, half_block)
        out_shape = (
            jax.ShapeDtypeStruct((joint_query.shape[0], width), jnp.float32),
            jax.ShapeDtypeStruct((joint_query.shape[0], width // 2), jnp.float32),
        )
    else:
        out_specs = pl.BlockSpec((count, rows_each + 8, width), lambda i: (i, 0, 0))
        out_shape = jax.ShapeDtypeStruct((receivers, rows_each + 8, width), jnp.bfloat16)
    scale = (width // 2) ** (-0.5)
    return pl.pallas_call(
        functools.partial(attend_kernel, scale, group_rows, moe_rows, first, len(blocks)),
        grid=(receivers // count,),
        in_specs=[
            pl.BlockSpec(memory_space=pltpu.SMEM),
            row_block,
            *[whole] * len(blocks),
            *([] if first else [row_block, half_block]),
        ],
        out_specs=out_specs,
        out_shape=out_shape,
        scratch_shapes=[
            pltpu.VMEM((len(blocks) // 2, 2 * blocks[0].shape[0], blocks[0].shape[1]), jnp.bfloat16),
            pltpu.VMEM((len(blocks) // 2, rows, 2 * blocks[0].shape[0]), jnp.float32),
        ],
        compiler_params=pltpu.CompilerParams(vmem_limit_bytes=40 << 20),
        name="attend",
    )(spans, joint_query, *blocks, *state)


def merge_kernel(
    place_ref,
    arrived_ref,
    tokens_ref,
    tangents_ref,
    gain_ref,
    routing_ref,
    w_own,
    w_near_own,
    w_near_other,
    w_far_own,
    w_far_other,
    residual_ref,
    block_ref,
    held_ref,
    sum_ref,
):
    parts, each = arrived_ref.shape[0], arrived_ref.shape[1] - 8
    width = arrived_ref.shape[2] // 2
    groups = held_ref.shape[0] // 2
    row_groups = parts // groups
    moe_rows = held_ref.shape[1] // 2
    half_cols = held_ref.shape[2]

    def merge_group(group, carry):
        stats = [
            jnp.sum(
                arrived_ref[part * groups + group, each:].astype(jnp.float32),
                axis=0,
                keepdims=True,
            )
            for part in range(row_groups)
        ]
        level = jnp.concatenate([v[:, :width] for v in stats], axis=0)
        slopes = jnp.concatenate([v[:, width:] for v in stats], axis=0)
        raw = jnp.exp(level - jnp.max(level, axis=0, keepdims=True))
        mix = raw / jnp.sum(raw, axis=0, keepdims=True)
        slope = jnp.sum(mix * slopes, axis=0, keepdims=True)
        turned = jnp.concatenate([mix, mix * (slopes - slope)], axis=0).T
        output = d_output = None
        for part in range(row_groups):
            data = arrived_ref[part * groups + group, :each].astype(jnp.float32)
            share = turned[:, part : part + 1]
            tilt = turned[:, row_groups + part : row_groups + part + 1]
            term = share * data[:, :width]
            d_term = share * data[:, width:] + tilt * data[:, :width]
            output = term if output is None else output + term
            d_output = d_term if d_output is None else d_output + d_term
        per_half = half_cols // width
        for head in range(each // moe_rows):
            place = 2 * group + head // per_half
            cols = slice(head % per_half * width, (head % per_half + 1) * width)
            rows = slice(head * moe_rows, (head + 1) * moe_rows)
            held_ref[place, :moe_rows, cols] = output[rows].astype(jnp.bfloat16)
            held_ref[place, moe_rows:, cols] = d_output[rows].astype(jnp.bfloat16)
        return carry

    lax.fori_loop(0, groups, merge_group, 0)
    here, near_own, near_other, far, core = (place_ref[k] for k in range(5))
    order = [
        (2 * here, w_own, 0),
        (2 * here + 1, w_own, 1),
        (2 * near_own, w_near_own, 0),
        (2 * near_own + 1, w_near_own, 1),
        (2 * near_other, w_near_other, 0),
        (2 * near_other + 1, w_near_other, 1),
        (2 * far + core, w_far_own, 0),
        (2 * far + 1 - core, w_far_other, 0),
    ]
    step = sum_ref.shape[1] // 4

    def project(n, carry):
        cols = pl.ds(pl.multiple_of(n * step, step), step)
        total = None
        for place, piece, half in order:
            term = jnp.dot(
                held_ref[place],
                piece[half * half_cols : (half + 1) * half_cols, cols],
                preferred_element_type=jnp.float32,
            )
            total = term if total is None else total + term
        sum_ref[:, cols] = total
        return carry

    lax.fori_loop(0, sum_ref.shape[1] // step, project, 0)
    start = pl.multiple_of(here * moe_rows, moe_rows)
    own = pl.ds(start, moe_rows)
    residual = tokens_ref[own].astype(jnp.float32) + sum_ref[:moe_rows]
    d_residual = tangents_ref[own].astype(jnp.float32) + sum_ref[moe_rows:]
    residual_ref[:moe_rows] = residual
    residual_ref[moe_rows:] = d_residual
    gain = gain_ref[...]
    root = lax.rsqrt(jnp.mean(residual * residual, axis=1, keepdims=True) + epsilon)
    slope = jnp.mean(residual * d_residual, axis=1, keepdims=True) * root * root * root
    block_ref[:moe_rows] = (residual * root * gain).astype(jnp.bfloat16)
    d_normed = (d_residual * root - residual * slope) * gain
    block_ref[moe_rows : 2 * moe_rows] = d_normed.astype(jnp.bfloat16)
    block_ref[2 * moe_rows :] = routing_ref[...]


def merge(places, arrived, tokens, tangents, gain, routing, pieces, head_count, moe_rows):
    model_width = tokens.shape[1]
    half_cols = pieces[0].shape[0] // 2
    vmem = pl.BlockSpec(memory_space=pltpu.VMEM)
    return pl.pallas_call(
        merge_kernel,
        in_specs=[pl.BlockSpec(memory_space=pltpu.SMEM)] + [vmem] * (5 + len(pieces)),
        out_specs=(vmem, vmem),
        out_shape=(
            jax.ShapeDtypeStruct((2 * moe_rows, model_width), jnp.float32),
            jax.ShapeDtypeStruct((2 * moe_rows + 8, model_width), jnp.bfloat16),
        ),
        scratch_shapes=[
            pltpu.VMEM((2 * head_count, 2 * moe_rows, half_cols), jnp.bfloat16),
            pltpu.VMEM((2 * moe_rows, model_width), jnp.float32),
        ],
        compiler_params=pltpu.CompilerParams(vmem_limit_bytes=48 << 20),
        name="merge",
    )(places, arrived, tokens, tangents, gain, routing, *pieces)


def turned_pair(values, tangent, gain, cosine, sine):
    root = lax.rsqrt(jnp.mean(values * values, axis=1, keepdims=True) + epsilon)
    slope = jnp.mean(values * tangent, axis=1, keepdims=True) * root * root * root
    normed = values * root * gain
    d_normed = (tangent * root - values * slope) * gain
    half = values.shape[1] // 2
    return (
        normed * cosine + pltpu.roll(normed, half, 1) * sine,
        d_normed * cosine + pltpu.roll(d_normed, half, 1) * sine,
    )


def keys_kernel(
    head_ref,
    tokens_ref,
    tangents_ref,
    gain_ref,
    w_key_ref,
    w_value_ref,
    key_gain_ref,
    cosine_ref,
    sine_ref,
    stacked_ref,
    packed_ref,
):
    count = tokens_ref.shape[0]
    step = count // 4
    gain = gain_ref[...]

    def norm(number, carry):
        start = pl.multiple_of(number * step, step)
        part = pl.ds(start, step)
        values = tokens_ref[part].astype(jnp.float32)
        tangent = tangents_ref[part].astype(jnp.float32)
        root = lax.rsqrt(jnp.mean(values * values, axis=1, keepdims=True) + epsilon)
        slope = jnp.mean(values * tangent, axis=1, keepdims=True) * root * root * root
        stacked_ref[part] = (values * root * gain).astype(jnp.bfloat16)
        d_normed = (tangent * root - values * slope) * gain
        stacked_ref[pl.ds(count + start, step)] = d_normed.astype(jnp.bfloat16)
        return carry

    lax.fori_loop(0, count // step, norm, 0)
    stacked = stacked_ref[...]
    width = w_key_ref.shape[1]
    key = jnp.dot(stacked, w_key_ref[...], preferred_element_type=jnp.float32)
    value = jnp.dot(stacked, w_value_ref[...], preferred_element_type=jnp.float32)
    key, d_key = turned_pair(
        key[:count], key[count:], key_gain_ref[...], cosine_ref[...], sine_ref[...]
    )
    for number, part in enumerate((key, d_key, value[:count], value[count:])):
        packed_ref[:, number * width : (number + 1) * width] = part.astype(jnp.bfloat16)


def keys_of(head, tokens, tangents, gain, w_key, w_value, key_gain, cosine, sine):
    count, model_width = tokens.shape
    width = key_gain.shape[1]
    whole = lambda array: pl.BlockSpec(array.shape, lambda i, head: (0, 0))
    column = pl.BlockSpec((model_width, width), lambda i, head: (0, head[0]))
    return pl.pallas_call(
        keys_kernel,
        grid_spec=pltpu.PrefetchScalarGridSpec(
            num_scalar_prefetch=1,
            grid=(1,),
            in_specs=[
                whole(tokens),
                whole(tangents),
                whole(gain),
                column,
                column,
                whole(key_gain),
                whole(cosine),
                whole(sine),
            ],
            out_specs=(
                pl.BlockSpec((2 * count, model_width), lambda i, head: (0, 0)),
                pl.BlockSpec((count, 4 * width), lambda i, head: (0, 0)),
            ),
        ),
        out_shape=(
            jax.ShapeDtypeStruct((2 * count, model_width), jnp.bfloat16),
            jax.ShapeDtypeStruct((count, 4 * width), jnp.bfloat16),
        ),
        name="keys_of",
    )(head, tokens, tangents, gain, w_key, w_value, key_gain, cosine, sine)


def queries_kernel(
    moe_rows,
    core_ref,
    stacked_ref,
    weight_ref,
    gain_ref,
    cosine_ref,
    sine_ref,
    w_out_ref,
    out_ref,
    far_ref,
    sem,
):
    half_rows = far_ref.shape[0]
    start = pl.multiple_of(core_ref[0] * half_rows, half_rows)
    far_copy = pltpu.make_async_copy(w_out_ref.at[pl.ds(start, half_rows)], far_ref, sem)
    far_copy.start()
    count = stacked_ref.shape[0] // 2
    width = gain_ref.shape[1]
    heads = weight_ref.shape[1] // width
    query_all = jnp.dot(stacked_ref[...], weight_ref[...], preferred_element_type=jnp.float32)
    for head in range(heads):
        column = query_all[:, head * width : (head + 1) * width]
        query, d_query = turned_pair(
            column[:count], column[count:], gain_ref[...], cosine_ref[...], sine_ref[...]
        )
        joint = jnp.concatenate([d_query, query], axis=1).astype(jnp.bfloat16)
        for receiver in range(count // moe_rows):
            start = (receiver * heads + head) * moe_rows
            for copy in range(out_ref.shape[0]):
                out_ref[copy, start : start + moe_rows] = joint[
                    receiver * moe_rows : (receiver + 1) * moe_rows
                ]
    far_copy.wait()


def queries_of(core, stacked, weight, gain, cosine, sine, w_out, copies, moe_rows):
    width = gain.shape[1]
    rows = stacked.shape[0] // 2 * (weight.shape[1] // width)
    vmem, hbm = (pl.BlockSpec(memory_space=space) for space in (pltpu.VMEM, pl.ANY))
    return pl.pallas_call(
        functools.partial(queries_kernel, moe_rows),
        in_specs=[pl.BlockSpec(memory_space=pltpu.SMEM)] + [vmem] * 5 + [hbm],
        out_specs=(vmem, vmem),
        out_shape=(
            jax.ShapeDtypeStruct((copies, rows, 2 * width), jnp.bfloat16),
            jax.ShapeDtypeStruct((w_out.shape[0] // 2, w_out.shape[1]), w_out.dtype),
        ),
        scratch_shapes=[pltpu.SemaphoreType.DMA],
        name="queries_of",
    )(core, stacked, weight, gain, cosine, sine, w_out)


def table_of(refs, rows, number):
    lanes = slice(128 * number, 128 * (number + 1))
    tiles = [ref[rows : rows + 8, lanes].astype(jnp.float32) for ref in refs]
    pairs = [tiles[k] + pltpu.roll(tiles[k + 1], 64, 1) for k in range(0, len(tiles), 2)]
    return jnp.concatenate(pairs, axis=1)


def placing(first_expert, routes, experts, capacity, slot_rows, moe_rows):
    count, cols = routes.shape
    expert = first_expert + lax.broadcasted_iota(jnp.int32, (experts, cols), 0)
    named = [
        jnp.broadcast_to(routes[k : k + 1], (experts, cols)) == expert.astype(jnp.float32)
        for k in range(count)
    ]
    hit = jnp.zeros((experts, cols), jnp.float32)
    for each in named:
        hit = hit + jnp.where(each, 1.0, 0.0)
    source = lax.broadcasted_iota(jnp.int32, (cols, cols), 0)
    target = lax.broadcasted_iota(jnp.int32, (cols, cols), 1)
    before = (source // moe_rows == target // moe_rows) & (source < target)
    rank = jnp.dot(
        hit.astype(jnp.bfloat16),
        jnp.where(before, 1.0, 0.0).astype(jnp.bfloat16),
        preferred_element_type=jnp.float32,
    )
    block = (lax.broadcasted_iota(jnp.int32, (experts, cols), 1) // (2 * moe_rows)).astype(jnp.float32)
    slot = jnp.where(hit > 0.0, block * capacity + rank, -1.0)
    row = lax.broadcasted_iota(jnp.int32, (slot_rows, cols), 0)
    half = lax.broadcasted_iota(jnp.int32, (slot_rows, cols), 1) // moe_rows % 2
    is_tangent = jnp.where((row // 8 == 1) | (row >= 20), 1, 0)
    row_slot = jnp.where(row < 8, row, jnp.where(row < 20, row - 8, row - 12))
    code = jnp.where(half == is_tangent, row_slot, -2).astype(jnp.float32)
    chosen = [
        jnp.broadcast_to(slot[j : j + 1], (slot_rows, cols)) == code for j in range(experts)
    ]
    return chosen, named


def pack_kernel(experts, capacity, slot_rows, moe_rows, first_ref, *refs):
    blocks, out_ref, table_ref = refs[:-2], refs[-2], refs[-1]
    rows = 2 * moe_rows
    routes = table_of(blocks, rows, 0)
    table_ref[:8] = routes
    table_ref[8:] = table_of(blocks, rows, 1)
    chosen, _ = placing(first_ref[0], routes, experts, capacity, slot_rows, moe_rows)
    pick = jnp.concatenate([jnp.where(c, 1.0, 0.0) for c in chosen], axis=0).astype(jnp.bfloat16)
    source = jnp.concatenate([block[:rows] for block in blocks], axis=0)
    out_ref[...] = jnp.dot(pick, source, preferred_element_type=jnp.float32).astype(jnp.bfloat16)


def mix_kernel(
    experts, capacity, slot_rows, moe_rows, first_ref, returned_ref, table_ref, out_ref
):
    routes = table_ref[:8]
    chosen, named = placing(first_ref[0], routes, experts, capacity, slot_rows, moe_rows)
    shares = table_ref[8:]
    share = jnp.zeros(named[0].shape, jnp.float32)
    for k, each in enumerate(named):
        share = share + jnp.where(each, jnp.broadcast_to(shares[k : k + 1], each.shape), 0.0)
    held = jnp.concatenate(
        [
            jnp.where(c, jnp.broadcast_to(share[j : j + 1], c.shape), 0.0)
            for j, c in enumerate(chosen)
        ],
        axis=0,
    )
    out_ref[...] = jnp.dot(
        held.T.astype(jnp.bfloat16), returned_ref[...], preferred_element_type=jnp.float32
    )


def pack(first, blocks, experts, capacity, slot_rows, moe_rows):
    vmem = pl.BlockSpec(memory_space=pltpu.VMEM)
    return pl.pallas_call(
        functools.partial(pack_kernel, experts, capacity, slot_rows, moe_rows),
        in_specs=[pl.BlockSpec(memory_space=pltpu.SMEM)] + [vmem] * len(blocks),
        out_specs=(vmem, vmem),
        out_shape=(
            jax.ShapeDtypeStruct((experts * slot_rows, blocks[0].shape[1]), jnp.bfloat16),
            jax.ShapeDtypeStruct((16, 2 * moe_rows * len(blocks)), jnp.float32),
        ),
        compiler_params=pltpu.CompilerParams(vmem_limit_bytes=40 << 20),
        name="pack",
    )(first, *blocks)


def mixed(first, returned, table, experts, capacity, slot_rows, moe_rows):
    vmem = pl.BlockSpec(memory_space=pltpu.VMEM)
    return pl.pallas_call(
        functools.partial(mix_kernel, experts, capacity, slot_rows, moe_rows),
        in_specs=[pl.BlockSpec(memory_space=pltpu.SMEM), vmem, vmem],
        out_specs=vmem,
        out_shape=jax.ShapeDtypeStruct((table.shape[1], returned.shape[1]), jnp.float32),
        compiler_params=pltpu.CompilerParams(vmem_limit_bytes=40 << 20),
        name="mixed",
    )(first, returned, table)


def expert_kernel(rows_ref, *refs):
    sources, out_ref, held, (sum_ref, hidden_ref, sems) = refs[:6], refs[6], refs[7:10], refs[10:]
    count, depth = rows_ref.shape
    units = sources[0].shape[1]
    step = depth // 4

    def copy(number, k):
        part = pl.ds(pl.multiple_of(k * step, step), step)
        side = number % 2 * units
        return pltpu.make_async_copy(
            sources[number].at[part],
            held[number // 2].at[part, side : side + units],
            sems.at[number, k],
        )

    for numbers in (range(4), range(4, 6)):
        for k in range(depth // step):
            for number in numbers:
                copy(number, k).start()
    sum_ref[...] = jnp.zeros_like(sum_ref)

    def contract(k, carry):
        part = pl.ds(pl.multiple_of(k * step, step), step)
        for number in range(2):
            copy(2 * number, k).wait()
            copy(2 * number + 1, k).wait()
            sum_ref[number] += jnp.dot(
                rows_ref[:, part], held[number][part], preferred_element_type=jnp.float32
            )
        return carry

    lax.fori_loop(0, depth // step, contract, 0)

    def pair(gate_value, gate_tangent, up_value, up_tangent):
        sigmoid_gate = jax.nn.sigmoid(gate_value)
        active = gate_value * sigmoid_gate
        active_slope = sigmoid_gate * (1.0 + gate_value * (1.0 - sigmoid_gate))
        primal = active * up_value
        return primal, active_slope * gate_tangent * up_value + active * up_tangent

    groups = 48

    def activate(number, carry):
        part = pl.ds(pl.multiple_of(number * groups, groups), groups)
        gate = sum_ref[0, part].reshape(groups // 24, 3, 8, 2 * units)
        up = sum_ref[1, part].reshape(groups // 24, 3, 8, 2 * units)
        primal, tangent = pair(gate[:, 0], gate[:, 1], up[:, 0], up[:, 1])
        mixed_gate, mixed_up = gate[:, 2], up[:, 2]
        turned_gate = pltpu.roll(mixed_gate, 4, 1)
        turned_up = pltpu.roll(mixed_up, 4, 1)
        first = lax.broadcasted_iota(jnp.int32, mixed_gate.shape, 1) < 4
        last_primal, last_tangent = pair(
            jnp.where(first, mixed_gate, turned_gate),
            jnp.where(first, turned_gate, mixed_gate),
            jnp.where(first, mixed_up, turned_up),
            jnp.where(first, turned_up, mixed_up),
        )
        last = jnp.where(first, last_primal, last_tangent)
        hidden = jnp.stack([primal, tangent, last], 1).reshape(groups, 2 * units)
        hidden_ref[part] = hidden.astype(jnp.bfloat16)
        return carry

    lax.fori_loop(0, count // groups, activate, 0)

    def produce(n, carry):
        part = pl.ds(pl.multiple_of(n * step, step), step)
        copy(4, n).wait()
        copy(5, n).wait()
        across = (((1,), (1,)), ((), ()))
        result = lax.dot_general(
            hidden_ref[...], held[2][part], across, preferred_element_type=jnp.float32
        )
        out_ref[:, part] = result.astype(out_ref.dtype)
        return carry

    lax.fori_loop(0, depth // step, produce, 0)


def expert_rows(rows, weights):
    gate, up, down, gate_other, up_other, down_other = weights
    count, (depth, units) = rows.shape[0], gate.shape
    vmem, hbm = (pl.BlockSpec(memory_space=space) for space in (pltpu.VMEM, pl.ANY))
    return pl.pallas_call(
        expert_kernel,
        in_specs=[vmem] + [hbm] * 6,
        out_specs=vmem,
        out_shape=jax.ShapeDtypeStruct(rows.shape, jnp.bfloat16),
        scratch_shapes=[
            *[pltpu.VMEM((depth, 2 * units), jnp.bfloat16)] * 3,
            pltpu.VMEM((2, count, 2 * units), jnp.float32),
            pltpu.VMEM((count, 2 * units), jnp.bfloat16),
            pltpu.SemaphoreType.DMA((6, 4)),
        ],
        compiler_params=pltpu.CompilerParams(vmem_limit_bytes=56 << 20),
        name="expert_rows",
    )(rows, gate, gate_other, up, up_other, down, down_other)


def layer(
    tokens,
    tangents,
    attn_gain,
    ffn_gain,
    w_query,
    w_key,
    w_value,
    w_out,
    query_gain,
    key_gain,
    expert_gate,
    expert_up,
    expert_down,
    routes,
    route_weights,
):
    tok_count, model_width = tokens.shape
    head_width = query_gain.shape[0]
    heads_here = w_query.shape[1] // head_width
    head_count = lax.axis_size("head")
    moe_rows = tok_count // head_count
    core = lax.axis_index("dp")
    other_core = [(0, 1), (1, 0)]

    own_halves = [expert_gate[0], expert_up[0], expert_down[0]]
    expert_halves = own_halves + [lax.ppermute(half, "dp", other_core) for half in own_halves]

    plane = lax.axis_index("seq_0")
    row_in_plane = lax.axis_index("seq_1")
    plane_rows = lax.axis_size("seq_1") * tok_count
    plane_count = lax.axis_size("seq_0")
    first_pos = plane * plane_rows + row_in_plane * tok_count
    positions = first_pos + jnp.arange(tok_count, dtype=jnp.int32)
    cosine, sine = turns_of(positions, head_width)
    kv_count = w_key.shape[1] // head_width
    devices_per_kv = lax.axis_size("head") // kv_count
    kv_head = (lax.axis_index("head") // devices_per_kv).astype(jnp.int32)[None]
    stacked, packed = keys_of(
        kv_head,
        tokens,
        tangents,
        attn_gain[None],
        w_key,
        w_value,
        key_gain[None],
        cosine,
        sine,
    )
    blocks = ring_blocks(packed, "seq_0")

    top_count = routes.shape[1]
    tables = jnp.stack([routes.astype(jnp.bfloat16), route_weights.astype(jnp.bfloat16)], 0)
    tables = jnp.transpose(tables, (2, 0, 1))
    tables = jnp.concatenate([tables, tables, jnp.zeros_like(tables), jnp.zeros_like(tables)], 2)
    tables = tables.reshape(top_count, 2 * 4 * moe_rows)
    tables = jnp.pad(tables, ((0, 0), (0, model_width - tables.shape[1])))

    row_groups = lax.axis_size("seq_1")
    copies, far_rows = queries_of(
        core.astype(jnp.int32)[None],
        stacked,
        w_query,
        query_gain[None],
        cosine,
        sine,
        w_out,
        row_groups,
        moe_rows,
    )

    ring = range(head_count)
    sides = [(i, (i + 1) % head_count) for i in ring]
    sides += [(head_count + i, head_count + (i - 1) % head_count) for i in ring]
    near_own = lax.ppermute(w_out, ("dp", "head"), sides)
    far_own = shifted(far_rows, "head", head_count // 2)
    near_other = lax.ppermute(near_own, "dp", other_core)
    far_other = lax.ppermute(far_own, "dp", other_core)
    out_pieces = (w_out, near_own, near_other, far_own, far_other)
    own_rows = copies.shape[1]
    joint_query = lax.all_to_all(copies, "seq_1", 0, 0, tiled=True)
    joint_query = joint_query.reshape(row_groups * own_rows, 2 * head_width)
    receivers = row_groups * head_count
    rows_each = heads_here * moe_rows
    state = ()
    for order in ((0, -1, 1, -2, 2, -3), (3, -4)):
        spans = [
            (lax.rem(plane + k + plane_count, plane_count) - plane) * plane_rows
            + row_in_plane * tok_count
            for k in order
        ]
        state = attend(
            jnp.stack(spans).astype(jnp.int32),
            joint_query,
            [blocks[k] for k in order],
            state,
            receivers,
            rows_each,
            own_rows,
            moe_rows,
        )
    sent = state
    arrived = lax.all_to_all(sent, ("seq_1", "head"), 0, 0, tiled=True)
    here = lax.axis_index("head")
    side = 1 - 2 * core
    places = jnp.stack(
        [
            here,
            lax.rem(here - side + head_count, head_count),
            lax.rem(here + side + head_count, head_count),
            lax.rem(here + head_count // 2, head_count),
            core,
        ]
    ).astype(jnp.int32)
    residual, moe_in = merge(
        places,
        arrived,
        tokens,
        tangents,
        ffn_gain[None],
        tables,
        out_pieces,
        head_count,
        moe_rows,
    )
    gathered = ring_blocks(moe_in, "seq_0")

    plane_experts = row_groups * head_count
    capacity = 3
    first_expert = (plane * plane_experts).astype(jnp.int32)[None]
    near, far = [0, 1, -1, 2], [-2, 3, -3, -4]
    block_rows = 2 * moe_rows
    slot_rows = 2 * capacity * len(near)
    layout = (plane_experts, capacity, slot_rows, moe_rows)

    results, lists = [], {}
    for name, group in (("near", near), ("far", far)):
        outgoing, lists[name] = pack(first_expert, [gathered[k] for k in group], *layout)
        outgoing = outgoing.reshape(plane_experts, slot_rows, model_width)
        received = lax.all_to_all(outgoing, ("seq_1", "head"), 0, 0, tiled=True)
        results.append(
            expert_rows(received.reshape(plane_experts * slot_rows, model_width), expert_halves)
        )
    share_of = {}
    for name, group, result in (("far", far, results[1]), ("near", near, results[0])):
        result = result.reshape(plane_experts, slot_rows, model_width)
        returned = lax.all_to_all(result, ("seq_1", "head"), 0, 0, tiled=True)
        returned = returned.reshape(plane_experts * slot_rows, model_width)
        sums = mixed(first_expert, returned, lists[name], *layout)
        sums = sums.reshape(len(group), block_rows, model_width)
        for number, k in enumerate(group):
            share_of[k] = sums[number]
    low = jnp.bfloat16
    up = shifted(share_of[-4].astype(low), "seq_0", 1)
    down = shifted(share_of[-3].astype(low), "seq_0", -1)
    for k in (3, 2, 1):
        up = shifted((share_of[k] + up.astype(jnp.float32)).astype(low), "seq_0", 1)
    for k in (-2, -1):
        down = shifted((share_of[k] + down.astype(jnp.float32)).astype(low), "seq_0", -1)
    moe_sum = share_of[0] + up.astype(jnp.float32) + down.astype(jnp.float32)
    result = (residual + moe_sum).astype(jnp.bfloat16)
    layer_out, layer_tangent = result[:moe_rows], result[moe_rows:]
    return (layer_out, layer_tangent)


def solution(mesh):
    split = Mesh(
        mesh.devices.reshape(mesh.shape["dp"], 8, 4, mesh.shape["head"]),
        ("dp", "seq_0", "seq_1", "head"),
    )
    return jax.shard_map(
        layer,
        mesh=split,
        in_specs=(
            P(DP_SEQ, None),
            P(DP_SEQ, None),
            P(),
            P(),
            P(None, "head"),
            P(),
            P(),
            P("head", None),
            P(),
            P(),
            P(SEQ_HEAD, None, "dp"),
            P(SEQ_HEAD, None, "dp"),
            P(SEQ_HEAD, None, "dp"),
            P(DP_SEQ_HEAD, None),
            P(DP_SEQ_HEAD, None),
        ),
        out_specs=(P(DP_SEQ_HEAD, None), P(DP_SEQ_HEAD, None)),
        check_vma=False,
    )
```

```python
import functools

import jax
import jax.numpy as jnp
from jax import lax
from jax.experimental import pallas as pl
from jax.experimental.pallas import tpu as pltpu
from jax.sharding import Mesh
from jax.sharding import PartitionSpec as P


SEQ_HEAD = ("seq_0", "seq_1", "head")
DP_SEQ = ("dp", "seq_0", "seq_1")
DP_SEQ_HEAD = ("dp", "seq_0", "seq_1", "head")


epsilon = 1e-06
rope_base = 1000000.0
masked_score = -1e30


def turns_of(positions, head_width):
    half_width = head_width // 2
    exponent = jnp.arange(half_width, dtype=jnp.float32) * (2.0 / head_width)
    frequency = jnp.power(jnp.float32(rope_base), -exponent)
    angle = positions.astype(jnp.float32)[:, None] * frequency[None, :]
    cosine, sine = jnp.cos(angle), jnp.sin(angle)
    return jnp.concatenate([cosine, cosine], 1), jnp.concatenate([-sine, sine], 1)


def shifted(array, axis, offset):
    size = lax.axis_size(axis)
    return lax.ppermute(array, axis, [(i, (i + offset) % size) for i in range(size)])


def ring_blocks(block, axis):
    size = lax.axis_size(axis)
    found = {0: block}
    up = down = block
    for step in range(1, size // 2 + 1):
        up = shifted(up, axis, 1)
        found[-step] = up
        if 2 * step < size:
            down = shifted(down, axis, -1)
            found[step] = down
    return found


def three_parts(values):
    high = values.astype(jnp.bfloat16).astype(jnp.float32)
    rest = values - high
    middle = rest.astype(jnp.bfloat16).astype(jnp.float32)
    low = rest - middle
    row = lax.broadcasted_iota(jnp.int32, values.shape, 0)
    return jnp.where(row == 0, high, jnp.where(row == 1, middle, jnp.where(row == 2, low, 0.0)))


def attend_kernel(scale, group_rows, moe_rows, first, count, span_ref, joint_ref, *refs):
    blocks, refs = refs[:count], refs[count:]
    if first:
        sums_ref, figures_ref, held_ref, score_ref = refs
    elif first is None:
        out_ref, held_ref, score_ref = refs
    else:
        old_sums_ref, old_figures_ref, out_ref, held_ref, score_ref = refs
    rows, width = joint_ref.shape[0], joint_ref.shape[1] // 2
    keys = blocks[0].shape[0]
    chunk = held_ref.shape[1]
    each_chunk = chunk // keys

    @pl.when(pl.program_id(0) == 0)
    def _():
        for number, block in enumerate(blocks):
            start = number % each_chunk * keys
            held_ref[number // each_chunk, start : start + keys] = block[...]

    joint = joint_ref[...]
    query = joint[:, width:]
    contract = (((1,), (1,)), ((), ()))
    shape = (rows, chunk)
    row = pl.program_id(0) * rows + lax.broadcasted_iota(jnp.int32, shape, 0)
    own = row // group_rows * keys + row % group_rows // keys * moe_rows + row % moe_rows
    lane = lax.broadcasted_iota(jnp.int32, shape, 1)
    own = own - lane % keys
    top = jnp.full(shape, masked_score, jnp.float32)
    for number in range(held_ref.shape[0]):
        score = lax.dot_general(
            query, held_ref[number, :, :width], contract, preferred_element_type=jnp.float32
        )
        lead = number * each_chunk
        span = jnp.where(lane < keys, span_ref[lead], span_ref[lead + 1])
        score = jnp.where(span <= own, score * scale, masked_score)
        score_ref[number] = score
        top = jnp.maximum(top, score)
    top = jnp.max(top, axis=1, keepdims=True)
    if first is False:
        old_top = old_figures_ref[:, :1]
        top = jnp.maximum(top, old_top)
    total = jnp.zeros(shape, jnp.float32)
    slope = jnp.zeros(shape, jnp.float32)
    sums = jnp.zeros((rows, 2 * width), jnp.float32)
    tilted = jnp.zeros((rows, width), jnp.float32)
    for number in range(held_ref.shape[0]):
        score = score_ref[number]
        d_score = lax.dot_general(
            joint, held_ref[number, :, : 2 * width], contract, preferred_element_type=jnp.float32
        ) * scale
        weight = jnp.where(score > 0.5 * masked_score, jnp.exp(score - top), 0.0)
        tilt = weight * d_score
        total = total + weight
        slope = slope + tilt
        sums = sums + jnp.dot(
            weight.astype(jnp.bfloat16),
            held_ref[number, :, 2 * width :],
            preferred_element_type=jnp.float32,
        )
        tilted = tilted + jnp.dot(
            tilt.astype(jnp.bfloat16),
            held_ref[number, :, 2 * width : 3 * width],
            preferred_element_type=jnp.float32,
        )
    total = jnp.sum(total, axis=1, keepdims=True)
    slope = jnp.sum(slope, axis=1, keepdims=True)
    lane = lax.broadcasted_iota(jnp.int32, (rows, width), 1)
    if first:
        sums_ref[:, :width] = sums[:, :width]
        sums_ref[:, width:] = sums[:, width:] + tilted
        figures_ref[...] = jnp.where(lane == 0, top, jnp.where(lane == 1, total, slope))
        return
    primal = sums[:, :width]
    tangent = sums[:, width:] + tilted
    if first is False:
        fade = jnp.exp(old_top - top)
        total = total + fade * old_figures_ref[:, 1:2]
        slope = slope + fade * old_figures_ref[:, 2:3]
        primal = primal + fade * old_sums_ref[:, :width]
        tangent = tangent + fade * old_sums_ref[:, width:]
    some = total > 0.0
    share = jnp.where(some, 1.0 / jnp.where(some, total, 1.0), 0.0)
    output = primal * share
    mean_slope = slope * share
    d_output = tangent * share - mean_slope * output
    level = jnp.where(some, top + jnp.log(jnp.where(some, total, 1.0)), masked_score)
    both = jnp.concatenate([output, d_output], axis=1).astype(jnp.bfloat16)
    figures = jnp.where(lane < width // 2, level, mean_slope)
    each = out_ref.shape[1] - 8
    for number in range(out_ref.shape[0]):
        out_ref[number, :each] = both[number * each : (number + 1) * each]
        turned = figures[number * each : (number + 1) * each].T
        stats = jnp.concatenate(
            [three_parts(turned[:8]), three_parts(turned[width // 2 : width // 2 + 8])], axis=1
        )
        out_ref[number, each:] = stats.astype(jnp.bfloat16)


def attend(spans, joint_query, blocks, state, receivers, rows_each, group_rows, moe_rows):
    width = joint_query.shape[1]
    count = 4 if state else 2
    rows = count * rows_each
    whole = pl.BlockSpec(blocks[0].shape, lambda i: (0, 0))
    row_block = pl.BlockSpec((rows, width), lambda i: (i, 0))
    half_block = pl.BlockSpec((rows, width // 2), lambda i: (i, 0))
    first = None if state is None else not state
    if first:
        out_specs = (row_block, half_block)
        out_shape = (
            jax.ShapeDtypeStruct((joint_query.shape[0], width), jnp.float32),
            jax.ShapeDtypeStruct((joint_query.shape[0], width // 2), jnp.float32),
        )
    else:
        out_specs = pl.BlockSpec((count, rows_each + 8, width), lambda i: (i, 0, 0))
        out_shape = jax.ShapeDtypeStruct((receivers, rows_each + 8, width), jnp.bfloat16)
    scale = (width // 2) ** (-0.5)
    return pl.pallas_call(
        functools.partial(attend_kernel, scale, group_rows, moe_rows, first, len(blocks)),
        grid=(receivers // count,),
        in_specs=[
            pl.BlockSpec(memory_space=pltpu.SMEM),
            row_block,
            *[whole] * len(blocks),
            *([row_block, half_block] if state else []),
        ],
        out_specs=out_specs,
        out_shape=out_shape,
        scratch_shapes=[
            pltpu.VMEM((len(blocks) // 2, 2 * blocks[0].shape[0], blocks[0].shape[1]), jnp.bfloat16),
            pltpu.VMEM((len(blocks) // 2, rows, 2 * blocks[0].shape[0]), jnp.float32),
        ],
        compiler_params=pltpu.CompilerParams(vmem_limit_bytes=40 << 20),
        name="attend",
    )(spans, joint_query, *blocks, *(state or ()))


def merge_kernel(
    place_ref,
    arrived_ref,
    tokens_ref,
    tangents_ref,
    gain_ref,
    routing_ref,
    w_own,
    w_near_own,
    w_near_other,
    w_far_own,
    w_far_other,
    residual_ref,
    block_ref,
    held_ref,
    sum_ref,
):
    parts, each = arrived_ref.shape[0], arrived_ref.shape[1] - 8
    width = arrived_ref.shape[2] // 2
    groups = held_ref.shape[0] // 2
    row_groups = parts // groups
    moe_rows = held_ref.shape[1] // 2
    half_cols = held_ref.shape[2]

    def merge_group(group, carry):
        stats = [
            jnp.sum(
                arrived_ref[part * groups + group, each:].astype(jnp.float32),
                axis=0,
                keepdims=True,
            )
            for part in range(row_groups)
        ]
        level = jnp.concatenate([v[:, :width] for v in stats], axis=0)
        slopes = jnp.concatenate([v[:, width:] for v in stats], axis=0)
        raw = jnp.exp(level - jnp.max(level, axis=0, keepdims=True))
        mix = raw / jnp.sum(raw, axis=0, keepdims=True)
        slope = jnp.sum(mix * slopes, axis=0, keepdims=True)
        turned = jnp.concatenate([mix, mix * (slopes - slope)], axis=0).T
        output = d_output = None
        for part in range(row_groups):
            data = arrived_ref[part * groups + group, :each].astype(jnp.float32)
            share = turned[:, part : part + 1]
            tilt = turned[:, row_groups + part : row_groups + part + 1]
            term = share * data[:, :width]
            d_term = share * data[:, width:] + tilt * data[:, :width]
            output = term if output is None else output + term
            d_output = d_term if d_output is None else d_output + d_term
        per_half = half_cols // width
        for head in range(each // moe_rows):
            place = 2 * group + head // per_half
            cols = slice(head % per_half * width, (head % per_half + 1) * width)
            rows = slice(head * moe_rows, (head + 1) * moe_rows)
            held_ref[place, :moe_rows, cols] = output[rows].astype(jnp.bfloat16)
            held_ref[place, moe_rows:, cols] = d_output[rows].astype(jnp.bfloat16)
        return carry

    lax.fori_loop(0, groups, merge_group, 0)
    here, near_own, near_other, far, core = (place_ref[k] for k in range(5))
    order = [
        (2 * here, w_own, 0),
        (2 * here + 1, w_own, 1),
        (2 * near_own, w_near_own, 0),
        (2 * near_own + 1, w_near_own, 1),
        (2 * near_other, w_near_other, 0),
        (2 * near_other + 1, w_near_other, 1),
        (2 * far + core, w_far_own, 0),
        (2 * far + 1 - core, w_far_other, 0),
    ]
    step = sum_ref.shape[1] // 4

    def project(n, carry):
        cols = pl.ds(pl.multiple_of(n * step, step), step)
        total = None
        for place, piece, half in order:
            term = jnp.dot(
                held_ref[place],
                piece[half * half_cols : (half + 1) * half_cols, cols],
                preferred_element_type=jnp.float32,
            )
            total = term if total is None else total + term
        sum_ref[:, cols] = total
        return carry

    lax.fori_loop(0, sum_ref.shape[1] // step, project, 0)
    start = pl.multiple_of(here * moe_rows, moe_rows)
    own = pl.ds(start, moe_rows)
    residual = tokens_ref[own].astype(jnp.float32) + sum_ref[:moe_rows]
    d_residual = tangents_ref[own].astype(jnp.float32) + sum_ref[moe_rows:]
    residual_ref[:moe_rows] = residual
    residual_ref[moe_rows:] = d_residual
    gain = gain_ref[...]
    root = lax.rsqrt(jnp.mean(residual * residual, axis=1, keepdims=True) + epsilon)
    slope = jnp.mean(residual * d_residual, axis=1, keepdims=True) * root * root * root
    block_ref[:moe_rows] = (residual * root * gain).astype(jnp.bfloat16)
    d_normed = (d_residual * root - residual * slope) * gain
    block_ref[moe_rows : 2 * moe_rows] = d_normed.astype(jnp.bfloat16)
    block_ref[2 * moe_rows :] = routing_ref[...]


def merge(places, arrived, tokens, tangents, gain, routing, pieces, head_count, moe_rows):
    model_width = tokens.shape[1]
    half_cols = pieces[0].shape[0] // 2
    vmem = pl.BlockSpec(memory_space=pltpu.VMEM)
    return pl.pallas_call(
        merge_kernel,
        in_specs=[pl.BlockSpec(memory_space=pltpu.SMEM)] + [vmem] * (5 + len(pieces)),
        out_specs=(vmem, vmem),
        out_shape=(
            jax.ShapeDtypeStruct((2 * moe_rows, model_width), jnp.float32),
            jax.ShapeDtypeStruct((2 * moe_rows + 8, model_width), jnp.bfloat16),
        ),
        scratch_shapes=[
            pltpu.VMEM((2 * head_count, 2 * moe_rows, half_cols), jnp.bfloat16),
            pltpu.VMEM((2 * moe_rows, model_width), jnp.float32),
        ],
        compiler_params=pltpu.CompilerParams(vmem_limit_bytes=48 << 20),
        name="merge",
    )(places, arrived, tokens, tangents, gain, routing, *pieces)


def turned_pair(values, tangent, gain, cosine, sine):
    root = lax.rsqrt(jnp.mean(values * values, axis=1, keepdims=True) + epsilon)
    slope = jnp.mean(values * tangent, axis=1, keepdims=True) * root * root * root
    normed = values * root * gain
    d_normed = (tangent * root - values * slope) * gain
    half = values.shape[1] // 2
    return (
        normed * cosine + pltpu.roll(normed, half, 1) * sine,
        d_normed * cosine + pltpu.roll(d_normed, half, 1) * sine,
    )


def keys_kernel(
    head_ref,
    tokens_ref,
    tangents_ref,
    gain_ref,
    w_key_ref,
    w_value_ref,
    key_gain_ref,
    cosine_ref,
    sine_ref,
    stacked_ref,
    packed_ref,
):
    count = tokens_ref.shape[0]
    step = count // 4
    gain = gain_ref[...]

    def norm(number, carry):
        start = pl.multiple_of(number * step, step)
        part = pl.ds(start, step)
        values = tokens_ref[part].astype(jnp.float32)
        tangent = tangents_ref[part].astype(jnp.float32)
        root = lax.rsqrt(jnp.mean(values * values, axis=1, keepdims=True) + epsilon)
        slope = jnp.mean(values * tangent, axis=1, keepdims=True) * root * root * root
        stacked_ref[part] = (values * root * gain).astype(jnp.bfloat16)
        d_normed = (tangent * root - values * slope) * gain
        stacked_ref[pl.ds(count + start, step)] = d_normed.astype(jnp.bfloat16)
        return carry

    lax.fori_loop(0, count // step, norm, 0)
    stacked = stacked_ref[...]
    width = w_key_ref.shape[1]
    key = jnp.dot(stacked, w_key_ref[...], preferred_element_type=jnp.float32)
    value = jnp.dot(stacked, w_value_ref[...], preferred_element_type=jnp.float32)
    key, d_key = turned_pair(
        key[:count], key[count:], key_gain_ref[...], cosine_ref[...], sine_ref[...]
    )
    for number, part in enumerate((key, d_key, value[:count], value[count:])):
        packed_ref[:, number * width : (number + 1) * width] = part.astype(jnp.bfloat16)


def keys_of(head, tokens, tangents, gain, w_key, w_value, key_gain, cosine, sine):
    count, model_width = tokens.shape
    width = key_gain.shape[1]
    whole = lambda array: pl.BlockSpec(array.shape, lambda i, head: (0, 0))
    column = pl.BlockSpec((model_width, width), lambda i, head: (0, head[0]))
    return pl.pallas_call(
        keys_kernel,
        grid_spec=pltpu.PrefetchScalarGridSpec(
            num_scalar_prefetch=1,
            grid=(1,),
            in_specs=[
                whole(tokens),
                whole(tangents),
                whole(gain),
                column,
                column,
                whole(key_gain),
                whole(cosine),
                whole(sine),
            ],
            out_specs=(
                pl.BlockSpec((2 * count, model_width), lambda i, head: (0, 0)),
                pl.BlockSpec((count, 4 * width), lambda i, head: (0, 0)),
            ),
        ),
        out_shape=(
            jax.ShapeDtypeStruct((2 * count, model_width), jnp.bfloat16),
            jax.ShapeDtypeStruct((count, 4 * width), jnp.bfloat16),
        ),
        name="keys_of",
    )(head, tokens, tangents, gain, w_key, w_value, key_gain, cosine, sine)


def queries_kernel(
    moe_rows,
    core_ref,
    stacked_ref,
    weight_ref,
    gain_ref,
    cosine_ref,
    sine_ref,
    w_out_ref,
    out_ref,
    far_ref,
    sem,
):
    half_rows = far_ref.shape[0]
    start = pl.multiple_of(core_ref[0] * half_rows, half_rows)
    far_copy = pltpu.make_async_copy(w_out_ref.at[pl.ds(start, half_rows)], far_ref, sem)
    far_copy.start()
    count = stacked_ref.shape[0] // 2
    width = gain_ref.shape[1]
    heads = weight_ref.shape[1] // width
    query_all = jnp.dot(stacked_ref[...], weight_ref[...], preferred_element_type=jnp.float32)
    for head in range(heads):
        column = query_all[:, head * width : (head + 1) * width]
        query, d_query = turned_pair(
            column[:count], column[count:], gain_ref[...], cosine_ref[...], sine_ref[...]
        )
        joint = jnp.concatenate([d_query, query], axis=1).astype(jnp.bfloat16)
        for receiver in range(count // moe_rows):
            start = (receiver * heads + head) * moe_rows
            for copy in range(out_ref.shape[0]):
                out_ref[copy, start : start + moe_rows] = joint[
                    receiver * moe_rows : (receiver + 1) * moe_rows
                ]
    far_copy.wait()


def queries_of(core, stacked, weight, gain, cosine, sine, w_out, copies, moe_rows):
    width = gain.shape[1]
    rows = stacked.shape[0] // 2 * (weight.shape[1] // width)
    vmem, hbm = (pl.BlockSpec(memory_space=space) for space in (pltpu.VMEM, pl.ANY))
    return pl.pallas_call(
        functools.partial(queries_kernel, moe_rows),
        in_specs=[pl.BlockSpec(memory_space=pltpu.SMEM)] + [vmem] * 5 + [hbm],
        out_specs=(vmem, vmem),
        out_shape=(
            jax.ShapeDtypeStruct((copies, rows, 2 * width), jnp.bfloat16),
            jax.ShapeDtypeStruct((w_out.shape[0] // 2, w_out.shape[1]), w_out.dtype),
        ),
        scratch_shapes=[pltpu.SemaphoreType.DMA],
        name="queries_of",
    )(core, stacked, weight, gain, cosine, sine, w_out)


def table_of(refs, rows, number):
    lanes = slice(128 * number, 128 * (number + 1))
    tiles = [ref[rows : rows + 8, lanes].astype(jnp.float32) for ref in refs]
    pairs = [tiles[k] + pltpu.roll(tiles[k + 1], 64, 1) for k in range(0, len(tiles), 2)]
    return jnp.concatenate(pairs, axis=1)


def placing(first_expert, routes, experts, capacity, slot_rows, moe_rows):
    count, cols = routes.shape
    expert = first_expert + lax.broadcasted_iota(jnp.int32, (experts, cols), 0)
    named = [
        jnp.broadcast_to(routes[k : k + 1], (experts, cols)) == expert.astype(jnp.float32)
        for k in range(count)
    ]
    hit = jnp.zeros((experts, cols), jnp.float32)
    for each in named:
        hit = hit + jnp.where(each, 1.0, 0.0)
    source = lax.broadcasted_iota(jnp.int32, (cols, cols), 0)
    target = lax.broadcasted_iota(jnp.int32, (cols, cols), 1)
    before = (source // moe_rows == target // moe_rows) & (source < target)
    rank = jnp.dot(
        hit.astype(jnp.bfloat16),
        jnp.where(before, 1.0, 0.0).astype(jnp.bfloat16),
        preferred_element_type=jnp.float32,
    )
    block = (lax.broadcasted_iota(jnp.int32, (experts, cols), 1) // (2 * moe_rows)).astype(jnp.float32)
    slot = jnp.where(hit > 0.0, block * capacity + rank, -1.0)
    row = lax.broadcasted_iota(jnp.int32, (slot_rows, cols), 0)
    half = lax.broadcasted_iota(jnp.int32, (slot_rows, cols), 1) // moe_rows % 2
    is_tangent = jnp.where((row // 8 == 1) | (row >= 20), 1, 0)
    row_slot = jnp.where(row < 8, row, jnp.where(row < 20, row - 8, row - 12))
    code = jnp.where(half == is_tangent, row_slot, -2).astype(jnp.float32)
    chosen = [
        jnp.broadcast_to(slot[j : j + 1], (slot_rows, cols)) == code for j in range(experts)
    ]
    return chosen, named


def pack_kernel(experts, capacity, slot_rows, moe_rows, first_ref, *refs):
    blocks, out_ref, table_ref = refs[:-2], refs[-2], refs[-1]
    rows = 2 * moe_rows
    routes = table_of(blocks, rows, 0)
    table_ref[:8] = routes
    table_ref[8:] = table_of(blocks, rows, 1)
    chosen, _ = placing(first_ref[0], routes, experts, capacity, slot_rows, moe_rows)
    pick = jnp.concatenate([jnp.where(c, 1.0, 0.0) for c in chosen], axis=0).astype(jnp.bfloat16)
    source = jnp.concatenate([block[:rows] for block in blocks], axis=0)
    out_ref[...] = jnp.dot(pick, source, preferred_element_type=jnp.float32).astype(jnp.bfloat16)


def mix_kernel(
    experts, capacity, slot_rows, moe_rows, first_ref, returned_ref, table_ref, out_ref
):
    routes = table_ref[:8]
    chosen, named = placing(first_ref[0], routes, experts, capacity, slot_rows, moe_rows)
    shares = table_ref[8:]
    share = jnp.zeros(named[0].shape, jnp.float32)
    for k, each in enumerate(named):
        share = share + jnp.where(each, jnp.broadcast_to(shares[k : k + 1], each.shape), 0.0)
    held = jnp.concatenate(
        [
            jnp.where(c, jnp.broadcast_to(share[j : j + 1], c.shape), 0.0)
            for j, c in enumerate(chosen)
        ],
        axis=0,
    )
    out_ref[...] = jnp.dot(
        held.T.astype(jnp.bfloat16), returned_ref[...], preferred_element_type=jnp.float32
    )


def pack(first, blocks, experts, capacity, slot_rows, moe_rows):
    vmem = pl.BlockSpec(memory_space=pltpu.VMEM)
    return pl.pallas_call(
        functools.partial(pack_kernel, experts, capacity, slot_rows, moe_rows),
        in_specs=[pl.BlockSpec(memory_space=pltpu.SMEM)] + [vmem] * len(blocks),
        out_specs=(vmem, vmem),
        out_shape=(
            jax.ShapeDtypeStruct((experts * slot_rows, blocks[0].shape[1]), jnp.bfloat16),
            jax.ShapeDtypeStruct((16, 2 * moe_rows * len(blocks)), jnp.float32),
        ),
        compiler_params=pltpu.CompilerParams(vmem_limit_bytes=40 << 20),
        name="pack",
    )(first, *blocks)


def mixed(first, returned, table, experts, capacity, slot_rows, moe_rows):
    vmem = pl.BlockSpec(memory_space=pltpu.VMEM)
    return pl.pallas_call(
        functools.partial(mix_kernel, experts, capacity, slot_rows, moe_rows),
        in_specs=[pl.BlockSpec(memory_space=pltpu.SMEM), vmem, vmem],
        out_specs=vmem,
        out_shape=jax.ShapeDtypeStruct((table.shape[1], returned.shape[1]), jnp.float32),
        compiler_params=pltpu.CompilerParams(vmem_limit_bytes=40 << 20),
        name="mixed",
    )(first, returned, table)


def expert_kernel(rows_ref, *refs):
    sources, out_ref, held, (sum_ref, hidden_ref, sems) = refs[:6], refs[6], refs[7:10], refs[10:]
    count, depth = rows_ref.shape
    units = sources[0].shape[1]
    step = depth // 4

    def copy(number, k):
        part = pl.ds(pl.multiple_of(k * step, step), step)
        side = number % 2 * units
        return pltpu.make_async_copy(
            sources[number].at[part],
            held[number // 2].at[part, side : side + units],
            sems.at[number, k],
        )

    for numbers in (range(4), range(4, 6)):
        for k in range(depth // step):
            for number in numbers:
                copy(number, k).start()
    sum_ref[...] = jnp.zeros_like(sum_ref)

    def contract(k, carry):
        part = pl.ds(pl.multiple_of(k * step, step), step)
        for number in range(2):
            copy(2 * number, k).wait()
            copy(2 * number + 1, k).wait()
            sum_ref[number] += jnp.dot(
                rows_ref[:, part], held[number][part], preferred_element_type=jnp.float32
            )
        return carry

    lax.fori_loop(0, depth // step, contract, 0)

    def pair(gate_value, gate_tangent, up_value, up_tangent):
        sigmoid_gate = jax.nn.sigmoid(gate_value)
        active = gate_value * sigmoid_gate
        active_slope = sigmoid_gate * (1.0 + gate_value * (1.0 - sigmoid_gate))
        primal = active * up_value
        return primal, active_slope * gate_tangent * up_value + active * up_tangent

    groups = 48

    def activate(number, carry):
        part = pl.ds(pl.multiple_of(number * groups, groups), groups)
        gate = sum_ref[0, part].reshape(groups // 24, 3, 8, 2 * units)
        up = sum_ref[1, part].reshape(groups // 24, 3, 8, 2 * units)
        primal, tangent = pair(gate[:, 0], gate[:, 1], up[:, 0], up[:, 1])
        mixed_gate, mixed_up = gate[:, 2], up[:, 2]
        turned_gate = pltpu.roll(mixed_gate, 4, 1)
        turned_up = pltpu.roll(mixed_up, 4, 1)
        first = lax.broadcasted_iota(jnp.int32, mixed_gate.shape, 1) < 4
        last_primal, last_tangent = pair(
            jnp.where(first, mixed_gate, turned_gate),
            jnp.where(first, turned_gate, mixed_gate),
            jnp.where(first, mixed_up, turned_up),
            jnp.where(first, turned_up, mixed_up),
        )
        last = jnp.where(first, last_primal, last_tangent)
        hidden = jnp.stack([primal, tangent, last], 1).reshape(groups, 2 * units)
        hidden_ref[part] = hidden.astype(jnp.bfloat16)
        return carry

    lax.fori_loop(0, count // groups, activate, 0)

    def produce(n, carry):
        part = pl.ds(pl.multiple_of(n * step, step), step)
        copy(4, n).wait()
        copy(5, n).wait()
        across = (((1,), (1,)), ((), ()))
        result = lax.dot_general(
            hidden_ref[...], held[2][part], across, preferred_element_type=jnp.float32
        )
        out_ref[:, part] = result.astype(out_ref.dtype)
        return carry

    lax.fori_loop(0, depth // step, produce, 0)


def expert_rows(rows, weights):
    gate, up, down, gate_other, up_other, down_other = weights
    count, (depth, units) = rows.shape[0], gate.shape
    vmem, hbm = (pl.BlockSpec(memory_space=space) for space in (pltpu.VMEM, pl.ANY))
    return pl.pallas_call(
        expert_kernel,
        in_specs=[vmem] + [hbm] * 6,
        out_specs=vmem,
        out_shape=jax.ShapeDtypeStruct(rows.shape, jnp.bfloat16),
        scratch_shapes=[
            *[pltpu.VMEM((depth, 2 * units), jnp.bfloat16)] * 3,
            pltpu.VMEM((2, count, 2 * units), jnp.float32),
            pltpu.VMEM((count, 2 * units), jnp.bfloat16),
            pltpu.SemaphoreType.DMA((6, 4)),
        ],
        compiler_params=pltpu.CompilerParams(vmem_limit_bytes=56 << 20),
        name="expert_rows",
    )(rows, gate, gate_other, up, up_other, down, down_other)


def layer(
    tokens,
    tangents,
    attn_gain,
    ffn_gain,
    w_query,
    w_key,
    w_value,
    w_out,
    query_gain,
    key_gain,
    expert_gate,
    expert_up,
    expert_down,
    routes,
    route_weights,
):
    tok_count, model_width = tokens.shape
    head_width = query_gain.shape[0]
    heads_here = w_query.shape[1] // head_width
    head_count = lax.axis_size("head")
    moe_rows = tok_count // head_count
    core = lax.axis_index("dp")
    other_core = [(0, 1), (1, 0)]

    own_halves = [expert_gate[0], expert_up[0], expert_down[0]]
    expert_halves = own_halves + [lax.ppermute(half, "dp", other_core) for half in own_halves]

    plane = lax.axis_index("seq_0")
    row_in_plane = lax.axis_index("seq_1")
    plane_rows = lax.axis_size("seq_1") * tok_count
    plane_count = lax.axis_size("seq_0")
    first_pos = plane * plane_rows + row_in_plane * tok_count
    positions = first_pos + jnp.arange(tok_count, dtype=jnp.int32)
    cosine, sine = turns_of(positions, head_width)
    kv_count = w_key.shape[1] // head_width
    devices_per_kv = lax.axis_size("head") // kv_count
    kv_head = (lax.axis_index("head") // devices_per_kv).astype(jnp.int32)[None]
    stacked, packed = keys_of(
        kv_head,
        tokens,
        tangents,
        attn_gain[None],
        w_key,
        w_value,
        key_gain[None],
        cosine,
        sine,
    )
    blocks = ring_blocks(packed, "seq_0")

    top_count = routes.shape[1]
    tables = jnp.stack([routes.astype(jnp.bfloat16), route_weights.astype(jnp.bfloat16)], 0)
    tables = jnp.transpose(tables, (2, 0, 1))
    tables = jnp.concatenate([tables, tables, jnp.zeros_like(tables), jnp.zeros_like(tables)], 2)
    tables = tables.reshape(top_count, 2 * 4 * moe_rows)
    tables = jnp.pad(tables, ((0, 0), (0, model_width - tables.shape[1])))

    row_groups = lax.axis_size("seq_1")
    copies, far_rows = queries_of(
        core.astype(jnp.int32)[None],
        stacked,
        w_query,
        query_gain[None],
        cosine,
        sine,
        w_out,
        row_groups,
        moe_rows,
    )

    ring = range(head_count)
    sides = [(i, (i + 1) % head_count) for i in ring]
    sides += [(head_count + i, head_count + (i - 1) % head_count) for i in ring]
    near_own = lax.ppermute(w_out, ("dp", "head"), sides)
    far_own = shifted(far_rows, "head", head_count // 2)
    near_other = lax.ppermute(near_own, "dp", other_core)
    far_other = lax.ppermute(far_own, "dp", other_core)
    out_pieces = (w_out, near_own, near_other, far_own, far_other)
    own_rows = copies.shape[1]
    joint_query = lax.all_to_all(copies, "seq_1", 0, 0, tiled=True)
    joint_query = joint_query.reshape(row_groups * own_rows, 2 * head_width)
    receivers = row_groups * head_count
    rows_each = heads_here * moe_rows
    state = None
    for order in ((0, -1, 1, -2, 2, -3, 3, -4),):
        spans = [
            (lax.rem(plane + k + plane_count, plane_count) - plane) * plane_rows
            + row_in_plane * tok_count
            for k in order
        ]
        state = attend(
            jnp.stack(spans).astype(jnp.int32),
            joint_query,
            [blocks[k] for k in order],
            state,
            receivers,
            rows_each,
            own_rows,
            moe_rows,
        )
    sent = state
    arrived = lax.all_to_all(sent, ("seq_1", "head"), 0, 0, tiled=True)
    here = lax.axis_index("head")
    side = 1 - 2 * core
    places = jnp.stack(
        [
            here,
            lax.rem(here - side + head_count, head_count),
            lax.rem(here + side + head_count, head_count),
            lax.rem(here + head_count // 2, head_count),
            core,
        ]
    ).astype(jnp.int32)
    residual, moe_in = merge(
        places,
        arrived,
        tokens,
        tangents,
        ffn_gain[None],
        tables,
        out_pieces,
        head_count,
        moe_rows,
    )
    gathered = ring_blocks(moe_in, "seq_0")

    plane_experts = row_groups * head_count
    capacity = 3
    first_expert = (plane * plane_experts).astype(jnp.int32)[None]
    near, far = [0, 1, -1, 2], [-2, 3, -3, -4]
    block_rows = 2 * moe_rows
    slot_rows = 2 * capacity * len(near)
    layout = (plane_experts, capacity, slot_rows, moe_rows)

    results, lists = [], {}
    for name, group in (("near", near), ("far", far)):
        outgoing, lists[name] = pack(first_expert, [gathered[k] for k in group], *layout)
        outgoing = outgoing.reshape(plane_experts, slot_rows, model_width)
        received = lax.all_to_all(outgoing, ("seq_1", "head"), 0, 0, tiled=True)
        results.append(
            expert_rows(received.reshape(plane_experts * slot_rows, model_width), expert_halves)
        )
    share_of = {}
    for name, group, result in (("far", far, results[1]), ("near", near, results[0])):
        result = result.reshape(plane_experts, slot_rows, model_width)
        returned = lax.all_to_all(result, ("seq_1", "head"), 0, 0, tiled=True)
        returned = returned.reshape(plane_experts * slot_rows, model_width)
        sums = mixed(first_expert, returned, lists[name], *layout)
        sums = sums.reshape(len(group), block_rows, model_width)
        for number, k in enumerate(group):
            share_of[k] = sums[number]
    low = jnp.bfloat16
    up = shifted(share_of[-4].astype(low), "seq_0", 1)
    down = shifted(share_of[-3].astype(low), "seq_0", -1)
    for k in (3, 2, 1):
        up = shifted((share_of[k] + up.astype(jnp.float32)).astype(low), "seq_0", 1)
    for k in (-2, -1):
        down = shifted((share_of[k] + down.astype(jnp.float32)).astype(low), "seq_0", -1)
    moe_sum = share_of[0] + up.astype(jnp.float32) + down.astype(jnp.float32)
    result = (residual + moe_sum).astype(jnp.bfloat16)
    layer_out, layer_tangent = result[:moe_rows], result[moe_rows:]
    return (layer_out, layer_tangent)


def solution(mesh):
    split = Mesh(
        mesh.devices.reshape(mesh.shape["dp"], 8, 4, mesh.shape["head"]),
        ("dp", "seq_0", "seq_1", "head"),
    )
    return jax.shard_map(
        layer,
        mesh=split,
        in_specs=(
            P(DP_SEQ, None),
            P(DP_SEQ, None),
            P(),
            P(),
            P(None, "head"),
            P(),
            P(),
            P("head", None),
            P(),
            P(),
            P(SEQ_HEAD, None, "dp"),
            P(SEQ_HEAD, None, "dp"),
            P(SEQ_HEAD, None, "dp"),
            P(DP_SEQ_HEAD, None),
            P(DP_SEQ_HEAD, None),
        ),
        out_specs=(P(DP_SEQ_HEAD, None), P(DP_SEQ_HEAD, None)),
        check_vma=False,
    )
```
